32 devices in a mesh: ty: 4 (over y, x), tx: 8 (over z, core).
Axes of the slice: x: 2, y: 2, z: 4, core: 2. Of those that a mesh axis runs over, the one named last changes fastest.
Arguments:
- adjoint: float32 [4, 36, 256, 1024], P(None, None, 'ty', 'tx'), may hold values from -6 to 6
- background_flow: float32 [2, 36, 256, 1024], P(None, None, 'ty', 'tx'), may hold values from -3 to 3
- vert_diff: float32 [36, 256, 1024], P(None, 'ty', 'tx'), may hold values from 0.05 to 4
- wet_levels: int32 [256, 1024], P('ty', 'tx'), may hold values from 0 to 36
- rotation: int32 [4, 8], P('ty', 'tx'), may hold values from 0 to 3
- face_map: int32 [4, 8], P('ty', 'tx'), may hold values from 0 to 3, as said below
- ctrl_owner: int32 [32], replicated, may hold values from 0 to 31, each once
Outputs:
- adjoint_out: float32 [4, 36, 256, 1024], P(None, None, 'ty', 'tx')
- sensitivity: float32 [32, 8192], P(('ty', 'tx'))
The draws below stay inside these ranges and needn't reach their ends.
Inputs may be any that keep to these rules, and one draw needn't show every extreme that they name: `rotation`: quarter turns from the common frame to the tile's frame. `wet_levels`: levels below the wet ones are land. `face_map`: each face is a band of 2 neighbouring whole tile columns, neighbouring with wrap-around; every face appears. A permutation: control tile j of face f belongs to the device of flat index ctrl_owner[f * 8 + j].
All inputs are finite; a program needn't handle non-finite values.
Results may differ from the reference program's by a relative error of at most 0.0003.
Values sent between devices are 32-bit elements; how exact they have to be, the bound alone decides.
No kernel may reach another device: no remote copies, remote signals or barrier semaphores. Data moves between devices by JAX's collectives and lax.ppermute only.
A program may use at most 192 MiB of HBM per device.

```python
import math
import jax
import jax.numpy as jnp
from jax import lax

LEV = 36
CY = 64
CX = 128
STEPS = 2
KY = 128
KX = 128
NFACE = 4
TILES_Y = 4
TILES_X = 8
NY = 256
NX = 1024
NCTRL = 32
CTW = 8192
N_TY = 4


def draw_face_map(key, part):
    shift_key = jax.random.fold_in(key, 11)
    label_key = jax.random.fold_in(key, 12)
    shift_value = jax.random.randint(shift_key, (), 0, TILES_X)
    labels = jax.random.permutation(label_key, NFACE)
    band = (jnp.arange(TILES_X) + shift_value) // (TILES_X // NFACE) % NFACE
    row_faces = labels[band]
    return jnp.broadcast_to(row_faces[None, :], (TILES_Y, TILES_X)).astype(jnp.int32)


def with_ends(entries, key, least, high):
    longest = entries.shape.index(max(entries.shape))
    spots = []
    for shift in (0, 1):
        where = [jax.random.randint(jax.random.fold_in(key, axis), (), 0, length) for axis, length in enumerate(entries.shape)]
        where[longest] = (where[longest] + shift) % entries.shape[longest]
        spots.append(tuple(where))
    return entries.at[spots[0]].set(least).at[spots[1]].set(high)


def level_of(rng, shape, split, low, largest):
    gain, own = 1.0, jax.random.fold_in(rng, 6)
    for position, shards_of in split:
        steps = jnp.exp(jax.random.uniform(jax.random.fold_in(own, position), (shards_of,), jnp.float32, low / len(split), largest / len(split)))
        gain = gain * jnp.repeat(steps, shape[position] // shards_of).reshape([-1 if axis == position else 1 for axis in range(len(shape))])
    return gain


def centred(stream_key, extent, deviation, reach, split=(), kind=jnp.bfloat16):
    factor_of = level_of(stream_key, extent, split, -0.22, 0.18) if split else 1.0
    values = jax.random.normal(stream_key, extent, jnp.float32) * deviation * factor_of
    return jnp.minimum(jnp.maximum(values, -reach), reach).astype(kind)


def setup_inputs(seed: int = 0) -> dict:
    key_list = jax.random.split(jax.random.key(seed), 8)
    adjoint = centred(key_list[0], (4, LEV, NY, NX), 1.0, 6.0, ((2, 4), (3, 8)), jnp.float32)
    background_flow = centred(key_list[1], (2, LEV, NY, NX), 0.7, 3.0, ((2, 4), (3, 8)), jnp.float32)
    vert_diff = jnp.clip(jnp.exp(math.log(4.0) - 4.3820266 * jax.random.uniform(key_list[2], (LEV, NY, NX), jnp.float32) ** level_of(key_list[2], (LEV, NY, NX), ((1, 4), (2, 8)), -0.2, 0.2)), 0.05, 4.0)
    wet_levels = with_ends(jax.random.randint(key_list[3], (NY, NX), 0, LEV + 1), jax.random.fold_in(key_list[3], 1), 0, LEV).astype(jnp.int32)
    rotation = with_ends(jax.random.randint(key_list[4], (TILES_Y, TILES_X), 0, 4), jax.random.fold_in(key_list[4], 1), 0, 3).astype(jnp.int32)
    face_map = draw_face_map(jax.random.fold_in(key_list[7], 71), 0)
    ctrl_owner = jax.random.permutation(key_list[6], NCTRL).astype(jnp.int32)
    return dict(adjoint=adjoint, background_flow=background_flow, vert_diff=vert_diff, wet_levels=wet_levels, rotation=rotation, face_map=face_map, ctrl_owner=ctrl_owner)


ADVECT_COEF = 0.3
DIFFUSE_COEF = 0.12
VISCOUS_COEF = 0.1
THERMAL_COEF = 0.4
HALINE_COEF = 0.3
PRESSURE_COEF = 0.4
SALINE_WEIGHT = 0.8
CORIOLIS_PEAK = 0.5
MOMENTUM_RATIO = 1.5

def turn_of(turn_codes):
    cosine = jnp.where(turn_codes == 0, 1.0, jnp.where(turn_codes == 2, -1.0, 0.0)).astype(jnp.float32)
    sine_part = jnp.where(turn_codes == 1, 1.0, jnp.where(turn_codes == 3, -1.0, 0.0)).astype(jnp.float32)
    return (cosine, sine_part)

def to_common(fields, cosine, sine_part):
    east_vel = fields[2]
    north_vel = fields[3]
    return jnp.stack([fields[0], fields[1], cosine * east_vel - sine_part * north_vel, sine_part * east_vel + cosine * north_vel])

def from_common(fields, cosine, sine_part):
    east_vel = fields[2]
    north_vel = fields[3]
    return jnp.stack([fields[0], fields[1], cosine * east_vel + sine_part * north_vel, cosine * north_vel - sine_part * east_vel])

def coriolis_rows(first_row, row_count, row_total):
    rows = (first_row + jnp.arange(row_count, dtype=jnp.int32)).astype(jnp.float32)
    return (CORIOLIS_PEAK * jnp.sin(math.pi * (rows + 0.5) / row_total - 0.5 * math.pi))[:, None]

def cosine_table(first_row, row_count, row_total, mode_count):
    rows = first_row + jnp.arange(row_count, dtype=jnp.int32)
    modes = jnp.arange(mode_count, dtype=jnp.int32)
    phase_index = (2 * rows[:, None] + 1) * modes[None, :] % (4 * row_total)
    return jnp.cos(phase_index.astype(jnp.float32) * (math.pi / (2 * row_total)))

def explicit(padded, background_flow, wet_mask, coriolis):
    height = padded.shape[2] - 4
    width = padded.shape[3] - 4

    def nearby(shift_y, shift_x, start_comp, stop_comp):
        return padded[start_comp:stop_comp, :, 2 + shift_y:2 + shift_y + height, 2 + shift_x:2 + shift_x + width]
    centre = nearby(0, 0, 0, 4)
    east_one = nearby(0, 1, 0, 4)
    west_one = nearby(0, -1, 0, 4)
    north_one = nearby(1, 0, 0, 4)
    south_one = nearby(-1, 0, 0, 4)
    east_two = nearby(0, 2, 0, 2)
    west_two = nearby(0, -2, 0, 2)
    north_two = nearby(2, 0, 0, 2)
    south_two = nearby(-2, 0, 0, 2)
    grad_x = (8.0 * (east_one[:2] - west_one[:2]) - (east_two - west_two)) / 12.0
    grad_y = (8.0 * (north_one[:2] - south_one[:2]) - (north_two - south_two)) / 12.0
    spread = east_one + west_one + north_one + south_one - 4.0 * centre
    inflow = 0.5 * (east_one[2] - west_one[2] + north_one[3] - south_one[3])
    buoy_x = 0.5 * (east_one[0] - SALINE_WEIGHT * east_one[1] - (west_one[0] - SALINE_WEIGHT * west_one[1]))
    buoy_y = 0.5 * (north_one[0] - SALINE_WEIGHT * north_one[1] - (south_one[0] - SALINE_WEIGHT * south_one[1]))
    carried = background_flow[0][None] * grad_x + background_flow[1][None] * grad_y
    heat_new = centre[0] + ADVECT_COEF * carried[0] + DIFFUSE_COEF * spread[0] + THERMAL_COEF * inflow
    salt_new = centre[1] + ADVECT_COEF * carried[1] + DIFFUSE_COEF * spread[1] - HALINE_COEF * inflow
    zonal_new = centre[2] + VISCOUS_COEF * spread[2] + coriolis * centre[3] - PRESSURE_COEF * buoy_x
    merid_new = centre[3] + VISCOUS_COEF * spread[3] - coriolis * centre[2] - PRESSURE_COEF * buoy_y
    return jnp.stack([heat_new, salt_new, zonal_new, merid_new]) * wet_mask[None]

def vertical(rhs_fields, vert_diff, wet_mask):
    levels = rhs_fields.shape[1]
    factor = jnp.array([1.0, 1.0, MOMENTUM_RATIO, MOMENTUM_RATIO], dtype=jnp.float32)[:, None, None]
    links = [factor * (vert_diff[level_index] * wet_mask[level_index + 1])[None] for level_index in range(levels - 1)]
    ratios = []
    values = []
    for level_index in range(levels):
        centre_coef = jnp.ones_like(rhs_fields[:, 0])
        if level_index > 0:
            centre_coef = centre_coef + links[level_index - 1]
        if level_index < levels - 1:
            centre_coef = centre_coef + links[level_index]
        if level_index == 0:
            pivot_value = centre_coef
            value_now = rhs_fields[:, 0] / pivot_value
        else:
            link_above = links[level_index - 1]
            pivot_value = centre_coef + link_above * ratios[-1]
            value_now = (rhs_fields[:, level_index] + link_above * values[-1]) / pivot_value
        if level_index < levels - 1:
            ratios.append(-links[level_index] / pivot_value)
        else:
            ratios.append(jnp.zeros_like(pivot_value))
        values.append(value_now)
    result = [values[-1]]
    for level_index in range(levels - 2, -1, -1):
        result.insert(0, values[level_index] - ratios[level_index] * result[0])
    return jnp.stack(result, 1)

def reference(adjoint, background_flow, vert_diff, wet_levels, rotation, face_map, ctrl_owner):
    wet_mask = (jnp.arange(LEV, dtype=jnp.int32)[:, None, None] < wet_levels[None]).astype(jnp.float32)
    cell_turns = jnp.repeat(jnp.repeat(rotation, CY, axis=0), CX, axis=1)
    cosine, sine_part = turn_of(cell_turns)
    fields = to_common(adjoint, cosine, sine_part)
    coriolis = coriolis_rows(0, NY, NY)
    surfaces = []
    for step_index in range(STEPS):
        padded = jnp.pad(fields, ((0, 0), (0, 0), (2, 2), (0, 0)))
        padded = jnp.pad(padded, ((0, 0), (0, 0), (0, 0), (2, 2)), mode='wrap')

        def advance_block(block_index, padded=padded):
            start_row = (block_index * CY).astype(jnp.int32)
            piece_rows = lax.dynamic_slice_in_dim(padded, start_row, CY + 4, 2)
            flow_rows = lax.dynamic_slice_in_dim(background_flow, start_row, CY, 2)
            mask_rows = lax.dynamic_slice_in_dim(wet_mask, start_row, CY, 1)
            diff_rows = lax.dynamic_slice_in_dim(vert_diff, start_row, CY, 1)
            turn_rows = lax.dynamic_slice_in_dim(coriolis, start_row, CY, 0)
            return vertical(explicit(piece_rows, flow_rows, mask_rows, turn_rows), diff_rows, mask_rows)
        blocks = lax.map(advance_block, jnp.arange(N_TY, dtype=jnp.int32))
        fields = jnp.moveaxis(blocks, 0, 2).reshape(4, LEV, NY, NX)
        surfaces.append(fields[:2, 0])
    adjoint_out = from_common(fields, cosine, sine_part)
    surface_all = jnp.stack(surfaces)
    face_cells = jnp.repeat(jnp.repeat(face_map, CY, axis=0), CX, axis=1)
    row_modes = cosine_table(0, NY, NY, KY)
    col_modes = cosine_table(0, NX, NX, KX)
    coef_list = []
    for face_index in range(NFACE):
        in_face = (face_cells == face_index).astype(jnp.float32)
        partial_value = jnp.einsum('yk,rfyx->rfkx', row_modes, surface_all * in_face, precision=lax.Precision.HIGHEST)
        coef_list.append(jnp.einsum('rfkx,xj->rfkj', partial_value, col_modes, precision=lax.Precision.HIGHEST))
    norm_factor = math.sqrt(2.0 * NFACE / (NY * NX))
    all_coefs = (jnp.stack(coef_list) * norm_factor).reshape(NCTRL, CTW)
    sensitivity = jnp.zeros((NCTRL, CTW), jnp.float32).at[ctrl_owner].set(all_coefs)
    return (adjoint_out, sensitivity)
```

```python
import functools
import math

import jax
import jax.numpy as jnp
from jax import lax
from jax.experimental import pallas as pl
from jax.experimental.pallas import tpu as pltpu
from jax.sharding import PartitionSpec as P

KY = 128
KX = 128
NFACE = 4

ADVECT_COEF = 0.3
DIFFUSE_COEF = 0.12
VISCOUS_COEF = 0.1
THERMAL_COEF = 0.4
HALINE_COEF = 0.3
PRESSURE_COEF = 0.4
SALINE_WEIGHT = 0.8
CORIOLIS_PEAK = 0.5
MOMENTUM_RATIO = 1.5

TILE = 8
LANES = 128
VMEM = pl.BlockSpec(memory_space=pltpu.VMEM)
SMEM = pl.BlockSpec(memory_space=pltpu.SMEM)
LIMIT = 56 << 20
F32 = jnp.float32
PREP_ROWS, PREP_UNROLL = 64, 6
FACTOR_ROWS, FACTOR_UNROLL = 64, 2
STEP_ROWS, UP_UNROLL, DOWN_UNROLL = 64, 4, 6


def shape(*dims):
    return jax.ShapeDtypeStruct(dims, F32)


def lanes_of(rows):
    return lax.broadcasted_iota(jnp.int32, (rows, LANES), 1)


def rows_of(rows):
    return lax.broadcasted_iota(jnp.int32, (rows, LANES), 0)


def loop(count, load, body, init, unroll):
    while count % unroll:
        unroll -= 1

    def several(i, carry):
        steps = [i * unroll + j for j in range(unroll)]
        loaded = [load(step) for step in steps]
        stores = []
        for step, values in zip(steps, loaded):
            carry, store = body(step, values, carry)
            stores.append(store)
        for store in stores:
            store()
        return carry

    return lax.fori_loop(0, count // unroll, several, init)


def turn_scalars(code):
    cosine = jnp.where(code == 0, 1.0, jnp.where(code == 2, -1.0, 0.0)).astype(F32)
    sine = jnp.where(code == 1, 1.0, jnp.where(code == 3, -1.0, 0.0)).astype(F32)
    return cosine, sine


def pack_columns(acc, k, fields, lane):
    at = 3 * k
    first, second, third = lane >= at, lane >= at + 1, lane >= at + 2
    east, west = [], []
    for g in range(2):
        tracer, flow = fields[g], fields[g + 2]
        rolled = pltpu.roll(tracer, at + 2, 1)
        east.append(jnp.where(first, jnp.where(third, pltpu.roll(flow, at + 3, 1), rolled), acc[g]))
        west.append(jnp.where(second, jnp.where(third, rolled, pltpu.roll(flow, at + 1, 1)), acc[g + 2]))
    return tuple(east + west)


def store_edge_rows(k, fields, block, last, south_ref, north_ref):
    size = fields[0].shape[0]
    for c in range(4):
        if block == 0:
            south_ref[k, 2 * c : 2 * c + 2, :] = fields[c][0:2, :]
        if block == last:
            north_ref[k, 2 * c : 2 * c + 2, :] = fields[c][size - 2 : size, :]


def prep_kernel(rot_ref, adj_ref, uv_ref, south_ref, north_ref, east_ref, west_ref):
    levels, height = adj_ref.shape[1], adj_ref.shape[2]
    cosine, sine = turn_scalars(rot_ref[0, 0])
    size = PREP_ROWS
    lane = lanes_of(size)
    blocks = height // size
    for block in range(blocks):
        rows = pl.ds(block * size, size)

        def load(k, rows=rows):
            return [adj_ref[c, k, rows, :] for c in range(4)]

        def level(k, loaded, acc, rows=rows, block=block):
            t, s, a, b = loaded
            u = cosine * a - sine * b
            v = sine * a + cosine * b
            fields = (t, s, u, v)

            def store():
                uv_ref[0, k, rows, :] = u
                uv_ref[1, k, rows, :] = v
                store_edge_rows(k, fields, block, blocks - 1, south_ref, north_ref)

            return pack_columns(acc, k, fields, lane), store

        zero = jnp.zeros((size, LANES), F32)
        acc = loop(levels, load, level, (zero,) * 4, PREP_UNROLL)
        for g in range(2):
            east_ref[g, rows, :] = acc[g]
            west_ref[g, rows, :] = acc[g + 2]


def factor_kernel(vd_ref, wet_ref, w1_ref, w2_ref, h1_ref, h2_ref, g1_ref, g2_ref):
    levels, height = vd_ref.shape[0], vd_ref.shape[1]
    out = ((w1_ref, h1_ref, g1_ref, 1.0), (w2_ref, h2_ref, g2_ref, MOMENTUM_RATIO))
    size = FACTOR_ROWS
    for block in range(height // size):
        rows = pl.ds(block * size, size)
        wet = wet_ref[rows, :]
        zero = jnp.zeros((size, LANES), F32)

        def load(i, rows=rows):
            return vd_ref[jnp.maximum(levels - 2 - i, 0), rows, :]

        def level(i, loaded, carry, rows=rows, wet=wet):
            k = levels - 1 - i
            below, inverses = carry
            mask = jnp.where(k < wet, 1.0, 0.0).astype(F32)
            above = jnp.where(k > 0, loaded * mask, 0.0)
            kept, stores = [], []
            for (w_ref, h_ref, g_ref, factor), inverse in zip(out, inverses):
                low, high = factor * below, factor * above
                pivot = 1.0 + high + low - low * (low * inverse)
                inverse = 1.0 / pivot
                masked = inverse * mask
                stores += [(w_ref, masked), (h_ref, low * masked), (g_ref, high * masked)]
                kept.append(inverse)

            def store():
                for ref, value in stores:
                    ref[k, rows, :] = value

            return (above, tuple(kept)), store

        loop(levels, load, level, (zero, (zero, zero)), FACTOR_UNROLL)


def step_kernel(final, *refs):
    refs = list(refs)
    rot_ref = refs.pop(0) if final else None
    ts_ref, uv_ref, flow_ref, w1_ref, w2_ref, h1_ref, h2_ref, g1_ref, g2_ref, cor_ref = refs[:10]
    south_ref, north_ref, east_ref, west_ref = refs[10:14]
    if final:
        out_ref, surface_ref, value_ref = refs[14:]
    else:
        ts_out, uv_out, surface_ref, south_out, north_out, east_out, west_out, value_ref = refs[14:]
    levels, height = ts_ref.shape[1], ts_ref.shape[2]
    size = STEP_ROWS
    blocks = height // size
    lane, row = lanes_of(size), rows_of(size)
    low_two, high_two = lane < 2, lane >= LANES - 2
    low_one, high_one = lane < 1, lane >= LANES - 1
    zero = jnp.zeros((size, LANES), F32)
    if final:
        cosine, sine = turn_scalars(rot_ref[0, 0])

    def get(c, k, start):
        rows = pl.ds(start, TILE)
        return ts_ref[c, k, rows, :] if c < 2 else uv_ref[c - 2, k, rows, :]

    def line(c, k, start, halos):
        if 0 <= start <= height - TILE:
            return get(c, k, start)
        south, north = halos
        part = rows_of(TILE)
        if start < 0:
            halo = pltpu.roll(south, (-2 * c - 2 - start) % TILE, 0)
            return jnp.where(part < -start, halo, pltpu.roll(get(c, k, 0), -start, 0))
        over = start + TILE - height
        halo = pltpu.roll(north, (TILE - over - 2 * c) % TILE, 0)
        return jnp.where(part >= TILE - over, halo, pltpu.roll(get(c, k, height - TILE), TILE - over, 0))

    for block in range(blocks):
        rows = pl.ds(block * size, size)
        first_row = block * size
        cor = cor_ref[rows, :]

        def fetch(c, k, shift, halos, first_row=first_row):
            start = first_row + shift
            if 0 <= start <= height - size:
                part = pl.ds(start, size)
                return ts_ref[c, k, part, :] if c < 2 else uv_ref[c - 2, k, part, :]
            lines = [line(c, k, start + i, halos) for i in range(0, size, TILE)]
            return lines[0] if len(lines) == 1 else jnp.concatenate(lines, axis=0)

        def load_up(i, rows=rows, block=block, fetch=fetch):
            k = levels - 1 - i
            halos = (south_ref[k] if block == 0 else None, north_ref[k] if block == blocks - 1 else None)
            turn = LANES - 2 - 3 * k
            east = [pltpu.roll(east_ref[g, rows, :], turn, 1) for g in range(2)]
            west = [pltpu.roll(west_ref[g, rows, :], turn, 1) for g in range(2)]
            lines = [{s: fetch(c, k, s, halos) for s in ((0, 1, -1, 2, -2) if c < 2 else (0, 1, -1))} for c in range(4)]
            flow = [flow_ref[i, k, rows, :] for i in range(2)]
            factors = [ref[k, rows, :] for ref in (w1_ref, w2_ref, h1_ref, h2_ref)]
            return east, west, lines, flow, factors

        def upward(i, loaded, below, cor=cor):
            k = levels - 1 - i
            east, west, lines, flow, factors = loaded
            flow_x = flow[0] * (ADVECT_COEF / 12.0)
            flow_y = flow[1] * (ADVECT_COEF / 12.0)
            rhs, diff_x, diff_y = [], [], []
            for c in range(2):
                mid = lines[c][0]
                e1 = pltpu.roll(jnp.where(low_one, east[c], mid), LANES - 1, 1)
                w1 = pltpu.roll(jnp.where(high_one, west[c], mid), 1, 1)
                e2 = pltpu.roll(jnp.where(low_two, east[c], mid), LANES - 2, 1)
                w2 = pltpu.roll(jnp.where(high_two, west[c], mid), 2, 1)
                n1, s1, n2, s2 = (lines[c][s] for s in (1, -1, 2, -2))
                dx, dy = e1 - w1, n1 - s1
                grad = flow_x * (8.0 * dx - (e2 - w2)) + flow_y * (8.0 * dy - (n2 - s2))
                near = (e1 + w1) + (n1 + s1)
                rhs.append((1.0 - 4.0 * DIFFUSE_COEF) * mid + DIFFUSE_COEF * near + grad)
                diff_x.append(dx)
                diff_y.append(dy)
            push = [
                (0.5 * PRESSURE_COEF) * (d[0] - SALINE_WEIGHT * d[1]) for d in (diff_x, diff_y)
            ]
            sides = []
            for c in range(2, 4):
                mid = lines[c][0]
                e1 = jnp.where(high_one, east[c - 2], pltpu.roll(mid, LANES - 1, 1))
                w1 = jnp.where(low_one, west[c - 2], pltpu.roll(mid, 1, 1))
                n1, s1 = lines[c][1], lines[c][-1]
                near = (e1 + w1) + (n1 + s1)
                sides.append(e1 - w1 if c == 2 else n1 - s1)
                rhs.append((1.0 - 4.0 * VISCOUS_COEF) * mid + VISCOUS_COEF * near - push[c - 2])
            spread = sides[0] + sides[1]
            rhs[0] = rhs[0] + (0.5 * THERMAL_COEF) * spread
            rhs[1] = rhs[1] - (0.5 * HALINE_COEF) * spread
            rhs[2] = rhs[2] + cor * lines[3][0]
            rhs[3] = rhs[3] - cor * lines[2][0]
            values = tuple(
                factors[c // 2] * rhs[c] + factors[2 + c // 2] * below[c] for c in range(4)
            )

            def store():
                for c in range(4):
                    value_ref[c, k] = values[c]

            return values, store

        top = loop(levels, load_up, upward, (zero,) * 4, UP_UNROLL)
        for c in range(2):
            surface_ref[c, rows, :] = top[c]

        def load_down(k, rows=rows):
            return [value_ref[c, k] for c in range(4)], (g1_ref[k, rows, :], g2_ref[k, rows, :])

        def downward(k, loaded, carry, rows=rows, block=block):
            above, acc = carry
            values, gains = loaded
            fields = tuple(values[c] + gains[c // 2] * above[c] for c in range(4))

            def store():
                if final:
                    u, v = fields[2], fields[3]
                    out_ref[0, k, rows, :] = fields[0]
                    out_ref[1, k, rows, :] = fields[1]
                    out_ref[2, k, rows, :] = cosine * u + sine * v
                    out_ref[3, k, rows, :] = cosine * v - sine * u
                    return
                for c in range(2):
                    ts_out[c, k, rows, :] = fields[c]
                    uv_out[c, k, rows, :] = fields[c + 2]
                store_edge_rows(k, fields, block, blocks - 1, south_out, north_out)

            return (fields, acc if final else pack_columns(acc, k, fields, lane)), store

        acc = () if final else (zero,) * 4
        _, acc = loop(levels, load_down, downward, ((zero,) * 4, acc), DOWN_UNROLL)
        if not final:
            for g in range(2):
                east_out[g, rows, :] = acc[g]
                west_out[g, rows, :] = acc[g + 2]


HIGHEST = lax.Precision.HIGHEST


def transform(parts, row_table_ref, col_table_ref, norm):
    height = parts[0].shape[1]
    out = []
    for c in range(2):
        total = None
        for i, part in enumerate(parts):
            table = row_table_ref[i * height : (i + 1) * height, :]
            piece = lax.dot_general(table, part[c], (((0,), (0,)), ((), ())), precision=HIGHEST, preferred_element_type=F32)
            total = piece if total is None else total + piece
        out.append(norm * jnp.dot(total, col_table_ref[...], precision=HIGHEST, preferred_element_type=F32))
    return out


def first_transform_kernel(norm, *refs):
    *parts, row_table_ref, col_table_ref, out_ref = refs
    for c, block in enumerate(transform(parts, row_table_ref, col_table_ref, norm)):
        out_ref[c * KY : (c + 1) * KY, :] = block


def second_transform_kernel(norm, count, slot_ref, valid_ref, *refs):
    refs, sends, table = refs[: -count - 1], refs[-count - 1 : -1], refs[-1]
    *parts, row_table_ref, col_table_ref, early_ref = refs
    table[0 : 2 * KY, :] = early_ref[...]
    for c, block in enumerate(transform(parts, row_table_ref, col_table_ref, norm)):
        table[(2 + c) * KY : (3 + c) * KY, :] = block
    for i, send in enumerate(sends):
        size = send.shape[0]
        start = pl.multiple_of(slot_ref[i] * size, TILE)
        mine = jnp.full((size, LANES), valid_ref[i], jnp.int32) > 0
        send[...] = jnp.where(mine, table[pl.ds(start, size), :], 0.0)


def call(kernel, outs, in_specs, scratch=()):
    many = isinstance(outs, (list, tuple))
    return pl.pallas_call(
        kernel,
        out_shape=outs,
        in_specs=in_specs,
        out_specs=[VMEM] * len(outs) if many else VMEM,
        scratch_shapes=list(scratch),
        compiler_params=pltpu.CompilerParams(vmem_limit_bytes=LIMIT),
    )


def exchange(south, north, east, west):
    ty, tx = lax.axis_size("ty"), lax.axis_size("tx")
    up = [(i, i + 1) for i in range(ty - 1)]
    down = [(i + 1, i) for i in range(ty - 1)]
    right = [(i, (i + 1) % tx) for i in range(tx)]
    left = [((i + 1) % tx, i) for i in range(tx)]
    return (
        lax.ppermute(north, "ty", up),
        lax.ppermute(south, "ty", down),
        lax.ppermute(west, "tx", left),
        lax.ppermute(east, "tx", right),
    )


def gather_rows(block):
    ty = lax.axis_size("ty")
    return [block] + [
        lax.ppermute(block, "ty", [(i, (i + s) % ty) for i in range(ty)]) for s in range(1, ty)
    ]


def cosine_table(rows, row_total, mode_count):
    modes = jnp.arange(mode_count, dtype=jnp.int32)
    phase_index = (2 * rows[:, None] + 1) * modes[None, :] % (4 * row_total)
    return jnp.cos(phase_index.astype(F32) * (math.pi / (2 * row_total)))


def body(adjoint, background_flow, vert_diff, wet_levels, rotation, face_map, ctrl_owner):
    _, levels, height, width = adjoint.shape
    ty, tx = lax.axis_size("ty"), lax.axis_size("tx")
    here_y, here_x = lax.axis_index("ty"), lax.axis_index("tx")
    rows_total, cols_total = height * ty, width * tx
    full = shape(levels, height, width)
    pair = shape(2, levels, height, width)
    edge_rows = [shape(levels, TILE, width)] * 2
    edge_cols = [shape(2, height, LANES)] * 2

    uv, *edges = call(prep_kernel, [pair] + edge_rows + edge_cols, [SMEM, VMEM])(rotation, adjoint)
    halos = exchange(*edges)
    factors = call(factor_kernel, [full] * 6, [VMEM] * 2)(vert_diff, wet_levels)

    rows = (here_y * height + jnp.arange(height, dtype=jnp.int32)).astype(F32)
    coriolis = CORIOLIS_PEAK * jnp.sin(math.pi * (rows + 0.5) / rows_total - 0.5 * math.pi)
    coriolis = jnp.broadcast_to(coriolis[:, None], (height, width))
    origin = (here_y - jnp.arange(ty, dtype=jnp.int32)) % ty
    source_rows = (origin[:, None] * height + jnp.arange(height, dtype=jnp.int32)[None, :]).reshape(-1)
    row_table = cosine_table(source_rows, rows_total, KY)
    col_table = cosine_table(here_x * width + jnp.arange(width, dtype=jnp.int32), cols_total, KX)
    norm = math.sqrt(2.0 * NFACE / (rows_total * cols_total))
    per_face = ctrl_owner.shape[0] // NFACE
    targets = here_y * tx + (here_x + jnp.arange(tx, dtype=jnp.int32)) % tx
    numbers = jnp.arange(ctrl_owner.shape[0], dtype=jnp.int32)
    owned = jnp.sum(jnp.where(ctrl_owner[None, :] == targets[:, None], numbers[None, :], 0), axis=1)
    slots = owned % per_face
    valid = (owned // per_face == face_map[0, 0]).astype(jnp.int32)

    scratch = [pltpu.VMEM((4, levels, STEP_ROWS, width), F32)]
    surface = shape(2, height, width)
    ts, uv, first, *edges = call(
        functools.partial(step_kernel, False),
        [pair, pair, surface] + edge_rows + edge_cols,
        [VMEM] * 14,
        scratch,
    )(adjoint, uv, background_flow, *factors, coriolis, *halos)
    halos = exchange(*edges)
    first_parts = gather_rows(first)
    early = call(
        functools.partial(first_transform_kernel, norm), shape(2 * KY, KX), [VMEM] * (ty + 2)
    )(*first_parts, row_table, col_table)
    adjoint_out, second = call(
        functools.partial(step_kernel, True),
        [shape(*adjoint.shape), surface],
        [SMEM] + [VMEM] * 14,
        scratch,
    )(rotation, ts, uv, background_flow, *factors, coriolis, *halos)
    second_parts = gather_rows(second)
    size = 4 * KY // per_face
    sends = call(
        functools.partial(second_transform_kernel, norm, tx),
        [shape(size, KX)] * tx,
        [SMEM] * 2 + [VMEM] * (ty + 3),
        [pltpu.VMEM((4 * KY, KX), F32)],
    )(slots, valid, *second_parts, row_table, col_table, early)
    total = sends[0]
    for s in range(1, tx):
        total = total + lax.ppermute(sends[s], "tx", [(i, (i + s) % tx) for i in range(tx)])
    return adjoint_out, total.reshape(1, -1)


def solution(mesh):
    return jax.shard_map(
        body,
        mesh=mesh,
        in_specs=(
            P(None, None, "ty", "tx"),
            P(None, None, "ty", "tx"),
            P(None, "ty", "tx"),
            P("ty", "tx"),
            P("ty", "tx"),
            P("ty", "tx"),
            P(),
        ),
        out_specs=(P(None, None, "ty", "tx"), P(("ty", "tx"), None)),
        check_vma=False,
    )
```

```python
import functools
import math

import jax
import jax.numpy as jnp
from jax import lax
from jax.experimental import pallas as pl
from jax.experimental.pallas import tpu as pltpu
from jax.sharding import PartitionSpec as P

KY = 128
KX = 128
NFACE = 4

ADVECT_COEF = 0.3
DIFFUSE_COEF = 0.12
VISCOUS_COEF = 0.1
THERMAL_COEF = 0.4
HALINE_COEF = 0.3
PRESSURE_COEF = 0.4
SALINE_WEIGHT = 0.8
CORIOLIS_PEAK = 0.5
MOMENTUM_RATIO = 1.5

TILE = 8
LANES = 128
VMEM = pl.BlockSpec(memory_space=pltpu.VMEM)
SMEM = pl.BlockSpec(memory_space=pltpu.SMEM)
LIMIT = 16 << 20
F32 = jnp.float32
PREP_ROWS, PREP_UNROLL = 64, 6
FACTOR_ROWS, FACTOR_UNROLL = 64, 2
STEP_ROWS, UP_UNROLL, DOWN_UNROLL = 64, 4, 6


def shape(*dims):
    return jax.ShapeDtypeStruct(dims, F32)


def lanes_of(rows):
    return lax.broadcasted_iota(jnp.int32, (rows, LANES), 1)


def rows_of(rows):
    return lax.broadcasted_iota(jnp.int32, (rows, LANES), 0)


def loop(count, load, body, init, unroll):
    while count % unroll:
        unroll -= 1

    def several(i, carry):
        steps = [i * unroll + j for j in range(unroll)]
        loaded = [load(step) for step in steps]
        stores = []
        for step, values in zip(steps, loaded):
            carry, store = body(step, values, carry)
            stores.append(store)
        for store in stores:
            store()
        return carry

    return lax.fori_loop(0, count // unroll, several, init)


def turn_scalars(code):
    cosine = jnp.where(code == 0, 1.0, jnp.where(code == 2, -1.0, 0.0)).astype(F32)
    sine = jnp.where(code == 1, 1.0, jnp.where(code == 3, -1.0, 0.0)).astype(F32)
    return cosine, sine


def pack_columns(acc, k, fields, lane):
    at = 3 * k
    first, second, third = lane >= at, lane >= at + 1, lane >= at + 2
    east, west = [], []
    for g in range(2):
        tracer, flow = fields[g], fields[g + 2]
        rolled = pltpu.roll(tracer, at + 2, 1)
        east.append(jnp.where(first, jnp.where(third, pltpu.roll(flow, at + 3, 1), rolled), acc[g]))
        west.append(jnp.where(second, jnp.where(third, rolled, pltpu.roll(flow, at + 1, 1)), acc[g + 2]))
    return tuple(east + west)


def store_edge_rows(k, fields, block, last, south_ref, north_ref):
    size = fields[0].shape[0]
    for c in range(4):
        if block == 0:
            south_ref[k, 2 * c : 2 * c + 2, :] = fields[c][0:2, :]
        if block == last:
            north_ref[k, 2 * c : 2 * c + 2, :] = fields[c][size - 2 : size, :]


def prep_kernel(rot_ref, adj_ref, uv_ref, south_ref, north_ref, east_ref, west_ref):
    levels, height = adj_ref.shape[1], adj_ref.shape[2]
    cosine, sine = turn_scalars(rot_ref[0, 0])
    size = PREP_ROWS
    lane = lanes_of(size)
    blocks = height // size
    for block in range(blocks):
        rows = pl.ds(block * size, size)

        def load(k, rows=rows):
            return [adj_ref[c, k, rows, :] for c in range(4)]

        def level(k, loaded, acc, rows=rows, block=block):
            t, s, a, b = loaded
            u = cosine * a - sine * b
            v = sine * a + cosine * b
            fields = (t, s, u, v)

            def store():
                uv_ref[0, k, rows, :] = u
                uv_ref[1, k, rows, :] = v
                store_edge_rows(k, fields, block, blocks - 1, south_ref, north_ref)

            return pack_columns(acc, k, fields, lane), store

        zero = jnp.zeros((size, LANES), F32)
        acc = loop(levels, load, level, (zero,) * 4, PREP_UNROLL)
        for g in range(2):
            east_ref[g, rows, :] = acc[g]
            west_ref[g, rows, :] = acc[g + 2]


def factor_kernel(vd_ref, wet_ref, w1_ref, w2_ref, h1_ref, h2_ref, g1_ref, g2_ref):
    levels, height = vd_ref.shape[0], vd_ref.shape[1]
    out = ((w1_ref, h1_ref, g1_ref, 1.0), (w2_ref, h2_ref, g2_ref, MOMENTUM_RATIO))
    size = FACTOR_ROWS
    for block in range(height // size):
        rows = pl.ds(block * size, size)
        wet = wet_ref[rows, :]
        zero = jnp.zeros((size, LANES), F32)

        def load(i, rows=rows):
            return vd_ref[jnp.maximum(levels - 2 - i, 0), rows, :]

        def level(i, loaded, carry, rows=rows, wet=wet):
            k = levels - 1 - i
            below, inverses = carry
            mask = jnp.where(k < wet, 1.0, 0.0).astype(F32)
            above = jnp.where(k > 0, loaded * mask, 0.0)
            kept, stores = [], []
            for (w_ref, h_ref, g_ref, factor), inverse in zip(out, inverses):
                low, high = factor * below, factor * above
                pivot = 1.0 + high + low - low * (low * inverse)
                inverse = 1.0 / pivot
                masked = inverse * mask
                stores += [(w_ref, masked), (h_ref, low * masked), (g_ref, high * masked)]
                kept.append(inverse)

            def store():
                for ref, value in stores:
                    ref[k, rows, :] = value

            return (above, tuple(kept)), store

        loop(levels, load, level, (zero, (zero, zero)), FACTOR_UNROLL)


def step_kernel(final, *refs):
    refs = list(refs)
    rot_ref = refs.pop(0) if final else None
    ts_ref, uv_ref, flow_ref, w1_ref, w2_ref, h1_ref, h2_ref, g1_ref, g2_ref, cor_ref = refs[:10]
    south_ref, north_ref, east_ref, west_ref = refs[10:14]
    if final:
        out_ref, surface_ref, value_ref = refs[14:]
    else:
        ts_out, uv_out, surface_ref, south_out, north_out, east_out, west_out, value_ref = refs[14:]
    levels, height = ts_ref.shape[1], ts_ref.shape[2]
    size = STEP_ROWS
    blocks = height // size
    lane, row = lanes_of(size), rows_of(size)
    low_two, high_two = lane < 2, lane >= LANES - 2
    low_one, high_one = lane < 1, lane >= LANES - 1
    zero = jnp.zeros((size, LANES), F32)
    if final:
        cosine, sine = turn_scalars(rot_ref[0, 0])

    def get(c, k, start):
        rows = pl.ds(start, TILE)
        return ts_ref[c, k, rows, :] if c < 2 else uv_ref[c - 2, k, rows, :]

    def line(c, k, start, halos):
        if 0 <= start <= height - TILE:
            return get(c, k, start)
        south, north = halos
        part = rows_of(TILE)
        if start < 0:
            halo = pltpu.roll(south, (-2 * c - 2 - start) % TILE, 0)
            return jnp.where(part < -start, halo, pltpu.roll(get(c, k, 0), -start, 0))
        over = start + TILE - height
        halo = pltpu.roll(north, (TILE - over - 2 * c) % TILE, 0)
        return jnp.where(part >= TILE - over, halo, pltpu.roll(get(c, k, height - TILE), TILE - over, 0))

    for block in range(blocks):
        rows = pl.ds(block * size, size)
        first_row = block * size
        cor = cor_ref[rows, :]

        def fetch(c, k, shift, halos, first_row=first_row):
            start = first_row + shift
            if 0 <= start <= height - size:
                part = pl.ds(start, size)
                return ts_ref[c, k, part, :] if c < 2 else uv_ref[c - 2, k, part, :]
            lines = [line(c, k, start + i, halos) for i in range(0, size, TILE)]
            return lines[0] if len(lines) == 1 else jnp.concatenate(lines, axis=0)

        def load_up(i, rows=rows, block=block, fetch=fetch):
            k = levels - 1 - i
            halos = (south_ref[k] if block == 0 else None, north_ref[k] if block == blocks - 1 else None)
            turn = LANES - 2 - 3 * k
            east = [pltpu.roll(east_ref[g, rows, :], turn, 1) for g in range(2)]
            west = [pltpu.roll(west_ref[g, rows, :], turn, 1) for g in range(2)]
            lines = [{s: fetch(c, k, s, halos) for s in ((0, 1, -1, 2, -2) if c < 2 else (0, 1, -1))} for c in range(4)]
            flow = [flow_ref[i, k, rows, :] for i in range(2)]
            factors = [ref[k, rows, :] for ref in (w1_ref, w2_ref, h1_ref, h2_ref)]
            return east, west, lines, flow, factors

        def upward(i, loaded, below, cor=cor):
            k = levels - 1 - i
            east, west, lines, flow, factors = loaded
            flow_x = flow[0] * (ADVECT_COEF / 12.0)
            flow_y = flow[1] * (ADVECT_COEF / 12.0)
            rhs, diff_x, diff_y = [], [], []
            for c in range(2):
                mid = lines[c][0]
                e1 = pltpu.roll(jnp.where(low_one, east[c], mid), LANES - 1, 1)
                w1 = pltpu.roll(jnp.where(high_one, west[c], mid), 1, 1)
                e2 = pltpu.roll(jnp.where(low_two, east[c], mid), LANES - 2, 1)
                w2 = pltpu.roll(jnp.where(high_two, west[c], mid), 2, 1)
                n1, s1, n2, s2 = (lines[c][s] for s in (1, -1, 2, -2))
                dx, dy = e1 - w1, n1 - s1
                grad = flow_x * (8.0 * dx - (e2 - w2)) + flow_y * (8.0 * dy - (n2 - s2))
                near = (e1 + w1) + (n1 + s1)
                rhs.append((1.0 - 4.0 * DIFFUSE_COEF) * mid + DIFFUSE_COEF * near + grad)
                diff_x.append(dx)
                diff_y.append(dy)
            push = [
                (0.5 * PRESSURE_COEF) * (d[0] - SALINE_WEIGHT * d[1]) for d in (diff_x, diff_y)
            ]
            sides = []
            for c in range(2, 4):
                mid = lines[c][0]
                e1 = jnp.where(high_one, east[c - 2], pltpu.roll(mid, LANES - 1, 1))
                w1 = jnp.where(low_one, west[c - 2], pltpu.roll(mid, 1, 1))
                n1, s1 = lines[c][1], lines[c][-1]
                near = (e1 + w1) + (n1 + s1)
                sides.append(e1 - w1 if c == 2 else n1 - s1)
                rhs.append((1.0 - 4.0 * VISCOUS_COEF) * mid + VISCOUS_COEF * near - push[c - 2])
            spread = sides[0] + sides[1]
            rhs[0] = rhs[0] + (0.5 * THERMAL_COEF) * spread
            rhs[1] = rhs[1] - (0.5 * HALINE_COEF) * spread
            rhs[2] = rhs[2] + cor * lines[3][0]
            rhs[3] = rhs[3] - cor * lines[2][0]
            values = tuple(
                factors[c // 2] * rhs[c] + factors[2 + c // 2] * below[c] for c in range(4)
            )

            def store():
                for c in range(4):
                    value_ref[c, k] = values[c]

            return values, store

        top = loop(levels, load_up, upward, (zero,) * 4, UP_UNROLL)
        for c in range(2):
            surface_ref[c, rows, :] = top[c]

        def load_down(k, rows=rows):
            return [value_ref[c, k] for c in range(4)], (g1_ref[k, rows, :], g2_ref[k, rows, :])

        def downward(k, loaded, carry, rows=rows, block=block):
            above, acc = carry
            values, gains = loaded
            fields = tuple(values[c] + gains[c // 2] * above[c] for c in range(4))

            def store():
                if final:
                    u, v = fields[2], fields[3]
                    out_ref[0, k, rows, :] = fields[0]
                    out_ref[1, k, rows, :] = fields[1]
                    out_ref[2, k, rows, :] = cosine * u + sine * v
                    out_ref[3, k, rows, :] = cosine * v - sine * u
                    return
                for c in range(2):
                    ts_out[c, k, rows, :] = fields[c]
                    uv_out[c, k, rows, :] = fields[c + 2]
                store_edge_rows(k, fields, block, blocks - 1, south_out, north_out)

            return (fields, acc if final else pack_columns(acc, k, fields, lane)), store

        acc = () if final else (zero,) * 4
        _, acc = loop(levels, load_down, downward, ((zero,) * 4, acc), DOWN_UNROLL)
        if not final:
            for g in range(2):
                east_out[g, rows, :] = acc[g]
                west_out[g, rows, :] = acc[g + 2]


HIGHEST = lax.Precision.HIGHEST


def transform(parts, row_table_ref, col_table_ref, norm):
    height = parts[0].shape[1]
    out = []
    for c in range(2):
        total = None
        for i, part in enumerate(parts):
            table = row_table_ref[i * height : (i + 1) * height, :]
            piece = lax.dot_general(table, part[c], (((0,), (0,)), ((), ())), precision=HIGHEST, preferred_element_type=F32)
            total = piece if total is None else total + piece
        out.append(norm * jnp.dot(total, col_table_ref[...], precision=HIGHEST, preferred_element_type=F32))
    return out


def first_transform_kernel(norm, *refs):
    *parts, row_table_ref, col_table_ref, out_ref = refs
    for c, block in enumerate(transform(parts, row_table_ref, col_table_ref, norm)):
        out_ref[c * KY : (c + 1) * KY, :] = block


def second_transform_kernel(norm, count, slot_ref, valid_ref, *refs):
    refs, sends, table = refs[: -count - 1], refs[-count - 1 : -1], refs[-1]
    *parts, row_table_ref, col_table_ref, early_ref = refs
    table[0 : 2 * KY, :] = early_ref[...]
    for c, block in enumerate(transform(parts, row_table_ref, col_table_ref, norm)):
        table[(2 + c) * KY : (3 + c) * KY, :] = block
    for i, send in enumerate(sends):
        size = send.shape[0]
        start = pl.multiple_of(slot_ref[i] * size, TILE)
        mine = jnp.full((size, LANES), valid_ref[i], jnp.int32) > 0
        send[...] = jnp.where(mine, table[pl.ds(start, size), :], 0.0)


def call(kernel, outs, in_specs, scratch=()):
    many = isinstance(outs, (list, tuple))
    return pl.pallas_call(
        kernel,
        out_shape=outs,
        in_specs=in_specs,
        out_specs=[VMEM] * len(outs) if many else VMEM,
        scratch_shapes=list(scratch),
        compiler_params=pltpu.CompilerParams(vmem_limit_bytes=LIMIT),
    )


def exchange(south, north, east, west):
    ty, tx = lax.axis_size("ty"), lax.axis_size("tx")
    up = [(i, i + 1) for i in range(ty - 1)]
    down = [(i + 1, i) for i in range(ty - 1)]
    right = [(i, (i + 1) % tx) for i in range(tx)]
    left = [((i + 1) % tx, i) for i in range(tx)]
    return (
        lax.ppermute(north, "ty", up),
        lax.ppermute(south, "ty", down),
        lax.ppermute(west, "tx", left),
        lax.ppermute(east, "tx", right),
    )


def gather_rows(block):
    ty = lax.axis_size("ty")
    return [block] + [
        lax.ppermute(block, "ty", [(i, (i + s) % ty) for i in range(ty)]) for s in range(1, ty)
    ]


def cosine_table(rows, row_total, mode_count):
    modes = jnp.arange(mode_count, dtype=jnp.int32)
    phase_index = (2 * rows[:, None] + 1) * modes[None, :] % (4 * row_total)
    return jnp.cos(phase_index.astype(F32) * (math.pi / (2 * row_total)))


def body(adjoint, background_flow, vert_diff, wet_levels, rotation, face_map, ctrl_owner):
    _, levels, height, width = adjoint.shape
    ty, tx = lax.axis_size("ty"), lax.axis_size("tx")
    here_y, here_x = lax.axis_index("ty"), lax.axis_index("tx")
    rows_total, cols_total = height * ty, width * tx
    full = shape(levels, height, width)
    pair = shape(2, levels, height, width)
    edge_rows = [shape(levels, TILE, width)] * 2
    edge_cols = [shape(2, height, LANES)] * 2

    uv, *edges = call(prep_kernel, [pair] + edge_rows + edge_cols, [SMEM, VMEM])(rotation, adjoint)
    halos = exchange(*edges)
    factors = call(factor_kernel, [full] * 6, [VMEM] * 2)(vert_diff, wet_levels)

    rows = (here_y * height + jnp.arange(height, dtype=jnp.int32)).astype(F32)
    coriolis = CORIOLIS_PEAK * jnp.sin(math.pi * (rows + 0.5) / rows_total - 0.5 * math.pi)
    coriolis = jnp.broadcast_to(coriolis[:, None], (height, width))
    origin = (here_y - jnp.arange(ty, dtype=jnp.int32)) % ty
    source_rows = (origin[:, None] * height + jnp.arange(height, dtype=jnp.int32)[None, :]).reshape(-1)
    row_table = cosine_table(source_rows, rows_total, KY)
    col_table = cosine_table(here_x * width + jnp.arange(width, dtype=jnp.int32), cols_total, KX)
    norm = math.sqrt(2.0 * NFACE / (rows_total * cols_total))
    per_face = ctrl_owner.shape[0] // NFACE
    targets = here_y * tx + (here_x + jnp.arange(tx, dtype=jnp.int32)) % tx
    numbers = jnp.arange(ctrl_owner.shape[0], dtype=jnp.int32)
    owned = jnp.sum(jnp.where(ctrl_owner[None, :] == targets[:, None], numbers[None, :], 0), axis=1)
    slots = owned % per_face
    valid = (owned // per_face == face_map[0, 0]).astype(jnp.int32)

    scratch = [pltpu.VMEM((4, levels, STEP_ROWS, width), F32)]
    surface = shape(2, height, width)
    ts, uv, first, *edges = call(
        functools.partial(step_kernel, False),
        [pair, pair, surface] + edge_rows + edge_cols,
        [VMEM] * 14,
        scratch,
    )(adjoint, uv, background_flow, *factors, coriolis, *halos)
    halos = exchange(*edges)
    first_parts = gather_rows(first)
    early = call(
        functools.partial(first_transform_kernel, norm), shape(2 * KY, KX), [VMEM] * (ty + 2)
    )(*first_parts, row_table, col_table)
    adjoint_out, second = call(
        functools.partial(step_kernel, True),
        [shape(*adjoint.shape), surface],
        [SMEM] + [VMEM] * 14,
        scratch,
    )(rotation, ts, uv, background_flow, *factors, coriolis, *halos)
    second_parts = gather_rows(second)
    size = 4 * KY // per_face
    sends = call(
        functools.partial(second_transform_kernel, norm, tx),
        [shape(size, KX)] * tx,
        [SMEM] * 2 + [VMEM] * (ty + 3),
        [pltpu.VMEM((4 * KY, KX), F32)],
    )(slots, valid, *second_parts, row_table, col_table, early)
    total = sends[0]
    for s in range(1, tx):
        total = total + lax.ppermute(sends[s], "tx", [(i, (i + s) % tx) for i in range(tx)])
    return adjoint_out, total.reshape(1, -1)


def solution(mesh):
    return jax.shard_map(
        body,
        mesh=mesh,
        in_specs=(
            P(None, None, "ty", "tx"),
            P(None, None, "ty", "tx"),
            P(None, "ty", "tx"),
            P("ty", "tx"),
            P("ty", "tx"),
            P("ty", "tx"),
            P(),
        ),
        out_specs=(P(None, None, "ty", "tx"), P(("ty", "tx"), None)),
        check_vma=False,
    )
```

```python
import functools
import math

import jax
import jax.numpy as jnp
import numpy as np
from jax import lax
from jax.experimental import pallas as pl
from jax.experimental.pallas import tpu as pltpu
from jax.sharding import PartitionSpec as P

KY = 128
KX = 128
NFACE = 4

ADVECT_COEF = 0.3
DIFFUSE_COEF = 0.12
VISCOUS_COEF = 0.1
THERMAL_COEF = 0.4
HALINE_COEF = 0.3
PRESSURE_COEF = 0.4
SALINE_WEIGHT = 0.8
CORIOLIS_PEAK = 0.5
MOMENTUM_RATIO = 1.5

TILE = 8
LANES = 128
ANY = pl.BlockSpec(memory_space=pl.ANY)
VMEM = pl.BlockSpec(memory_space=pltpu.VMEM)
SMEM = pl.BlockSpec(memory_space=pltpu.SMEM)
F32 = jnp.float32
PREP_UNROLL = 6
FACTOR_ROWS, FACTOR_UNROLL = 64, 2
STEP_ROWS, UP_UNROLL, DOWN_UNROLL = 64, 4, 6


def shape(*dims):
    return jax.ShapeDtypeStruct(dims, F32)


def lanes_of(rows):
    return lax.broadcasted_iota(jnp.int32, (rows, LANES), 1)


def rows_of(rows):
    return lax.broadcasted_iota(jnp.int32, (rows, LANES), 0)


def loop(count, load, body, init, unroll):
    while count % unroll:
        unroll -= 1

    def several(i, carry):
        steps = [i * unroll + j for j in range(unroll)]
        loaded = [load(step) for step in steps]
        stores = []
        for step, values in zip(steps, loaded):
            carry, store = body(step, values, carry)
            stores.append(store)
        for store in stores:
            store()
        return carry

    return lax.fori_loop(0, count // unroll, several, init)


def turn_scalars(code):
    cosine = jnp.where(code == 0, 1.0, jnp.where(code == 2, -1.0, 0.0)).astype(F32)
    sine = jnp.where(code == 1, 1.0, jnp.where(code == 3, -1.0, 0.0)).astype(F32)
    return cosine, sine


def pack_columns(acc, k, fields, lane):
    at = 3 * k
    first, second, third = lane >= at, lane >= at + 1, lane >= at + 2
    east, west = [], []
    for g in range(2):
        tracer, flow = fields[g], fields[g + 2]
        rolled = pltpu.roll(tracer, at + 2, 1)
        east.append(jnp.where(first, jnp.where(third, pltpu.roll(flow, at + 3, 1), rolled), acc[g]))
        west.append(jnp.where(second, jnp.where(third, rolled, pltpu.roll(flow, at + 1, 1)), acc[g + 2]))
    return tuple(east + west)


def store_edge_rows(k, fields, block, last, south_ref, north_ref):
    size = fields[0].shape[0]
    for c in range(4):
        if block == 0:
            south_ref[k, 2 * c : 2 * c + 2, :] = fields[c][0:2, :]
        if block == last:
            north_ref[k, 2 * c : 2 * c + 2, :] = fields[c][size - 2 : size, :]


def write_messages(refs, south_ref, north_ref, east, west):
    row_a, row_b, col_a, col_b = refs
    even_y, even_x = lax.axis_index("ty") % 2 == 0, lax.axis_index("tx") % 2 == 0
    south, north = south_ref[...], north_ref[...]
    row_a[...] = jnp.where(even_y, north, south)
    row_b[...] = jnp.where(even_y, south, north)
    for rows, e, w in zip(east[0], east[1], west):
        for g in range(2):
            col_a[g, rows, :] = jnp.where(even_x, e[g], w[g])
            col_b[g, rows, :] = jnp.where(even_x, w[g], e[g])


def read_messages(refs, south_ref, north_ref, east_ref, west_ref):
    row_a, row_b, col_a, col_b = (ref[...] for ref in refs)
    here = lax.axis_index("ty")
    even_y, even_x = here % 2 == 0, lax.axis_index("tx") % 2 == 0
    south = jnp.where(even_y, row_b, row_a)
    north = jnp.where(even_y, row_a, row_b)
    south_ref[...] = jnp.where(here == 0, 0.0, south)
    north_ref[...] = jnp.where(here == lax.axis_size("ty") - 1, 0.0, north)
    east_ref[...] = jnp.where(even_x, col_a, col_b)
    west_ref[...] = jnp.where(even_x, col_b, col_a)


def prep_kernel(rot_ref, adj_ref, ts_ref, uv_ref, row_a, row_b, col_a, col_b, raw_ref, south_ref, north_ref, sems):
    levels, height = adj_ref.shape[1], adj_ref.shape[2]
    cosine, sine = turn_scalars(rot_ref[0, 0])
    step = PREP_UNROLL
    chunks = levels // step
    copies = []
    for i in range(chunks):
        part = pl.ds(i * step, step)
        for h, target in enumerate((ts_ref, raw_ref)):
            copy = pltpu.make_async_copy(adj_ref.at[pl.ds(2 * h, 2), part], target.at[:, part], sems.at[2 * i + h])
            copy.start()
            copies.append(copy)
    lane = lanes_of(height)
    zero = jnp.zeros((height, LANES), F32)
    acc = (zero,) * 4
    for i in range(chunks):
        copies[2 * i].wait()
        copies[2 * i + 1].wait()
        levels_here = range(i * step, (i + 1) * step)
        loaded = [(ts_ref[0, k], ts_ref[1, k], raw_ref[0, k], raw_ref[1, k]) for k in levels_here]
        stores = []
        for k, (t, s, a, b) in zip(levels_here, loaded):
            fields = (t, s, cosine * a - sine * b, sine * a + cosine * b)
            acc = pack_columns(acc, k, fields, lane)
            stores.append((k, fields))
        for k, fields in stores:
            uv_ref[0, k] = fields[2]
            uv_ref[1, k] = fields[3]
            store_edge_rows(k, fields, 0, 0, south_ref, north_ref)
    write_messages((row_a, row_b, col_a, col_b), south_ref, north_ref, ([pl.ds(0, height)], [acc[:2]]), [acc[2:]])


def factor_kernel(vd_ref, wet_ref, w1_ref, w2_ref, h1_ref, h2_ref, g1_ref, g2_ref):
    levels, height = vd_ref.shape[0], vd_ref.shape[1]
    out = ((w1_ref, h1_ref, g1_ref, 1.0), (w2_ref, h2_ref, g2_ref, MOMENTUM_RATIO))
    size = FACTOR_ROWS
    for block in range(height // size):
        rows = pl.ds(block * size, size)
        wet = wet_ref[rows, :]
        zero = jnp.zeros((size, LANES), F32)

        def load(i, rows=rows):
            return vd_ref[jnp.maximum(levels - 2 - i, 0), rows, :]

        def level(i, loaded, carry, rows=rows, wet=wet):
            k = levels - 1 - i
            below, inverses = carry
            mask = jnp.where(k < wet, 1.0, 0.0).astype(F32)
            above = jnp.where(k > 0, loaded * mask, 0.0)
            kept, stores = [], []
            for (w_ref, h_ref, g_ref, factor), inverse in zip(out, inverses):
                low, high = factor * below, factor * above
                pivot = 1.0 + high + low - low * (low * inverse)
                inverse = 1.0 / pivot
                masked = inverse * mask
                stores += [(w_ref, masked), (h_ref, low * masked), (g_ref, high * masked)]
                kept.append(inverse)

            def store():
                for ref, value in stores:
                    ref[k, rows, :] = value

            return (above, tuple(kept)), store

        loop(levels, load, level, (zero, (zero, zero)), FACTOR_UNROLL)


def step_kernel(final, *refs):
    ts_ref, uv_ref, flow_ref, w1_ref, w2_ref, h1_ref, h2_ref = refs[:7]
    if final:
        cor_ref, *messages = refs[7:12]
        first_ref, value_ref, surface_ref = refs[12:15]
        surface_ref[0:2] = first_ref[...]
        surface_at = 2
    else:
        g1_ref, g2_ref, cor_ref, *messages = refs[7:14]
        ts_out, uv_out, surface_ref, *sent = refs[14:21]
        value_ref, south_out, north_out = refs[21:24]
        surface_at = 0
    south_ref, north_ref, east_ref, west_ref = refs[-4:]
    read_messages(messages, south_ref, north_ref, east_ref, west_ref)
    levels, height = ts_ref.shape[1], ts_ref.shape[2]
    size = STEP_ROWS
    blocks = height // size
    lane, row = lanes_of(size), rows_of(size)
    low_two, high_two = lane < 2, lane >= LANES - 2
    low_one, high_one = lane < 1, lane >= LANES - 1
    zero = jnp.zeros((size, LANES), F32)
    first_cor = pl.multiple_of(lax.axis_index("ty") * height, TILE)
    packed = []

    def get(c, k, start):
        rows = pl.ds(start, TILE)
        return ts_ref[c, k, rows, :] if c < 2 else uv_ref[c - 2, k, rows, :]

    def line(c, k, start, halos):
        if 0 <= start <= height - TILE:
            return get(c, k, start)
        south, north = halos
        part = rows_of(TILE)
        if start < 0:
            halo = pltpu.roll(south, (-2 * c - 2 - start) % TILE, 0)
            return jnp.where(part < -start, halo, pltpu.roll(get(c, k, 0), -start, 0))
        over = start + TILE - height
        halo = pltpu.roll(north, (TILE - over - 2 * c) % TILE, 0)
        return jnp.where(part >= TILE - over, halo, pltpu.roll(get(c, k, height - TILE), TILE - over, 0))

    for block in range(blocks):
        rows = pl.ds(block * size, size)
        first_row = block * size
        cor = cor_ref[pl.ds(first_cor + block * size, size), :]

        def fetch(c, k, shift, halos, first_row=first_row):
            start = first_row + shift
            if 0 <= start <= height - size:
                part = pl.ds(start, size)
                return ts_ref[c, k, part, :] if c < 2 else uv_ref[c - 2, k, part, :]
            lines = [line(c, k, start + i, halos) for i in range(0, size, TILE)]
            return lines[0] if len(lines) == 1 else jnp.concatenate(lines, axis=0)

        def load_up(i, rows=rows, block=block, fetch=fetch):
            k = levels - 1 - i
            halos = (south_ref[k] if block == 0 else None, north_ref[k] if block == blocks - 1 else None)
            turn = LANES - 2 - 3 * k
            east = [pltpu.roll(east_ref[g, rows, :], turn, 1) for g in range(2)]
            west = [pltpu.roll(west_ref[g, rows, :], turn, 1) for g in range(2)]
            lines = [{s: fetch(c, k, s, halos) for s in ((0, 1, -1, 2, -2) if c < 2 else (0, 1, -1))} for c in range(4)]
            flow = [flow_ref[i, k, rows, :] for i in range(2)]
            factors = [ref[k, rows, :] for ref in (w1_ref, w2_ref, h1_ref, h2_ref)]
            return east, west, lines, flow, factors

        def upward(i, loaded, below, cor=cor, rows=rows):
            k = levels - 1 - i
            east, west, lines, flow, factors = loaded
            flow_x = flow[0] * (ADVECT_COEF / 12.0)
            flow_y = flow[1] * (ADVECT_COEF / 12.0)
            rhs, diff_x, diff_y = [], [], []
            for c in range(2):
                mid = lines[c][0]
                e1 = pltpu.roll(jnp.where(low_one, east[c], mid), LANES - 1, 1)
                w1 = pltpu.roll(jnp.where(high_one, west[c], mid), 1, 1)
                e2 = pltpu.roll(jnp.where(low_two, east[c], mid), LANES - 2, 1)
                w2 = pltpu.roll(jnp.where(high_two, west[c], mid), 2, 1)
                n1, s1, n2, s2 = (lines[c][s] for s in (1, -1, 2, -2))
                dx, dy = e1 - w1, n1 - s1
                grad = flow_x * (8.0 * dx - (e2 - w2)) + flow_y * (8.0 * dy - (n2 - s2))
                near = (e1 + w1) + (n1 + s1)
                rhs.append((1.0 - 4.0 * DIFFUSE_COEF) * mid + DIFFUSE_COEF * near + grad)
                diff_x.append(dx)
                diff_y.append(dy)
            push = [
                (0.5 * PRESSURE_COEF) * (d[0] - SALINE_WEIGHT * d[1]) for d in (diff_x, diff_y)
            ]
            sides = []
            for c in range(2, 4):
                mid = lines[c][0]
                e1 = jnp.where(high_one, east[c - 2], pltpu.roll(mid, LANES - 1, 1))
                w1 = jnp.where(low_one, west[c - 2], pltpu.roll(mid, 1, 1))
                n1, s1 = lines[c][1], lines[c][-1]
                near = (e1 + w1) + (n1 + s1)
                sides.append(e1 - w1 if c == 2 else n1 - s1)
                rhs.append((1.0 - 4.0 * VISCOUS_COEF) * mid + VISCOUS_COEF * near - push[c - 2])
            spread = sides[0] + sides[1]
            rhs[0] = rhs[0] + (0.5 * THERMAL_COEF) * spread
            rhs[1] = rhs[1] - (0.5 * HALINE_COEF) * spread
            rhs[2] = rhs[2] + cor * lines[3][0]
            rhs[3] = rhs[3] - cor * lines[2][0]
            values = tuple(
                factors[c // 2] * rhs[c] + factors[2 + c // 2] * below[c] for c in range(4)
            )

            def store():
                for c in range(4):
                    value_ref[c, k, rows, :] = values[c]

            return values, store

        top = loop(levels, load_up, upward, (zero,) * 4, UP_UNROLL)
        for c in range(2):
            surface_ref[surface_at + c, rows, :] = top[c]
        if final:
            continue

        def load_down(k, rows=rows):
            return [value_ref[c, k, rows, :] for c in range(4)], (g1_ref[k, rows, :], g2_ref[k, rows, :])

        def downward(k, loaded, carry, rows=rows, block=block):
            above, acc = carry
            values, gains = loaded
            fields = tuple(values[c] + gains[c // 2] * above[c] for c in range(4))

            def store():
                for c in range(2):
                    ts_out[c, k, rows, :] = fields[c]
                    uv_out[c, k, rows, :] = fields[c + 2]
                store_edge_rows(k, fields, block, blocks - 1, south_out, north_out)

            return (fields, pack_columns(acc, k, fields, lane)), store

        _, acc = loop(levels, load_down, downward, ((zero,) * 4, (zero,) * 4), DOWN_UNROLL)
        packed.append((rows, acc[:2], acc[2:]))
    if not final:
        parts, east, west = zip(*packed)
        write_messages(sent, south_out, north_out, (parts, east), west)


def last_kernel(rot_ref, value_ref, g1_ref, g2_ref, out_ref, field_ref, sems):
    levels = value_ref.shape[1]
    cosine, sine = turn_scalars(rot_ref[0, 0])
    step = DOWN_UNROLL
    above, copies = None, []
    for i in range(levels // step):
        group = range(i * step, (i + 1) * step)
        loaded = [([value_ref[c, k] for c in range(4)], (g1_ref[k], g2_ref[k])) for k in group]
        done = []
        for values, gains in loaded:
            if above is not None:
                values = [values[c] + gains[c // 2] * above[c] for c in range(4)]
            above = values
            u, v = values[2:]
            done.append((values[0], values[1], cosine * u + sine * v, cosine * v - sine * u))
        for k, fields in zip(group, done):
            for c in range(4):
                field_ref[c, k] = fields[c]
        part = pl.ds(i * step, step)
        copy = pltpu.make_async_copy(field_ref.at[:, part], out_ref.at[:, part], sems.at[i])
        copy.start()
        copies.append(copy)
    for copy in copies:
        copy.wait()


HIGHEST = lax.Precision.HIGHEST


def halving_order(count):
    bits = [1 << i for i in range(1, count.bit_length() - 1)]
    order = [0]
    for bit in reversed(bits):
        order = order + [place | bit for place in order]
    return order


def transform_kernel(count, norm, owner_ref, face_ref, row_table_ref, col_table_ref, *refs):
    parts, (keep_ref, send_ref, cells, table, inverse) = refs[: -5], refs[-5:]
    height, width = parts[0].shape[1:]
    here_y, here_x = lax.axis_index("ty"), lax.axis_index("tx")
    targets = owner_ref.shape[0]
    per_face = targets // NFACE

    def note(i, _):
        inverse[owner_ref[i]] = i
        return 0

    lax.fori_loop(0, targets, note, 0)
    for i, part in enumerate(parts):
        rows = pl.ds(pl.multiple_of((here_y ^ i) * height, TILE), height)
        for c in range(4):
            cells[rows, c * width : (c + 1) * width] = part[c]
    along_rows = jnp.dot(row_table_ref[...], cells[...], precision=HIGHEST, preferred_element_type=F32)
    stacked = jnp.concatenate([along_rows[:, c * width : (c + 1) * width] for c in range(4)], axis=0)
    columns = col_table_ref[pl.ds(pl.multiple_of(here_x * width, TILE), width), :]
    table[...] = norm * jnp.dot(stacked, columns, precision=HIGHEST, preferred_element_type=F32)
    size = table.shape[0] // per_face
    for i, place in enumerate(halving_order(count)):
        for ref, relative in ((keep_ref, place), (send_ref, place ^ 1)):
            tile = inverse[here_y * count + (here_x ^ relative)]
            start = pl.multiple_of(lax.rem(tile, per_face) * size, TILE)
            mine = lax.div(tile, per_face) == face_ref[0, 0]
            ref[i * size : (i + 1) * size, :] = jnp.where(mine, table[pl.ds(start, size), :], 0.0)


def call(kernel, outs, in_specs, scratch=(), out_specs=None, limit=4):
    many = isinstance(outs, (list, tuple))
    return pl.pallas_call(
        kernel,
        out_shape=outs,
        in_specs=in_specs,
        out_specs=out_specs or ([VMEM] * len(outs) if many else VMEM),
        scratch_shapes=list(scratch),
        compiler_params=pltpu.CompilerParams(vmem_limit_bytes=limit << 20),
    )


def swap(block, axis, bit):
    return lax.ppermute(block, axis, [(i, i ^ bit) for i in range(lax.axis_size(axis))])


def exchange(row_a, row_b, col_a, col_b):
    received = []
    for axis, first, second in (("ty", row_a, row_b), ("tx", col_a, col_b)):
        count = lax.axis_size(axis)
        others = [(i, (i + 1 if i % 2 else i - 1) % count) for i in range(count)]
        received += [swap(first, axis, 1), lax.ppermute(second, axis, others)]
    return received


def cosines(total, mode_count):
    phase = (2 * np.arange(total)[:, None] + 1) * np.arange(mode_count)[None, :] % (4 * total)
    return np.cos(phase * (math.pi / (2 * total)))


def body(adjoint, background_flow, vert_diff, wet_levels, rotation, face_map, ctrl_owner):
    _, levels, height, width = adjoint.shape
    ty, tx = lax.axis_size("ty"), lax.axis_size("tx")
    rows_total, cols_total = height * ty, width * tx
    full = shape(levels, height, width)
    pair = shape(2, levels, height, width)
    messages = [shape(levels, TILE, width)] * 2 + [shape(2, height, LANES)] * 2
    rows_scratch = [pltpu.VMEM((levels, TILE, width), F32)] * 2
    halo_scratch = rows_scratch + [pltpu.VMEM((2, height, LANES), F32)] * 2
    whole_scratch = pltpu.VMEM((4, levels, height, width), F32)

    places = np.arange(rows_total)
    coriolis = CORIOLIS_PEAK * np.sin(math.pi * (places + 0.5) / rows_total - 0.5 * math.pi)
    coriolis = jnp.asarray(np.repeat(coriolis[:, None], width, axis=1), F32)
    row_table = jnp.asarray(cosines(rows_total, KY).T, F32)
    col_table = jnp.asarray(cosines(cols_total, KX), F32)
    norm = math.sqrt(2.0 * NFACE / (rows_total * cols_total))

    ts, uv, *sent = call(
        prep_kernel,
        [pair, pair] + messages,
        [SMEM, ANY],
        [pltpu.VMEM((2, levels, height, width), F32)] + rows_scratch + [pltpu.SemaphoreType.DMA((2 * levels // PREP_UNROLL,))],
        limit=6,
    )(rotation, adjoint)
    received = exchange(*sent)
    w1, w2, h1, h2, g1, g2 = call(factor_kernel, [full] * 6, [VMEM] * 2)(vert_diff, wet_levels)
    ts, uv, first, *sent = call(
        functools.partial(step_kernel, False),
        [pair, pair, shape(2, height, width)] + messages,
        [VMEM] * 14,
        [whole_scratch] + rows_scratch + halo_scratch,
        limit=12,
    )(ts, uv, background_flow, w1, w2, h1, h2, g1, g2, coriolis, *received)
    received = exchange(*sent)
    values, surfaces = call(
        functools.partial(step_kernel, True),
        [shape(4, levels, height, width), shape(4, height, width)],
        [VMEM] * 13,
        halo_scratch,
        limit=8,
    )(ts, uv, background_flow, w1, w2, h1, h2, coriolis, *received, first)
    parts = [surfaces] + [swap(surfaces, "ty", bit) for bit in range(1, ty)]
    adjoint_out = call(
        last_kernel,
        shape(*adjoint.shape),
        [SMEM] + [VMEM] * 3,
        [whole_scratch, pltpu.SemaphoreType.DMA((levels // DOWN_UNROLL,))],
        out_specs=ANY,
        limit=8,
    )(rotation, values, g1, g2)
    size = 4 * KY * NFACE // ctrl_owner.shape[0]
    keep, send = call(
        functools.partial(transform_kernel, tx, norm),
        [shape(size * tx // 2, KX)] * 2,
        [SMEM] * 2 + [VMEM] * (ty + 2),
        [pltpu.VMEM((rows_total, 4 * width), F32), pltpu.VMEM((4 * KY, KX), F32), pltpu.SMEM(ctrl_owner.shape, jnp.int32)],
        limit=6,
    )(ctrl_owner, face_map, row_table, col_table, *parts)
    bit = 1
    while True:
        keep = keep + swap(send, "tx", bit)
        bit *= 2
        if bit == tx:
            break
        half = keep.shape[0] // 2
        keep, send = keep[:half], keep[half:]
    return adjoint_out, keep.reshape(1, -1)


def solution(mesh):
    return jax.shard_map(
        body,
        mesh=mesh,
        in_specs=(
            P(None, None, "ty", "tx"),
            P(None, None, "ty", "tx"),
            P(None, "ty", "tx"),
            P("ty", "tx"),
            P("ty", "tx"),
            P("ty", "tx"),
            P(),
        ),
        out_specs=(P(None, None, "ty", "tx"), P(("ty", "tx"), None)),
        check_vma=False,
    )
```

```python
import functools
import math

import jax
import jax.numpy as jnp
import numpy as np
from jax import lax
from jax.experimental import pallas as pl
from jax.experimental.pallas import tpu as pltpu
from jax.sharding import PartitionSpec as P

KY = 128
KX = 128
NFACE = 4

ADVECT_COEF = 0.3
DIFFUSE_COEF = 0.12
VISCOUS_COEF = 0.1
THERMAL_COEF = 0.4
HALINE_COEF = 0.3
PRESSURE_COEF = 0.4
SALINE_WEIGHT = 0.8
CORIOLIS_PEAK = 0.5
MOMENTUM_RATIO = 1.5

TILE = 8
LANES = 128
ANY = pl.BlockSpec(memory_space=pl.ANY)
VMEM = pl.BlockSpec(memory_space=pltpu.VMEM)
SMEM = pl.BlockSpec(memory_space=pltpu.SMEM)
F32 = jnp.float32
PREP_UNROLL = 6
FACTOR_ROWS, FACTOR_UNROLL = 64, 2
UNROLLS = {16: (6, 9), 32: (4, 6)}
DOWN_UNROLL = 6
EDGE = 16


def shape(*dims):
    return jax.ShapeDtypeStruct(dims, F32)


def lanes_of(rows):
    return lax.broadcasted_iota(jnp.int32, (rows, LANES), 1)


def rows_of(rows):
    return lax.broadcasted_iota(jnp.int32, (rows, LANES), 0)


def loop(count, load, body, init, unroll):
    while count % unroll:
        unroll -= 1

    def several(i, carry):
        steps = [i * unroll + j for j in range(unroll)]
        loaded = [load(step) for step in steps]
        stores = []
        for step, values in zip(steps, loaded):
            carry, store = body(step, values, carry)
            stores.append(store)
        for store in stores:
            store()
        return carry

    return lax.fori_loop(0, count // unroll, several, init)


def turn_scalars(code):
    cosine = jnp.where(code == 0, 1.0, jnp.where(code == 2, -1.0, 0.0)).astype(F32)
    sine = jnp.where(code == 1, 1.0, jnp.where(code == 3, -1.0, 0.0)).astype(F32)
    return cosine, sine


def pack_columns(acc, k, fields, lane):
    at = 3 * k
    first, second, third = lane >= at, lane >= at + 1, lane >= at + 2
    east, west = [], []
    for g in range(2):
        tracer, flow = fields[g], fields[g + 2]
        rolled = pltpu.roll(tracer, at + 2, 1)
        east.append(jnp.where(first, jnp.where(third, pltpu.roll(flow, at + 3, 1), rolled), acc[g]))
        west.append(jnp.where(second, jnp.where(third, rolled, pltpu.roll(flow, at + 1, 1)), acc[g + 2]))
    return tuple(east + west)


def store_edge_rows(k, fields, block, last, south_ref, north_ref):
    size = fields[0].shape[0]
    for c in range(4):
        if block == 0:
            south_ref[k, 2 * c : 2 * c + 2, :] = fields[c][0:2, :]
        if block == last or block is last:
            north_ref[k, 2 * c : 2 * c + 2, :] = fields[c][size - 2 : size, :]


def write_rows(row_a, row_b, south_ref, north_ref):
    even = lax.axis_index("ty") % 2 == 0
    south, north = south_ref[...], north_ref[...]
    row_a[...] = jnp.where(even, north, south)
    row_b[...] = jnp.where(even, south, north)


def write_columns(col_a, col_b, east, west):
    even = lax.axis_index("tx") % 2 == 0
    col_a[...] = jnp.where(even, east, west)
    col_b[...] = jnp.where(even, west, east)


def read_rows(row_a, row_b, south_ref, north_ref):
    here = lax.axis_index("ty")
    even = here % 2 == 0
    first, second = row_a[...], row_b[...]
    south_ref[...] = jnp.where(here == 0, 0.0, jnp.where(even, second, first))
    north_ref[...] = jnp.where(here == lax.axis_size("ty") - 1, 0.0, jnp.where(even, first, second))


def read_columns(col_a, col_b, east_ref, west_ref):
    even = lax.axis_index("tx") % 2 == 0
    first, second = col_a[...], col_b[...]
    east_ref[...] = jnp.where(even, first, second)
    west_ref[...] = jnp.where(even, second, first)


def prep_rows_kernel(rot_ref, adj_ref, row_a, row_b, raw_ref, south_ref, north_ref, sems):
    levels, height = adj_ref.shape[1], adj_ref.shape[2]
    cosine, sine = turn_scalars(rot_ref[0, 0])
    copies = []
    for i, start in enumerate((0, height - TILE)):
        copies.append(pltpu.make_async_copy(adj_ref.at[:, :, pl.ds(start, TILE)], raw_ref.at[i], sems.at[i]))
        copies[-1].start()
    for copy in copies:
        copy.wait()

    def load(k):
        return [[raw_ref[i, c, k] for c in range(4)] for i in range(2)]

    def level(k, loaded, carry):
        rotated = [(t, s, cosine * a - sine * b, sine * a + cosine * b) for t, s, a, b in loaded]

        def store():
            store_edge_rows(k, rotated[0], 0, None, south_ref, north_ref)
            store_edge_rows(k, rotated[1], None, None, south_ref, north_ref)

        return carry, store

    loop(levels, load, level, 0, 6)
    write_rows(row_a, row_b, south_ref, north_ref)


def prep_columns_kernel(rot_ref, adj_ref, ts_ref, uv_ref, col_a, col_b, raw_ref, sems):
    levels, height = adj_ref.shape[1], adj_ref.shape[2]
    cosine, sine = turn_scalars(rot_ref[0, 0])
    step = PREP_UNROLL
    chunks = levels // step
    copies = []
    for i in range(chunks):
        part = pl.ds(i * step, step)
        for h, target in enumerate((ts_ref, raw_ref)):
            copy = pltpu.make_async_copy(adj_ref.at[pl.ds(2 * h, 2), part], target.at[:, part], sems.at[2 * i + h])
            copy.start()
            copies.append(copy)
    lane = lanes_of(height)
    zero = jnp.zeros((height, LANES), F32)
    acc = (zero,) * 4
    for i in range(chunks):
        copies[2 * i].wait()
        copies[2 * i + 1].wait()
        group = range(i * step, (i + 1) * step)
        loaded = [(ts_ref[0, k], ts_ref[1, k], raw_ref[0, k], raw_ref[1, k]) for k in group]
        stores = []
        for k, (t, s, a, b) in zip(group, loaded):
            fields = (t, s, cosine * a - sine * b, sine * a + cosine * b)
            acc = pack_columns(acc, k, fields, lane)
            stores.append((k, fields))
        for k, fields in stores:
            uv_ref[0, k] = fields[2]
            uv_ref[1, k] = fields[3]
    write_columns(col_a, col_b, jnp.stack(acc[:2]), jnp.stack(acc[2:]))


def factor_kernel(vd_ref, wet_ref, w1_ref, w2_ref, h1_ref, h2_ref, g1_ref, g2_ref):
    levels, height = vd_ref.shape[0], vd_ref.shape[1]
    out = ((w1_ref, h1_ref, g1_ref, 1.0), (w2_ref, h2_ref, g2_ref, MOMENTUM_RATIO))
    size = FACTOR_ROWS
    for block in range(height // size):
        rows = pl.ds(block * size, size)
        wet = wet_ref[rows, :]
        zero = jnp.zeros((size, LANES), F32)

        def load(i, rows=rows):
            return vd_ref[jnp.maximum(levels - 2 - i, 0), rows, :]

        def level(i, loaded, carry, rows=rows, wet=wet):
            k = levels - 1 - i
            below, inverses = carry
            mask = jnp.where(k < wet, 1.0, 0.0).astype(F32)
            above = jnp.where(k > 0, loaded * mask, 0.0)
            kept, stores = [], []
            for (w_ref, h_ref, g_ref, factor), inverse in zip(out, inverses):
                low, high = factor * below, factor * above
                pivot = 1.0 + high + low - low * (low * inverse)
                inverse = 1.0 / pivot
                masked = inverse * mask
                stores += [(w_ref, masked), (h_ref, low * masked), (g_ref, high * masked)]
                kept.append(inverse)

            def store():
                for ref, value in stores:
                    ref[k, rows, :] = value

            return (above, tuple(kept)), store

        loop(levels, load, level, (zero, (zero, zero)), FACTOR_UNROLL)


def step_kernel(stage, blocks, *refs):
    refs = list(refs)

    def take(count):
        taken, refs[:] = refs[:count], refs[count:]
        return taken

    ts_ref, uv_ref, flow_ref, w1_ref, w2_ref, h1_ref, h2_ref, cor_ref, col_a, col_b = take(10)
    south_ref = north_ref = None
    if stage != "middle":
        row_a, row_b = take(2)
    if stage == "up":
        (first_ref,) = take(1)
        value_ref, surface_ref = take(2)
        surface_ref[0:2] = first_ref[...]
    else:
        g1_ref, g2_ref = take(2)
        if stage == "middle":
            ts_in, uv_in, surface_in, east_in, west_in = take(5)
            ts_out, uv_out, surface_ref, east_out, west_out = take(5)
        else:
            ts_out, uv_out, surface_ref, east_out, west_out, sent_a, sent_b = take(7)
            south_out, north_out = take(2)
        (value_ref,) = take(1)
    east_ref, west_ref = take(2)
    read_columns(col_a, col_b, east_ref, west_ref)
    if stage != "middle":
        south_ref, north_ref = take(2)
        read_rows(row_a, row_b, south_ref, north_ref)
    levels, height = ts_ref.shape[1], ts_ref.shape[2]
    first_cor = pl.multiple_of(lax.axis_index("ty") * height, TILE)
    packed = {}
    done, others = (), ()
    if stage == "middle":
        ((first_row, size),) = blocks
        done = ((ts_in, ts_out), (uv_in, uv_out))
        others = (pl.ds(0, first_row), pl.ds(first_row + size, height - first_row - size))

    def get(c, k, start):
        rows = pl.ds(start, TILE)
        return ts_ref[c, k, rows, :] if c < 2 else uv_ref[c - 2, k, rows, :]

    def line(c, k, start, halos):
        if 0 <= start <= height - TILE:
            return get(c, k, start)
        south, north = halos
        part = rows_of(TILE)
        if start < 0:
            halo = pltpu.roll(south, (-2 * c - 2 - start) % TILE, 0)
            return jnp.where(part < -start, halo, pltpu.roll(get(c, k, 0), -start, 0))
        over = start + TILE - height
        halo = pltpu.roll(north, (TILE - over - 2 * c) % TILE, 0)
        return jnp.where(part >= TILE - over, halo, pltpu.roll(get(c, k, height - TILE), TILE - over, 0))

    for block, (first_row, size) in enumerate(blocks):
        lane = lanes_of(size)
        low_two, high_two = lane < 2, lane >= LANES - 2
        low_one, high_one = lane < 1, lane >= LANES - 1
        zero = jnp.zeros((size, LANES), F32)
        rows = pl.ds(first_row, size)
        kept_rows = rows if stage == "up" else pl.ds(0, size)
        south_end, north_end = first_row == 0, first_row + size == height
        cor = cor_ref[pl.ds(first_cor + first_row, size), :]
        up_unroll, down_unroll = UNROLLS[min(size, 32)]

        def fetch(c, k, shift, halos, first_row=first_row, size=size):
            start = first_row + shift
            if 0 <= start <= height - size:
                part = pl.ds(start, size)
                return ts_ref[c, k, part, :] if c < 2 else uv_ref[c - 2, k, part, :]
            lines = [line(c, k, start + i, halos) for i in range(0, size, TILE)]
            return lines[0] if len(lines) == 1 else jnp.concatenate(lines, axis=0)

        def load_up(i, rows=rows, ends=(south_end, north_end), fetch=fetch):
            k = levels - 1 - i
            halos = (south_ref[k] if ends[0] else None, north_ref[k] if ends[1] else None)
            turn = LANES - 2 - 3 * k
            east = [pltpu.roll(east_ref[g, rows, :], turn, 1) for g in range(2)]
            west = [pltpu.roll(west_ref[g, rows, :], turn, 1) for g in range(2)]
            lines = [{s: fetch(c, k, s, halos) for s in ((0, 1, -1, 2, -2) if c < 2 else (0, 1, -1))} for c in range(4)]
            flow = [flow_ref[i, k, rows, :] for i in range(2)]
            factors = [ref[k, rows, :] for ref in (w1_ref, w2_ref, h1_ref, h2_ref)]
            return east, west, lines, flow, factors

        def upward(i, loaded, below, cor=cor, rows=kept_rows):
            k = levels - 1 - i
            east, west, lines, flow, factors = loaded
            flow_x = flow[0] * (ADVECT_COEF / 12.0)
            flow_y = flow[1] * (ADVECT_COEF / 12.0)
            rhs, diff_x, diff_y = [], [], []
            for c in range(2):
                mid = lines[c][0]
                e1 = pltpu.roll(jnp.where(low_one, east[c], mid), LANES - 1, 1)
                w1 = pltpu.roll(jnp.where(high_one, west[c], mid), 1, 1)
                e2 = pltpu.roll(jnp.where(low_two, east[c], mid), LANES - 2, 1)
                w2 = pltpu.roll(jnp.where(high_two, west[c], mid), 2, 1)
                n1, s1, n2, s2 = (lines[c][s] for s in (1, -1, 2, -2))
                dx, dy = e1 - w1, n1 - s1
                grad = flow_x * (8.0 * dx - (e2 - w2)) + flow_y * (8.0 * dy - (n2 - s2))
                near = (e1 + w1) + (n1 + s1)
                rhs.append((1.0 - 4.0 * DIFFUSE_COEF) * mid + DIFFUSE_COEF * near + grad)
                diff_x.append(dx)
                diff_y.append(dy)
            push = [
                (0.5 * PRESSURE_COEF) * (d[0] - SALINE_WEIGHT * d[1]) for d in (diff_x, diff_y)
            ]
            sides = []
            for c in range(2, 4):
                mid = lines[c][0]
                e1 = jnp.where(high_one, east[c - 2], pltpu.roll(mid, LANES - 1, 1))
                w1 = jnp.where(low_one, west[c - 2], pltpu.roll(mid, 1, 1))
                n1, s1 = lines[c][1], lines[c][-1]
                near = (e1 + w1) + (n1 + s1)
                sides.append(e1 - w1 if c == 2 else n1 - s1)
                rhs.append((1.0 - 4.0 * VISCOUS_COEF) * mid + VISCOUS_COEF * near - push[c - 2])
            spread = sides[0] + sides[1]
            rhs[0] = rhs[0] + (0.5 * THERMAL_COEF) * spread
            rhs[1] = rhs[1] - (0.5 * HALINE_COEF) * spread
            rhs[2] = rhs[2] + cor * lines[3][0]
            rhs[3] = rhs[3] - cor * lines[2][0]
            values = tuple(
                factors[c // 2] * rhs[c] + factors[2 + c // 2] * below[c] for c in range(4)
            )

            def store():
                for c in range(4):
                    value_ref[c, k, rows, :] = values[c]

            return values, store

        top = loop(levels, load_up, upward, (zero,) * 4, up_unroll)
        for c in range(2):
            surface_ref[(2 if stage == "up" else 0) + c, rows, :] = top[c]
        if stage == "up":
            continue

        def load_down(k, rows=rows, kept_rows=kept_rows):
            passed = [
                (source, target, c, part, source[c, k, part, :])
                for source, target in done
                for c in range(2)
                for part in others
            ]
            values = [value_ref[c, k, kept_rows, :] for c in range(4)]
            return values, (g1_ref[k, rows, :], g2_ref[k, rows, :]), passed

        def downward(k, loaded, carry, rows=rows, ends=(south_end, north_end), lane=lane):
            above, acc = carry
            values, gains, passed = loaded
            fields = tuple(values[c] + gains[c // 2] * above[c] for c in range(4))

            def store():
                for c in range(2):
                    ts_out[c, k, rows, :] = fields[c]
                    uv_out[c, k, rows, :] = fields[c + 2]
                for _, target, c, part, value in passed:
                    target[c, k, part, :] = value
                if ends[0] or ends[1]:
                    store_edge_rows(k, fields, 0 if ends[0] else 1, 1 if ends[1] else 2, south_out, north_out)

            return (fields, pack_columns(acc, k, fields, lane)), store

        _, acc = loop(levels, load_down, downward, ((zero,) * 4, (zero,) * 4), down_unroll)
        packed[first_row] = acc
    if stage == "edge":
        for (first_row, size), acc in zip(blocks, packed.values()):
            for g in range(2):
                east_out[g, pl.ds(first_row, size), :] = acc[g]
                west_out[g, pl.ds(first_row, size), :] = acc[g + 2]
        write_rows(sent_a, sent_b, south_out, north_out)
    if stage == "middle":
        for c in range(2):
            for part in others:
                surface_ref[c, part, :] = surface_in[c, part, :]
        acc = packed[first_row]
        spans = (slice(0, first_row), slice(first_row + size, height))
        east, west = (
            jnp.stack([jnp.concatenate([ref[g, spans[0], :], acc[g + at], ref[g, spans[1], :]], axis=0) for g in range(2)])
            for ref, at in ((east_in, 0), (west_in, 2))
        )
        write_columns(east_out, west_out, east, west)


def last_kernel(rot_ref, value_ref, g1_ref, g2_ref, out_ref, token_ref, field_ref, sems):
    token_ref[...] = jnp.zeros_like(token_ref)
    levels = value_ref.shape[1]
    cosine, sine = turn_scalars(rot_ref[0, 0])
    step = DOWN_UNROLL
    above, copies = None, []
    for i in range(levels // step):
        group = range(i * step, (i + 1) * step)
        loaded = [([value_ref[c, k] for c in range(4)], (g1_ref[k], g2_ref[k])) for k in group]
        done = []
        for values, gains in loaded:
            if above is not None:
                values = [values[c] + gains[c // 2] * above[c] for c in range(4)]
            above = values
            u, v = values[2:]
            done.append((values[0], values[1], cosine * u + sine * v, cosine * v - sine * u))
        for k, fields in zip(group, done):
            for c in range(4):
                field_ref[c, k] = fields[c]
        part = pl.ds(i * step, step)
        copy = pltpu.make_async_copy(field_ref.at[:, part], out_ref.at[:, part], sems.at[i])
        copy.start()
        copies.append(copy)
    for copy in copies:
        copy.wait()


HIGHEST = lax.Precision.HIGHEST


def halving_order(count):
    bits = [1 << i for i in range(1, count.bit_length() - 1)]
    order = [0]
    for bit in reversed(bits):
        order = order + [place | bit for place in order]
    return order


def transform_kernel(count, norm, owner_ref, face_ref, row_table_ref, col_table_ref, _, *refs):
    parts, (keep_ref, send_ref, cells, table, inverse) = refs[: -5], refs[-5:]
    height, width = parts[0].shape[1:]
    here_y, here_x = lax.axis_index("ty"), lax.axis_index("tx")
    targets = owner_ref.shape[0]
    per_face = targets // NFACE

    def note(i, _):
        inverse[owner_ref[i]] = i
        return 0

    lax.fori_loop(0, targets, note, 0)
    for i, part in enumerate(parts):
        rows = pl.ds(pl.multiple_of((here_y ^ i) * height, TILE), height)
        for c in range(4):
            cells[rows, c * width : (c + 1) * width] = part[c]
    along_rows = jnp.dot(row_table_ref[...], cells[...], precision=HIGHEST, preferred_element_type=F32)
    stacked = jnp.concatenate([along_rows[:, c * width : (c + 1) * width] for c in range(4)], axis=0)
    columns = col_table_ref[pl.ds(pl.multiple_of(here_x * width, TILE), width), :]
    table[...] = norm * jnp.dot(stacked, columns, precision=HIGHEST, preferred_element_type=F32)
    size = table.shape[0] // per_face
    for i, place in enumerate(halving_order(count)):
        for ref, relative in ((keep_ref, place), (send_ref, place ^ 1)):
            tile = inverse[here_y * count + (here_x ^ relative)]
            start = pl.multiple_of(lax.rem(tile, per_face) * size, TILE)
            mine = lax.div(tile, per_face) == face_ref[0, 0]
            ref[i * size : (i + 1) * size, :] = jnp.where(mine, table[pl.ds(start, size), :], 0.0)


def call(kernel, outs, in_specs, scratch=(), out_specs=None, limit=4, aliases=None, work=0):
    return pl.pallas_call(
        kernel,
        out_shape=outs,
        in_specs=in_specs,
        out_specs=out_specs or [VMEM] * len(outs),
        scratch_shapes=list(scratch),
        input_output_aliases=aliases or {},
        cost_estimate=pl.CostEstimate(flops=work, transcendentals=0, bytes_accessed=work) if work else None,
        compiler_params=pltpu.CompilerParams(vmem_limit_bytes=limit << 20),
    )


def swap(block, axis, bit):
    return lax.ppermute(block, axis, [(i, i ^ bit) for i in range(lax.axis_size(axis))])


def exchange(axis, first, second):
    count = lax.axis_size(axis)
    others = [(i, (i + 1 if i % 2 else i - 1) % count) for i in range(count)]
    return lax.ppermute(second, axis, others), swap(first, axis, 1)


def cosines(total, mode_count):
    phase = (2 * np.arange(total)[:, None] + 1) * np.arange(mode_count)[None, :] % (4 * total)
    return np.cos(phase * (math.pi / (2 * total)))


def body(adjoint, background_flow, vert_diff, wet_levels, rotation, face_map, ctrl_owner):
    _, levels, height, width = adjoint.shape
    ty, tx = lax.axis_size("ty"), lax.axis_size("tx")
    rows_total, cols_total = height * ty, width * tx
    full = shape(levels, height, width)
    pair = shape(2, levels, height, width)
    row_pair, col_pair = [shape(levels, TILE, width)] * 2, [shape(2, height, LANES)] * 2
    rows_scratch = [pltpu.VMEM((levels, TILE, width), F32)] * 2
    cols_scratch = [pltpu.VMEM((2, height, LANES), F32)] * 2
    state = [pair, pair, shape(2, height, width)]

    def kept(rows):
        return pltpu.VMEM((4, levels, rows, width), F32)

    places = np.arange(rows_total)
    coriolis = CORIOLIS_PEAK * np.sin(math.pi * (places + 0.5) / rows_total - 0.5 * math.pi)
    coriolis = jnp.asarray(np.repeat(coriolis[:, None], width, axis=1), F32)
    row_table = jnp.asarray(cosines(rows_total, KY).T, F32)
    col_table = jnp.asarray(cosines(cols_total, KX), F32)
    norm = math.sqrt(2.0 * NFACE / (rows_total * cols_total))

    dma = pltpu.SemaphoreType.DMA
    adjoint = pltpu.with_memory_space_constraint(adjoint, pltpu.HBM)
    edge_raw = pltpu.VMEM((2, 4, levels, TILE, width), F32)
    rows = call(prep_rows_kernel, row_pair, [SMEM, ANY], [edge_raw] + rows_scratch + [dma((2,))])(rotation, adjoint)
    row_b, row_a = exchange("ty", *rows)
    ts, uv, *cols = call(
        prep_columns_kernel,
        [pair, pair] + col_pair,
        [SMEM, ANY],
        [pltpu.VMEM((2, levels, height, width), F32), dma((2 * levels // PREP_UNROLL,))],
        limit=6,
        work=1 << 23,
    )(rotation, adjoint)
    col_b, col_a = exchange("tx", *cols)
    w1, w2, h1, h2, g1, g2 = call(factor_kernel, [full] * 6, [VMEM] * 2, work=1 << 22)(vert_diff, wet_levels)
    edge_blocks = ((0, EDGE), (height - EDGE, EDGE))
    middle = height - 2 * EDGE
    ts1, uv1, first, east, west, *rows = call(
        functools.partial(step_kernel, "edge", edge_blocks),
        state + col_pair + row_pair,
        [VMEM] * 14,
        rows_scratch + [kept(EDGE)] + cols_scratch + rows_scratch,
        limit=8,
    )(ts, uv, background_flow, w1, w2, h1, h2, coriolis, col_a, col_b, row_a, row_b, g1, g2)
    row_b, row_a = exchange("ty", *rows)
    ts, uv, first, *cols = call(
        functools.partial(step_kernel, "middle", ((EDGE, middle),)),
        state + col_pair,
        [VMEM] * 17,
        [kept(middle)] + cols_scratch,
        limit=8,
        aliases={12: 0, 13: 1, 14: 2},
        work=1 << 24,
    )(ts, uv, background_flow, w1, w2, h1, h2, coriolis, col_a, col_b, g1, g2, ts1, uv1, first, east, west)
    col_b, col_a = exchange("tx", *cols)
    values, surfaces = call(
        functools.partial(step_kernel, "up", ((0, height),)),
        [shape(4, levels, height, width), shape(4, height, width)],
        [VMEM] * 13,
        cols_scratch + rows_scratch,
        limit=8,
    )(ts, uv, background_flow, w1, w2, h1, h2, coriolis, col_a, col_b, row_a, row_b, first)
    parts = [surfaces] + [swap(surfaces, "ty", bit) for bit in range(1, ty)]
    adjoint_out, token = call(
        last_kernel,
        [shape(*adjoint.shape), shape(TILE, LANES)],
        [SMEM] + [VMEM] * 3,
        [kept(height), dma((levels // DOWN_UNROLL,))],
        out_specs=[ANY, VMEM],
        limit=8,
        work=1 << 23,
    )(rotation, values, g1, g2)
    size = 4 * KY * NFACE // ctrl_owner.shape[0]
    keep, send = call(
        functools.partial(transform_kernel, tx, norm),
        [shape(size * tx // 2, KX)] * 2,
        [SMEM] * 2 + [VMEM] * (ty + 3),
        [pltpu.VMEM((rows_total, 4 * width), F32), pltpu.VMEM((4 * KY, KX), F32), pltpu.SMEM(ctrl_owner.shape, jnp.int32)],
        limit=6,
    )(ctrl_owner, face_map, row_table, col_table, token, *parts)
    bit = 1
    while True:
        keep = keep + swap(send, "tx", bit)
        bit *= 2
        if bit == tx:
            break
        half = keep.shape[0] // 2
        keep, send = keep[:half], keep[half:]
    return adjoint_out, keep.reshape(1, -1)


def solution(mesh):
    return jax.shard_map(
        body,
        mesh=mesh,
        in_specs=(
            P(None, None, "ty", "tx"),
            P(None, None, "ty", "tx"),
            P(None, "ty", "tx"),
            P("ty", "tx"),
            P("ty", "tx"),
            P("ty", "tx"),
            P(),
        ),
        out_specs=(P(None, None, "ty", "tx"), P(("ty", "tx"), None)),
        check_vma=False,
    )
```

```python
import functools
import math

import jax
import jax.numpy as jnp
import numpy as np
from jax import lax
from jax.experimental import pallas as pl
from jax.experimental.pallas import tpu as pltpu
from jax.sharding import PartitionSpec as P

KY = 128
KX = 128
NFACE = 4

ADVECT_COEF = 0.3
DIFFUSE_COEF = 0.12
VISCOUS_COEF = 0.1
THERMAL_COEF = 0.4
HALINE_COEF = 0.3
PRESSURE_COEF = 0.4
SALINE_WEIGHT = 0.8
CORIOLIS_PEAK = 0.5
MOMENTUM_RATIO = 1.5

TILE = 8
LANES = 128
ANY = pl.BlockSpec(memory_space=pl.ANY)
VMEM = pl.BlockSpec(memory_space=pltpu.VMEM)
SMEM = pl.BlockSpec(memory_space=pltpu.SMEM)
F32 = jnp.float32
PREP_UNROLL = 6
FACTOR_ROWS, FACTOR_UNROLL = 64, 2
UNROLLS = {16: (6, 9), 32: (4, 6), 64: (4, 6)}
DOWN_UNROLL = 6
EDGE = 16


def shape(*dims):
    return jax.ShapeDtypeStruct(dims, F32)


def lanes_of(rows):
    return lax.broadcasted_iota(jnp.int32, (rows, LANES), 1)


def rows_of(rows):
    return lax.broadcasted_iota(jnp.int32, (rows, LANES), 0)


def loop(count, load, body, init, unroll):
    while count % unroll:
        unroll -= 1

    def several(i, carry):
        steps = [i * unroll + j for j in range(unroll)]
        loaded = [load(step) for step in steps]
        stores = []
        for step, values in zip(steps, loaded):
            carry, store = body(step, values, carry)
            stores.append(store)
        for store in stores:
            store()
        return carry

    return lax.fori_loop(0, count // unroll, several, init)


def turn_scalars(code):
    cosine = jnp.where(code == 0, 1.0, jnp.where(code == 2, -1.0, 0.0)).astype(F32)
    sine = jnp.where(code == 1, 1.0, jnp.where(code == 3, -1.0, 0.0)).astype(F32)
    return cosine, sine


def pack_columns(acc, k, fields, lane):
    at = 3 * k
    first, second, third = lane >= at, lane >= at + 1, lane >= at + 2
    east, west = [], []
    for g in range(2):
        tracer, flow = fields[g], fields[g + 2]
        rolled = pltpu.roll(tracer, at + 2, 1)
        east.append(jnp.where(first, jnp.where(third, pltpu.roll(flow, at + 3, 1), rolled), acc[g]))
        west.append(jnp.where(second, jnp.where(third, rolled, pltpu.roll(flow, at + 1, 1)), acc[g + 2]))
    return tuple(east + west)


def store_edge_rows(k, fields, ends, south_ref, north_ref):
    size = fields[0].shape[0]
    for c in range(4):
        if ends[0]:
            south_ref[k, 2 * c : 2 * c + 2, :] = fields[c][0:2, :]
        if ends[1]:
            north_ref[k, 2 * c : 2 * c + 2, :] = fields[c][size - 2 : size, :]


def write_rows(row_a, row_b, south_ref, north_ref):
    even = lax.axis_index("ty") % 2 == 0
    south, north = south_ref[...], north_ref[...]
    row_a[...] = jnp.where(even, north, south)
    row_b[...] = jnp.where(even, south, north)


def write_columns(col_a, col_b, east, west):
    even = lax.axis_index("tx") % 2 == 0
    col_a[...] = jnp.where(even, east, west)
    col_b[...] = jnp.where(even, west, east)


def read_rows(row_a, row_b, south_ref, north_ref):
    here = lax.axis_index("ty")
    even = here % 2 == 0
    first, second = row_a[...], row_b[...]
    south_ref[...] = jnp.where(here == 0, 0.0, jnp.where(even, second, first))
    north_ref[...] = jnp.where(here == lax.axis_size("ty") - 1, 0.0, jnp.where(even, first, second))


def read_columns(col_a, col_b, east_ref, west_ref):
    even = lax.axis_index("tx") % 2 == 0
    first, second = col_a[...], col_b[...]
    east_ref[...] = jnp.where(even, first, second)
    west_ref[...] = jnp.where(even, second, first)


def prep_kernel(rot_ref, adj_ref, ts_ref, uv_ref, col_a, col_b, row_a, row_b, raw_ref, south_ref, north_ref, sems):
    levels, height = adj_ref.shape[1], adj_ref.shape[2]
    cosine, sine = turn_scalars(rot_ref[0, 0])
    step = PREP_UNROLL
    chunks = levels // step
    copies = []
    for i in range(chunks):
        part = pl.ds(i * step, step)
        for h, target in enumerate((ts_ref, raw_ref)):
            copy = pltpu.make_async_copy(adj_ref.at[pl.ds(2 * h, 2), part], target.at[:, part], sems.at[2 * i + h])
            copy.start()
            copies.append(copy)
    lane = lanes_of(height)
    zero = jnp.zeros((height, LANES), F32)
    acc = (zero,) * 4
    for i in range(chunks):
        copies[2 * i].wait()
        copies[2 * i + 1].wait()
        group = range(i * step, (i + 1) * step)
        loaded = [(ts_ref[0, k], ts_ref[1, k], raw_ref[0, k], raw_ref[1, k]) for k in group]
        stores = []
        for k, (t, s, a, b) in zip(group, loaded):
            fields = (t, s, cosine * a - sine * b, sine * a + cosine * b)
            acc = pack_columns(acc, k, fields, lane)
            stores.append((k, fields))
        for k, fields in stores:
            uv_ref[0, k] = fields[2]
            uv_ref[1, k] = fields[3]
            store_edge_rows(k, fields, (True, True), south_ref, north_ref)
    write_rows(row_a, row_b, south_ref, north_ref)
    write_columns(col_a, col_b, jnp.stack(acc[:2]), jnp.stack(acc[2:]))


def factor_kernel(vd_ref, wet_ref, w1_ref, w2_ref, h1_ref, h2_ref, g1_ref, g2_ref):
    levels, height = vd_ref.shape[0], vd_ref.shape[1]
    out = ((w1_ref, h1_ref, g1_ref, 1.0), (w2_ref, h2_ref, g2_ref, MOMENTUM_RATIO))
    size = FACTOR_ROWS
    for block in range(height // size):
        rows = pl.ds(block * size, size)
        wet = wet_ref[rows, :]
        zero = jnp.zeros((size, LANES), F32)

        def load(i, rows=rows):
            return vd_ref[jnp.maximum(levels - 2 - i, 0), rows, :]

        def level(i, loaded, carry, rows=rows, wet=wet):
            k = levels - 1 - i
            below, inverses = carry
            mask = jnp.where(k < wet, 1.0, 0.0).astype(F32)
            above = jnp.where(k > 0, loaded * mask, 0.0)
            kept, stores = [], []
            for (w_ref, h_ref, g_ref, factor), inverse in zip(out, inverses):
                low, high = factor * below, factor * above
                pivot = 1.0 + high + low - low * (low * inverse)
                inverse = 1.0 / pivot
                masked = inverse * mask
                stores += [(w_ref, masked), (h_ref, low * masked), (g_ref, high * masked)]
                kept.append(inverse)

            def store():
                for ref, value in stores:
                    ref[k, rows, :] = value

            return (above, tuple(kept)), store

        loop(levels, load, level, (zero, (zero, zero)), FACTOR_UNROLL)


def step_kernel(stage, blocks, *refs):
    refs = list(refs)

    def take(count):
        taken, refs[:] = refs[:count], refs[count:]
        return taken

    ts_ref, uv_ref, flow_ref, w1_ref, w2_ref, h1_ref, h2_ref, cor_ref, col_b, col_a = take(10)
    south_ref = north_ref = None
    if stage != "inner":
        row_b, row_a = take(2)
    if stage == "outer":
        first_ref, inner_ref = take(2)
    if stage == "whole":
        g1_ref, g2_ref = take(2)
        ts_out, uv_out, surface_ref, *sent = take(7)
        south_out, north_out, value_ref = take(3)
    else:
        value_ref, surface_ref = take(2)
    east_ref, west_ref = take(2)
    read_columns(col_a, col_b, east_ref, west_ref)
    if stage != "inner":
        south_ref, north_ref = take(2)
        read_rows(row_a, row_b, south_ref, north_ref)
    levels, height = ts_ref.shape[1], ts_ref.shape[2]
    first_cor = pl.multiple_of(lax.axis_index("ty") * height, TILE)
    def get(c, k, start):
        rows = pl.ds(start, TILE)
        return ts_ref[c, k, rows, :] if c < 2 else uv_ref[c - 2, k, rows, :]

    def line(c, k, start, halos):
        if 0 <= start <= height - TILE:
            return get(c, k, start)
        south, north = halos
        part = rows_of(TILE)
        if start < 0:
            halo = pltpu.roll(south, (-2 * c - 2 - start) % TILE, 0)
            return jnp.where(part < -start, halo, pltpu.roll(get(c, k, 0), -start, 0))
        over = start + TILE - height
        halo = pltpu.roll(north, (TILE - over - 2 * c) % TILE, 0)
        return jnp.where(part >= TILE - over, halo, pltpu.roll(get(c, k, height - TILE), TILE - over, 0))

    for block, (first_row, size) in enumerate(blocks):
        lane = lanes_of(size)
        low_two, high_two = lane < 2, lane >= LANES - 2
        low_one, high_one = lane < 1, lane >= LANES - 1
        zero = jnp.zeros((size, LANES), F32)
        rows = pl.ds(first_row, size)
        kept_rows = pl.ds(block * size, size)
        south_end, north_end = first_row == 0, first_row + size == height
        cor = cor_ref[pl.ds(first_cor + first_row, size), :]
        up_unroll, down_unroll = UNROLLS[size]

        def fetch(c, k, shift, halos, first_row=first_row, size=size):
            start = first_row + shift
            if 0 <= start <= height - size:
                part = pl.ds(start, size)
                return ts_ref[c, k, part, :] if c < 2 else uv_ref[c - 2, k, part, :]
            lines = [line(c, k, start + i, halos) for i in range(0, size, TILE)]
            return lines[0] if len(lines) == 1 else jnp.concatenate(lines, axis=0)

        def load_up(i, rows=rows, ends=(south_end, north_end), fetch=fetch):
            k = levels - 1 - i
            halos = (south_ref[k] if ends[0] else None, north_ref[k] if ends[1] else None)
            turn = LANES - 2 - 3 * k
            east = [pltpu.roll(east_ref[g, rows, :], turn, 1) for g in range(2)]
            west = [pltpu.roll(west_ref[g, rows, :], turn, 1) for g in range(2)]
            lines = [{s: fetch(c, k, s, halos) for s in ((0, 1, -1, 2, -2) if c < 2 else (0, 1, -1))} for c in range(4)]
            flow = [flow_ref[i, k, rows, :] for i in range(2)]
            factors = [ref[k, rows, :] for ref in (w1_ref, w2_ref, h1_ref, h2_ref)]
            return east, west, lines, flow, factors

        def upward(i, loaded, below, cor=cor, rows=kept_rows):
            k = levels - 1 - i
            east, west, lines, flow, factors = loaded
            flow_x = flow[0] * (ADVECT_COEF / 12.0)
            flow_y = flow[1] * (ADVECT_COEF / 12.0)
            rhs, diff_x, diff_y = [], [], []
            for c in range(2):
                mid = lines[c][0]
                e1 = pltpu.roll(jnp.where(low_one, east[c], mid), LANES - 1, 1)
                w1 = pltpu.roll(jnp.where(high_one, west[c], mid), 1, 1)
                e2 = pltpu.roll(jnp.where(low_two, east[c], mid), LANES - 2, 1)
                w2 = pltpu.roll(jnp.where(high_two, west[c], mid), 2, 1)
                n1, s1, n2, s2 = (lines[c][s] for s in (1, -1, 2, -2))
                dx, dy = e1 - w1, n1 - s1
                grad = flow_x * (8.0 * dx - (e2 - w2)) + flow_y * (8.0 * dy - (n2 - s2))
                near = (e1 + w1) + (n1 + s1)
                rhs.append((1.0 - 4.0 * DIFFUSE_COEF) * mid + DIFFUSE_COEF * near + grad)
                diff_x.append(dx)
                diff_y.append(dy)
            push = [
                (0.5 * PRESSURE_COEF) * (d[0] - SALINE_WEIGHT * d[1]) for d in (diff_x, diff_y)
            ]
            sides = []
            for c in range(2, 4):
                mid = lines[c][0]
                e1 = jnp.where(high_one, east[c - 2], pltpu.roll(mid, LANES - 1, 1))
                w1 = jnp.where(low_one, west[c - 2], pltpu.roll(mid, 1, 1))
                n1, s1 = lines[c][1], lines[c][-1]
                near = (e1 + w1) + (n1 + s1)
                sides.append(e1 - w1 if c == 2 else n1 - s1)
                rhs.append((1.0 - 4.0 * VISCOUS_COEF) * mid + VISCOUS_COEF * near - push[c - 2])
            spread = sides[0] + sides[1]
            rhs[0] = rhs[0] + (0.5 * THERMAL_COEF) * spread
            rhs[1] = rhs[1] - (0.5 * HALINE_COEF) * spread
            rhs[2] = rhs[2] + cor * lines[3][0]
            rhs[3] = rhs[3] - cor * lines[2][0]
            values = tuple(
                factors[c // 2] * rhs[c] + factors[2 + c // 2] * below[c] for c in range(4)
            )

            def store():
                for c in range(4):
                    value_ref[c, k, rows, :] = values[c]

            return values, store

        top = loop(levels, load_up, upward, (zero,) * 4, up_unroll)
        for c in range(2):
            if stage == "outer":
                surface_ref[2 + c, rows, :] = top[c]
            else:
                surface_ref[c, kept_rows, :] = top[c]
        if stage != "whole":
            continue

        def load_down(k, rows=rows, kept_rows=kept_rows):
            values = [value_ref[c, k, kept_rows, :] for c in range(4)]
            return values, (g1_ref[k, rows, :], g2_ref[k, rows, :])

        def downward(k, loaded, carry, rows=rows, ends=(south_end, north_end), lane=lane):
            above, acc = carry
            values, gains = loaded
            fields = tuple(values[c] + gains[c // 2] * above[c] for c in range(4))

            def store():
                for c in range(2):
                    ts_out[c, k, rows, :] = fields[c]
                    uv_out[c, k, rows, :] = fields[c + 2]
                store_edge_rows(k, fields, ends, south_out, north_out)

            return (fields, pack_columns(acc, k, fields, lane)), store

        _, acc = loop(levels, load_down, downward, ((zero,) * 4, (zero,) * 4), down_unroll)
        write_rows(sent[2], sent[3], south_out, north_out)
        write_columns(sent[0], sent[1], jnp.stack(acc[:2]), jnp.stack(acc[2:]))
    if stage == "outer":
        surface_ref[0:2] = first_ref[...]
        for c in range(2):
            surface_ref[2 + c, blocks[0][1] : blocks[1][0], :] = inner_ref[c]


def last_kernel(rot_ref, inner_ref, outer_ref, g1_ref, g2_ref, out_ref, token_ref, field_ref, sems):
    token_ref[...] = jnp.zeros_like(token_ref)
    levels = inner_ref.shape[1]
    cosine, sine = turn_scalars(rot_ref[0, 0])
    step = DOWN_UNROLL

    def column(c, k):
        return jnp.concatenate([outer_ref[c, k, 0:EDGE, :], inner_ref[c, k], outer_ref[c, k, EDGE:, :]], axis=0)

    above, copies = None, []
    for i in range(levels // step):
        group = range(i * step, (i + 1) * step)
        loaded = [([column(c, k) for c in range(4)], (g1_ref[k], g2_ref[k])) for k in group]
        done = []
        for values, gains in loaded:
            if above is not None:
                values = [values[c] + gains[c // 2] * above[c] for c in range(4)]
            above = values
            u, v = values[2:]
            done.append((values[0], values[1], cosine * u + sine * v, cosine * v - sine * u))
        for k, fields in zip(group, done):
            for c in range(4):
                field_ref[c, k] = fields[c]
        part = pl.ds(i * step, step)
        copy = pltpu.make_async_copy(field_ref.at[:, part], out_ref.at[:, part], sems.at[i])
        copy.start()
        copies.append(copy)
    for copy in copies:
        copy.wait()


HIGHEST = lax.Precision.HIGHEST


def halving_order(count):
    bits = [1 << i for i in range(1, count.bit_length() - 1)]
    order = [0]
    for bit in reversed(bits):
        order = order + [place | bit for place in order]
    return order


def transform_kernel(count, norm, owner_ref, face_ref, row_table_ref, col_table_ref, _, *refs):
    parts, (keep_ref, send_ref, cells, table, inverse) = refs[: -5], refs[-5:]
    height, width = parts[0].shape[1:]
    here_y, here_x = lax.axis_index("ty"), lax.axis_index("tx")
    targets = owner_ref.shape[0]
    per_face = targets // NFACE

    def note(i, _):
        inverse[owner_ref[i]] = i
        return 0

    lax.fori_loop(0, targets, note, 0)
    for i, part in enumerate(parts):
        rows = pl.ds(pl.multiple_of((here_y ^ i) * height, TILE), height)
        for c in range(4):
            cells[rows, c * width : (c + 1) * width] = part[c]
    along_rows = jnp.dot(row_table_ref[...], cells[...], precision=HIGHEST, preferred_element_type=F32)
    stacked = jnp.concatenate([along_rows[:, c * width : (c + 1) * width] for c in range(4)], axis=0)
    columns = col_table_ref[pl.ds(pl.multiple_of(here_x * width, TILE), width), :]
    table[...] = norm * jnp.dot(stacked, columns, precision=HIGHEST, preferred_element_type=F32)
    size = table.shape[0] // per_face
    for i, place in enumerate(halving_order(count)):
        for ref, relative in ((keep_ref, place), (send_ref, place ^ 1)):
            tile = inverse[here_y * count + (here_x ^ relative)]
            start = pl.multiple_of(lax.rem(tile, per_face) * size, TILE)
            mine = lax.div(tile, per_face) == face_ref[0, 0]
            ref[i * size : (i + 1) * size, :] = jnp.where(mine, table[pl.ds(start, size), :], 0.0)


def call(kernel, outs, in_specs, scratch=(), out_specs=None, limit=4, aliases=None, work=0):
    return pl.pallas_call(
        kernel,
        out_shape=outs,
        in_specs=in_specs,
        out_specs=out_specs or [VMEM] * len(outs),
        scratch_shapes=list(scratch),
        input_output_aliases=aliases or {},
        cost_estimate=pl.CostEstimate(flops=work, transcendentals=0, bytes_accessed=work) if work else None,
        compiler_params=pltpu.CompilerParams(vmem_limit_bytes=limit << 20),
    )


def swap(block, axis, bit):
    return lax.ppermute(block, axis, [(i, i ^ bit) for i in range(lax.axis_size(axis))])


def exchange(axis, first, second):
    count = lax.axis_size(axis)
    others = [(i, (i + 1 if i % 2 else i - 1) % count) for i in range(count)]
    return lax.ppermute(second, axis, others), swap(first, axis, 1)


def cosines(total, mode_count):
    phase = (2 * np.arange(total)[:, None] + 1) * np.arange(mode_count)[None, :] % (4 * total)
    return np.cos(phase * (math.pi / (2 * total)))


def body(adjoint, background_flow, vert_diff, wet_levels, rotation, face_map, ctrl_owner):
    _, levels, height, width = adjoint.shape
    ty, tx = lax.axis_size("ty"), lax.axis_size("tx")
    rows_total, cols_total = height * ty, width * tx
    full = shape(levels, height, width)
    pair = shape(2, levels, height, width)
    row_pair, col_pair = [shape(levels, TILE, width)] * 2, [shape(2, height, LANES)] * 2
    rows_scratch = [pltpu.VMEM((levels, TILE, width), F32)] * 2
    cols_scratch = [pltpu.VMEM((2, height, LANES), F32)] * 2
    surface = shape(2, height, width)

    def kept(rows):
        return pltpu.VMEM((4, levels, rows, width), F32)

    places = np.arange(rows_total)
    coriolis = CORIOLIS_PEAK * np.sin(math.pi * (places + 0.5) / rows_total - 0.5 * math.pi)
    coriolis = jnp.asarray(np.repeat(coriolis[:, None], width, axis=1), F32)
    row_table = jnp.asarray(cosines(rows_total, KY).T, F32)
    col_table = jnp.asarray(cosines(cols_total, KX), F32)
    norm = math.sqrt(2.0 * NFACE / (rows_total * cols_total))

    dma = pltpu.SemaphoreType.DMA
    adjoint = pltpu.with_memory_space_constraint(adjoint, pltpu.HBM)
    ts, uv, *sent = call(
        prep_kernel,
        [pair, pair] + col_pair + row_pair,
        [SMEM, ANY],
        [pltpu.VMEM((2, levels, height, width), F32)] + rows_scratch + [dma((2 * levels // PREP_UNROLL,))],
        limit=6,
        work=1 << 23,
    )(rotation, adjoint)
    cols, rows = exchange("tx", *sent[:2]), exchange("ty", *sent[2:])
    w1, w2, h1, h2, g1, g2 = call(factor_kernel, [full] * 6, [VMEM] * 2, work=1 << 22)(vert_diff, wet_levels)
    coefficients = (background_flow, w1, w2, h1, h2, coriolis)
    ts, uv, first, *sent = call(
        functools.partial(step_kernel, "whole", ((0, height),)),
        [pair, pair, surface] + col_pair + row_pair,
        [VMEM] * 14,
        rows_scratch + [kept(height)] + cols_scratch + rows_scratch,
        limit=12,
    )(ts, uv, *coefficients, *cols, *rows, g1, g2)
    cols, rows = exchange("tx", *sent[:2]), exchange("ty", *sent[2:])
    middle = height - 2 * EDGE
    inner, inner_surface = call(
        functools.partial(step_kernel, "inner", ((EDGE, middle),)),
        [shape(4, levels, middle, width), shape(2, middle, width)],
        [VMEM] * 10,
        cols_scratch,
        work=1 << 24,
    )(ts, uv, *coefficients, *cols)
    outer, surfaces = call(
        functools.partial(step_kernel, "outer", ((0, EDGE), (height - EDGE, EDGE))),
        [shape(4, levels, 2 * EDGE, width), shape(4, height, width)],
        [VMEM] * 14,
        cols_scratch + rows_scratch,
    )(ts, uv, *coefficients, *cols, *rows, first, inner_surface)
    parts = [surfaces] + [swap(surfaces, "ty", bit) for bit in range(1, ty)]
    adjoint_out, token = call(
        last_kernel,
        [shape(*adjoint.shape), shape(TILE, LANES)],
        [SMEM] + [VMEM] * 4,
        [kept(height), dma((levels // DOWN_UNROLL,))],
        out_specs=[ANY, VMEM],
        limit=8,
        work=1 << 23,
    )(rotation, inner, outer, g1, g2)
    size = 4 * KY * NFACE // ctrl_owner.shape[0]
    keep, send = call(
        functools.partial(transform_kernel, tx, norm),
        [shape(size * tx // 2, KX)] * 2,
        [SMEM] * 2 + [VMEM] * (ty + 3),
        [pltpu.VMEM((rows_total, 4 * width), F32), pltpu.VMEM((4 * KY, KX), F32), pltpu.SMEM(ctrl_owner.shape, jnp.int32)],
        limit=6,
    )(ctrl_owner, face_map, row_table, col_table, token, *parts)
    bit = 1
    while True:
        keep = keep + swap(send, "tx", bit)
        bit *= 2
        if bit == tx:
            break
        half = keep.shape[0] // 2
        keep, send = keep[:half], keep[half:]
    return adjoint_out, keep.reshape(1, -1)


def solution(mesh):
    return jax.shard_map(
        body,
        mesh=mesh,
        in_specs=(
            P(None, None, "ty", "tx"),
            P(None, None, "ty", "tx"),
            P(None, "ty", "tx"),
            P("ty", "tx"),
            P("ty", "tx"),
            P("ty", "tx"),
            P(),
        ),
        out_specs=(P(None, None, "ty", "tx"), P(("ty", "tx"), None)),
        check_vma=False,
    )
```

```python
import functools
import math

import jax
import jax.numpy as jnp
import numpy as np
from jax import lax
from jax.experimental import pallas as pl
from jax.experimental.pallas import tpu as pltpu
from jax.sharding import PartitionSpec as P

KY = 128
KX = 128
NFACE = 4

ADVECT_COEF = 0.3
DIFFUSE_COEF = 0.12
VISCOUS_COEF = 0.1
THERMAL_COEF = 0.4
HALINE_COEF = 0.3
PRESSURE_COEF = 0.4
SALINE_WEIGHT = 0.8
CORIOLIS_PEAK = 0.5
MOMENTUM_RATIO = 1.5

TILE = 8
LANES = 128
ANY = pl.BlockSpec(memory_space=pl.ANY)
VMEM = pl.BlockSpec(memory_space=pltpu.VMEM)
SMEM = pl.BlockSpec(memory_space=pltpu.SMEM)
F32 = jnp.float32
PREP_UNROLL = 6
FACTOR_ROWS, FACTOR_UNROLL = 64, 2
UNROLLS = {16: (12, 9), 32: (6, 6), 64: (6, 9)}
DOWN_UNROLL = 6
EDGE = 16


def shape(*dims):
    return jax.ShapeDtypeStruct(dims, F32)


def lanes_of(rows):
    return lax.broadcasted_iota(jnp.int32, (rows, LANES), 1)


def rows_of(rows):
    return lax.broadcasted_iota(jnp.int32, (rows, LANES), 0)


def loop(count, load, body, init, unroll, prepare=lambda loaded: loaded):
    while count % unroll:
        unroll -= 1

    def several(i, carry):
        steps = [i * unroll + j for j in range(unroll)]
        loaded = prepare([load(step) for step in steps])
        stores = []
        for step, values in zip(steps, loaded):
            carry, store = body(step, values, carry)
            stores.append(store)
        for store in stores:
            store()
        return carry

    return lax.fori_loop(0, count // unroll, several, init)


def turn_scalars(code):
    cosine = jnp.where(code == 0, 1.0, jnp.where(code == 2, -1.0, 0.0)).astype(F32)
    sine = jnp.where(code == 1, 1.0, jnp.where(code == 3, -1.0, 0.0)).astype(F32)
    return cosine, sine


def pack_columns(acc, k, fields, lane):
    at = 3 * k
    first, second, third = lane >= at, lane >= at + 1, lane >= at + 2
    east, west = [], []
    for g in range(2):
        tracer, flow = fields[g], fields[g + 2]
        rolled = pltpu.roll(tracer, at + 2, 1)
        east.append(jnp.where(first, jnp.where(third, pltpu.roll(flow, at + 3, 1), rolled), acc[g]))
        west.append(jnp.where(second, jnp.where(third, rolled, pltpu.roll(flow, at + 1, 1)), acc[g + 2]))
    return tuple(east + west)


def store_edge_rows(k, fields, ends, south_ref, north_ref):
    size = fields[0].shape[0]
    for c in range(4):
        if ends[0]:
            south_ref[k, 2 * c : 2 * c + 2, :] = fields[c][0:2, :]
        if ends[1]:
            north_ref[k, 2 * c : 2 * c + 2, :] = fields[c][size - 2 : size, :]


def write_rows(row_a, row_b, south_ref, north_ref):
    even = lax.axis_index("ty") % 2 == 0
    south, north = south_ref[...], north_ref[...]
    row_a[...] = jnp.where(even, north, south)
    row_b[...] = jnp.where(even, south, north)


def write_columns(col_a, col_b, east, west):
    even = lax.axis_index("tx") % 2 == 0
    col_a[...] = jnp.where(even, east, west)
    col_b[...] = jnp.where(even, west, east)


def read_rows(row_a, row_b, south_ref, north_ref):
    here = lax.axis_index("ty")
    even = here % 2 == 0
    first, second = row_a[...], row_b[...]
    south_ref[...] = jnp.where(here == 0, 0.0, jnp.where(even, second, first))
    north_ref[...] = jnp.where(here == lax.axis_size("ty") - 1, 0.0, jnp.where(even, first, second))


def read_columns(col_a, col_b, east_ref, west_ref):
    even = lax.axis_index("tx") % 2 == 0
    first, second = col_a[...], col_b[...]
    east_ref[...] = jnp.where(even, first, second)
    west_ref[...] = jnp.where(even, second, first)


def prep_kernel(rot_ref, adj_ref, ts_ref, uv_ref, col_a, col_b, row_a, row_b, raw_ref, south_ref, north_ref, sems):
    levels, height = adj_ref.shape[1], adj_ref.shape[2]
    cosine, sine = turn_scalars(rot_ref[0, 0])
    step = PREP_UNROLL
    chunks = levels // step
    copies = []
    for i in range(chunks):
        part = pl.ds(i * step, step)
        for h, target in enumerate((ts_ref, raw_ref)):
            copy = pltpu.make_async_copy(adj_ref.at[pl.ds(2 * h, 2), part], target.at[:, part], sems.at[2 * i + h])
            copy.start()
            copies.append(copy)
    lane = lanes_of(height)
    zero = jnp.zeros((height, LANES), F32)
    acc = (zero,) * 4
    for i in range(chunks):
        copies[2 * i].wait()
        copies[2 * i + 1].wait()
        group = range(i * step, (i + 1) * step)
        loaded = [(ts_ref[0, k], ts_ref[1, k], raw_ref[0, k], raw_ref[1, k]) for k in group]
        stores = []
        for k, (t, s, a, b) in zip(group, loaded):
            fields = (t, s, cosine * a - sine * b, sine * a + cosine * b)
            acc = pack_columns(acc, k, fields, lane)
            stores.append((k, fields))
        for k, fields in stores:
            uv_ref[0, k] = fields[2]
            uv_ref[1, k] = fields[3]
            store_edge_rows(k, fields, (True, True), south_ref, north_ref)
    write_rows(row_a, row_b, south_ref, north_ref)
    write_columns(col_a, col_b, jnp.stack(acc[:2]), jnp.stack(acc[2:]))


def factor_kernel(vd_ref, wet_ref, w1_ref, w2_ref, h1_ref, h2_ref, g1_ref, g2_ref):
    levels, height = vd_ref.shape[0], vd_ref.shape[1]
    out = ((w1_ref, h1_ref, g1_ref, 1.0), (w2_ref, h2_ref, g2_ref, MOMENTUM_RATIO))
    size = FACTOR_ROWS
    for block in range(height // size):
        rows = pl.ds(block * size, size)
        wet = wet_ref[rows, :]
        zero = jnp.zeros((size, LANES), F32)

        def load(i, rows=rows):
            return vd_ref[jnp.maximum(levels - 2 - i, 0), rows, :]

        def level(i, loaded, carry, rows=rows, wet=wet):
            k = levels - 1 - i
            below, inverses = carry
            mask = jnp.where(k < wet, 1.0, 0.0).astype(F32)
            above = jnp.where(k > 0, loaded * mask, 0.0)
            kept, stores = [], []
            for (w_ref, h_ref, g_ref, factor), inverse in zip(out, inverses):
                low, high = factor * below, factor * above
                pivot = 1.0 + high + low - low * (low * inverse)
                inverse = 1.0 / pivot
                masked = inverse * mask
                stores += [(w_ref, masked), (h_ref, low * masked), (g_ref, high * masked)]
                kept.append(inverse)

            def store():
                for ref, value in stores:
                    ref[k, rows, :] = value

            return (above, tuple(kept)), store

        loop(levels, load, level, (zero, (zero, zero)), FACTOR_UNROLL)


def step_kernel(stage, blocks, *refs):
    refs = list(refs)

    def take(count):
        taken, refs[:] = refs[:count], refs[count:]
        return taken

    ts_ref, uv_ref, flow_ref, w1_ref, w2_ref, h1_ref, h2_ref, cor_ref, band_ref, col_b, col_a = take(11)
    south_ref = north_ref = None
    if stage != "inner":
        row_b, row_a = take(2)
    if stage == "outer":
        first_ref, inner_ref = take(2)
    if stage == "whole":
        g1_ref, g2_ref = take(2)
        ts_out, uv_out, surface_ref, *sent = take(7)
        south_out, north_out, value_ref = take(3)
    else:
        value_ref, surface_ref = take(2)
    east_ref, west_ref = take(2)
    read_columns(col_a, col_b, east_ref, west_ref)
    if stage != "inner":
        south_ref, north_ref = take(2)
        read_rows(row_a, row_b, south_ref, north_ref)
    levels, height = ts_ref.shape[1], ts_ref.shape[2]
    first_cor = pl.multiple_of(lax.axis_index("ty") * height, TILE)
    def get(c, k, start):
        rows = pl.ds(start, TILE)
        return ts_ref[c, k, rows, :] if c < 2 else uv_ref[c - 2, k, rows, :]

    def line(c, k, start, halos):
        if 0 <= start <= height - TILE:
            return get(c, k, start)
        south, north = halos
        part = rows_of(TILE)
        if start < 0:
            halo = pltpu.roll(south, (-2 * c - 2 - start) % TILE, 0)
            return jnp.where(part < -start, halo, pltpu.roll(get(c, k, 0), -start, 0))
        over = start + TILE - height
        halo = pltpu.roll(north, (TILE - over - 2 * c) % TILE, 0)
        return jnp.where(part >= TILE - over, halo, pltpu.roll(get(c, k, height - TILE), TILE - over, 0))

    for block, (first_row, size) in enumerate(blocks):
        lane = lanes_of(size)
        low_one, high_one = lane < 1, lane >= LANES - 1
        zero = jnp.zeros((size, LANES), F32)
        rows = pl.ds(first_row, size)
        kept_rows = pl.ds(block * size, size)
        south_end, north_end = first_row == 0, first_row + size == height
        cor = cor_ref[pl.ds(first_cor + first_row, size), :]
        up_unroll, down_unroll = UNROLLS[size]

        def fetch(c, k, shift, halos, first_row=first_row, size=size):
            start = first_row + shift
            if 0 <= start <= height - size:
                part = pl.ds(start, size)
                return ts_ref[c, k, part, :] if c < 2 else uv_ref[c - 2, k, part, :]
            lines = [line(c, k, start + i, halos) for i in range(0, size, TILE)]
            return lines[0] if len(lines) == 1 else jnp.concatenate(lines, axis=0)

        def load_up(i, rows=rows, ends=(south_end, north_end), fetch=fetch):
            k = levels - 1 - i
            halos = (south_ref[k] if ends[0] else None, north_ref[k] if ends[1] else None)
            turn = LANES - 2 - 3 * k
            east = [pltpu.roll(east_ref[g, rows, :], turn, 1) for g in range(2)]
            west = [pltpu.roll(west_ref[g, rows, :], turn, 1) for g in range(2)]
            lines = [{s: fetch(c, k, s, halos) for s in ((0, 1, -1, 2, -2) if c < 2 else (0, 1, -1))} for c in range(4)]
            flow = [flow_ref[i, k, rows, :] for i in range(2)]
            factors = [ref[k, rows, :] for ref in (w1_ref, w2_ref, h1_ref, h2_ref)]
            return east, west, lines, flow, factors

        def along_x(loaded, lane=lane, size=size):
            fields = [
                jnp.concatenate([item[2][c][0], jnp.where(lane < LANES // 2, item[0][c], item[1][c])], axis=1)
                for item in loaded
                for c in range(2)
            ]
            fields = jnp.concatenate(fields, axis=0)
            high = fields.astype(jnp.bfloat16)
            low = (fields - high.astype(F32)).astype(jnp.bfloat16)
            mixed = sum(jnp.dot(part, band_ref[...], preferred_element_type=F32) for part in (high, low))
            parts = [mixed[i * size : (i + 1) * size] for i in range(2 * len(loaded))]
            return [
                (*item, [(part[:, :LANES], part[:, LANES:]) for part in parts[2 * i : 2 * i + 2]])
                for i, item in enumerate(loaded)
            ]

        def upward(i, loaded, below, cor=cor, rows=kept_rows):
            k = levels - 1 - i
            east, west, lines, flow, factors, mixed = loaded
            flow_x = flow[0] * (ADVECT_COEF / 12.0)
            flow_y = flow[1] * (ADVECT_COEF / 12.0)
            rhs, diff_y = [], []
            for c in range(2):
                mid = lines[c][0]
                n1, s1, n2, s2 = (lines[c][s] for s in (1, -1, 2, -2))
                grad_x, near_x = mixed[c]
                dy = n1 - s1
                grad = flow_x * grad_x + flow_y * (8.0 * dy - (n2 - s2))
                near = near_x + (n1 + s1)
                rhs.append((1.0 - 4.0 * DIFFUSE_COEF) * mid + DIFFUSE_COEF * near + grad)
                diff_y.append(dy)
            buoyant, at_east, at_west = (
                pair[0] - SALINE_WEIGHT * pair[1] for pair in ((lines[0][0], lines[1][0]), east, west)
            )
            diff_x = pltpu.roll(jnp.where(low_one, at_east, buoyant), LANES - 1, 1) - pltpu.roll(
                jnp.where(high_one, at_west, buoyant), 1, 1
            )
            push = [(0.5 * PRESSURE_COEF) * d for d in (diff_x, diff_y[0] - SALINE_WEIGHT * diff_y[1])]
            sides = []
            for c in range(2, 4):
                mid = lines[c][0]
                e1 = jnp.where(high_one, east[c - 2], pltpu.roll(mid, LANES - 1, 1))
                w1 = jnp.where(low_one, west[c - 2], pltpu.roll(mid, 1, 1))
                n1, s1 = lines[c][1], lines[c][-1]
                near = (e1 + w1) + (n1 + s1)
                sides.append(e1 - w1 if c == 2 else n1 - s1)
                rhs.append((1.0 - 4.0 * VISCOUS_COEF) * mid + VISCOUS_COEF * near - push[c - 2])
            spread = sides[0] + sides[1]
            rhs[0] = rhs[0] + (0.5 * THERMAL_COEF) * spread
            rhs[1] = rhs[1] - (0.5 * HALINE_COEF) * spread
            rhs[2] = rhs[2] + cor * lines[3][0]
            rhs[3] = rhs[3] - cor * lines[2][0]
            values = tuple(
                factors[c // 2] * rhs[c] + factors[2 + c // 2] * below[c] for c in range(4)
            )

            def store():
                for c in range(4):
                    value_ref[c, k, rows, :] = values[c]

            return values, store

        top = loop(levels, load_up, upward, (zero,) * 4, up_unroll, along_x)
        for c in range(2):
            if stage == "outer":
                surface_ref[2 + c, rows, :] = top[c]
            else:
                surface_ref[c, kept_rows, :] = top[c]
        if stage != "whole":
            continue

        def load_down(k, rows=rows, kept_rows=kept_rows):
            values = [value_ref[c, k, kept_rows, :] for c in range(4)]
            return values, (g1_ref[k, rows, :], g2_ref[k, rows, :])

        def downward(k, loaded, carry, rows=rows, ends=(south_end, north_end), lane=lane):
            above, acc = carry
            values, gains = loaded
            fields = tuple(values[c] + gains[c // 2] * above[c] for c in range(4))

            def store():
                for c in range(2):
                    ts_out[c, k, rows, :] = fields[c]
                    uv_out[c, k, rows, :] = fields[c + 2]
                store_edge_rows(k, fields, ends, south_out, north_out)

            return (fields, pack_columns(acc, k, fields, lane)), store

        _, acc = loop(levels, load_down, downward, ((zero,) * 4, (zero,) * 4), down_unroll)
        write_rows(sent[2], sent[3], south_out, north_out)
        write_columns(sent[0], sent[1], jnp.stack(acc[:2]), jnp.stack(acc[2:]))
    if stage == "outer":
        surface_ref[0:2] = first_ref[...]
        for c in range(2):
            surface_ref[2 + c, blocks[0][1] : blocks[1][0], :] = inner_ref[c]


def last_kernel(rot_ref, inner_ref, outer_ref, g1_ref, g2_ref, out_ref, token_ref, field_ref, sems):
    token_ref[...] = jnp.zeros_like(token_ref)
    levels = inner_ref.shape[1]
    cosine, sine = turn_scalars(rot_ref[0, 0])
    step = DOWN_UNROLL

    def column(c, k):
        return jnp.concatenate([outer_ref[c, k, 0:EDGE, :], inner_ref[c, k], outer_ref[c, k, EDGE:, :]], axis=0)

    above, copies = None, []
    for i in range(levels // step):
        group = range(i * step, (i + 1) * step)
        loaded = [([column(c, k) for c in range(4)], (g1_ref[k], g2_ref[k])) for k in group]
        done = []
        for values, gains in loaded:
            if above is not None:
                values = [values[c] + gains[c // 2] * above[c] for c in range(4)]
            above = values
            u, v = values[2:]
            done.append((values[0], values[1], cosine * u + sine * v, cosine * v - sine * u))
        for k, fields in zip(group, done):
            for c in range(4):
                field_ref[c, k] = fields[c]
        part = pl.ds(i * step, step)
        copy = pltpu.make_async_copy(field_ref.at[:, part], out_ref.at[:, part], sems.at[i])
        copy.start()
        copies.append(copy)
    for copy in copies:
        copy.wait()


HIGHEST = lax.Precision.HIGHEST


def halving_order(count):
    bits = [1 << i for i in range(1, count.bit_length() - 1)]
    order = [0]
    for bit in reversed(bits):
        order = order + [place | bit for place in order]
    return order


def transform_kernel(count, norm, owner_ref, face_ref, row_table_ref, col_table_ref, _, *refs):
    parts, (keep_ref, send_ref, cells, table, inverse) = refs[: -5], refs[-5:]
    height, width = parts[0].shape[1:]
    here_y, here_x = lax.axis_index("ty"), lax.axis_index("tx")
    targets = owner_ref.shape[0]
    per_face = targets // NFACE

    def note(i, _):
        inverse[owner_ref[i]] = i
        return 0

    lax.fori_loop(0, targets, note, 0)
    for i, part in enumerate(parts):
        rows = pl.ds(pl.multiple_of((here_y ^ i) * height, TILE), height)
        for c in range(4):
            cells[rows, c * width : (c + 1) * width] = part[c]
    along_rows = jnp.dot(row_table_ref[...], cells[...], precision=HIGHEST, preferred_element_type=F32)
    stacked = jnp.concatenate([along_rows[:, c * width : (c + 1) * width] for c in range(4)], axis=0)
    columns = col_table_ref[pl.ds(pl.multiple_of(here_x * width, TILE), width), :]
    table[...] = norm * jnp.dot(stacked, columns, precision=HIGHEST, preferred_element_type=F32)
    size = table.shape[0] // per_face
    for i, place in enumerate(halving_order(count)):
        for ref, relative in ((keep_ref, place), (send_ref, place ^ 1)):
            tile = inverse[here_y * count + (here_x ^ relative)]
            start = pl.multiple_of(lax.rem(tile, per_face) * size, TILE)
            mine = lax.div(tile, per_face) == face_ref[0, 0]
            ref[i * size : (i + 1) * size, :] = jnp.where(mine, table[pl.ds(start, size), :], 0.0)


def call(kernel, outs, in_specs, scratch=(), out_specs=None, limit=4, aliases=None, work=0):
    return pl.pallas_call(
        kernel,
        out_shape=outs,
        in_specs=in_specs,
        out_specs=out_specs or [VMEM] * len(outs),
        scratch_shapes=list(scratch),
        input_output_aliases=aliases or {},
        cost_estimate=pl.CostEstimate(flops=work, transcendentals=0, bytes_accessed=work) if work else None,
        compiler_params=pltpu.CompilerParams(vmem_limit_bytes=limit << 20),
    )


def swap(block, axis, bit):
    return lax.ppermute(block, axis, [(i, i ^ bit) for i in range(lax.axis_size(axis))])


def exchange(axis, first, second):
    count = lax.axis_size(axis)
    others = [(i, (i + 1 if i % 2 else i - 1) % count) for i in range(count)]
    return lax.ppermute(second, axis, others), swap(first, axis, 1)


def band_matrix():
    band = np.zeros((2 * LANES, 2 * LANES))
    for out in range(LANES):
        for shift, gradient, near in ((1, 8, 1), (-1, -8, 1), (2, -1, 0), (-2, 1, 0)):
            source = out + shift
            row = source if 0 <= source < LANES else LANES + source % LANES
            band[row, out] = gradient
            band[row, LANES + out] = near
    return band


def cosines(total, mode_count):
    phase = (2 * np.arange(total)[:, None] + 1) * np.arange(mode_count)[None, :] % (4 * total)
    return np.cos(phase * (math.pi / (2 * total)))


def body(adjoint, background_flow, vert_diff, wet_levels, rotation, face_map, ctrl_owner):
    _, levels, height, width = adjoint.shape
    ty, tx = lax.axis_size("ty"), lax.axis_size("tx")
    rows_total, cols_total = height * ty, width * tx
    full = shape(levels, height, width)
    pair = shape(2, levels, height, width)
    row_pair, col_pair = [shape(levels, TILE, width)] * 2, [shape(2, height, LANES)] * 2
    rows_scratch = [pltpu.VMEM((levels, TILE, width), F32)] * 2
    cols_scratch = [pltpu.VMEM((2, height, LANES), F32)] * 2
    surface = shape(2, height, width)

    def kept(rows):
        return pltpu.VMEM((4, levels, rows, width), F32)

    places = np.arange(rows_total)
    coriolis = CORIOLIS_PEAK * np.sin(math.pi * (places + 0.5) / rows_total - 0.5 * math.pi)
    coriolis = jnp.asarray(np.repeat(coriolis[:, None], width, axis=1), F32)
    row_table = jnp.asarray(cosines(rows_total, KY).T, F32)
    col_table = jnp.asarray(cosines(cols_total, KX), F32)
    norm = math.sqrt(2.0 * NFACE / (rows_total * cols_total))

    dma = pltpu.SemaphoreType.DMA
    adjoint = pltpu.with_memory_space_constraint(adjoint, pltpu.HBM)
    ts, uv, *sent = call(
        prep_kernel,
        [pair, pair] + col_pair + row_pair,
        [SMEM, ANY],
        [pltpu.VMEM((2, levels, height, width), F32)] + rows_scratch + [dma((2 * levels // PREP_UNROLL,))],
        limit=6,
        work=1 << 23,
    )(rotation, adjoint)
    cols, rows = exchange("tx", *sent[:2]), exchange("ty", *sent[2:])
    w1, w2, h1, h2, g1, g2 = call(factor_kernel, [full] * 6, [VMEM] * 2, work=1 << 22)(vert_diff, wet_levels)
    coefficients = (background_flow, w1, w2, h1, h2, coriolis, jnp.asarray(band_matrix(), jnp.bfloat16))
    ts, uv, first, *sent = call(
        functools.partial(step_kernel, "whole", ((0, height),)),
        [pair, pair, surface] + col_pair + row_pair,
        [VMEM] * 15,
        rows_scratch + [kept(height)] + cols_scratch + rows_scratch,
        limit=12,
    )(ts, uv, *coefficients, *cols, *rows, g1, g2)
    cols, rows = exchange("tx", *sent[:2]), exchange("ty", *sent[2:])
    middle = height - 2 * EDGE
    inner, inner_surface = call(
        functools.partial(step_kernel, "inner", ((EDGE, middle),)),
        [shape(4, levels, middle, width), shape(2, middle, width)],
        [VMEM] * 11,
        cols_scratch,
        work=1 << 24,
    )(ts, uv, *coefficients, *cols)
    outer, surfaces = call(
        functools.partial(step_kernel, "outer", ((0, EDGE), (height - EDGE, EDGE))),
        [shape(4, levels, 2 * EDGE, width), shape(4, height, width)],
        [VMEM] * 15,
        cols_scratch + rows_scratch,
    )(ts, uv, *coefficients, *cols, *rows, first, inner_surface)
    parts = [surfaces] + [swap(surfaces, "ty", bit) for bit in range(1, ty)]
    adjoint_out, token = call(
        last_kernel,
        [shape(*adjoint.shape), shape(TILE, LANES)],
        [SMEM] + [VMEM] * 4,
        [kept(height), dma((levels // DOWN_UNROLL,))],
        out_specs=[ANY, VMEM],
        limit=8,
        work=1 << 23,
    )(rotation, inner, outer, g1, g2)
    size = 4 * KY * NFACE // ctrl_owner.shape[0]
    keep, send = call(
        functools.partial(transform_kernel, tx, norm),
        [shape(size * tx // 2, KX)] * 2,
        [SMEM] * 2 + [VMEM] * (ty + 3),
        [pltpu.VMEM((rows_total, 4 * width), F32), pltpu.VMEM((4 * KY, KX), F32), pltpu.SMEM(ctrl_owner.shape, jnp.int32)],
        limit=6,
    )(ctrl_owner, face_map, row_table, col_table, token, *parts)
    bit = 1
    while True:
        keep = keep + swap(send, "tx", bit)
        bit *= 2
        if bit == tx:
            break
        half = keep.shape[0] // 2
        keep, send = keep[:half], keep[half:]
    return adjoint_out, keep.reshape(1, -1)


def solution(mesh):
    return jax.shard_map(
        body,
        mesh=mesh,
        in_specs=(
            P(None, None, "ty", "tx"),
            P(None, None, "ty", "tx"),
            P(None, "ty", "tx"),
            P("ty", "tx"),
            P("ty", "tx"),
            P("ty", "tx"),
            P(),
        ),
        out_specs=(P(None, None, "ty", "tx"), P(("ty", "tx"), None)),
        check_vma=False,
    )
```

```python
import functools
import math

import jax
import jax.numpy as jnp
import numpy as np
from jax import lax
from jax.experimental import pallas as pl
from jax.experimental.pallas import tpu as pltpu
from jax.sharding import PartitionSpec as P

KY = 128
KX = 128
NFACE = 4

ADVECT_COEF = 0.3
DIFFUSE_COEF = 0.12
VISCOUS_COEF = 0.1
THERMAL_COEF = 0.4
HALINE_COEF = 0.3
PRESSURE_COEF = 0.4
SALINE_WEIGHT = 0.8
CORIOLIS_PEAK = 0.5
MOMENTUM_RATIO = 1.5

TILE = 8
LANES = 128
ANY = pl.BlockSpec(memory_space=pl.ANY)
VMEM = pl.BlockSpec(memory_space=pltpu.VMEM)
SMEM = pl.BlockSpec(memory_space=pltpu.SMEM)
F32 = jnp.float32
PREP_UNROLL = 6
FACTOR_ROWS, FACTOR_UNROLL = 64, 2
UNROLLS = {16: (12, 9), 32: (6, 6), 64: (6, 9)}
DOWN_UNROLL = 6
EDGE = 16


def shape(*dims):
    return jax.ShapeDtypeStruct(dims, F32)


def lanes_of(rows):
    return lax.broadcasted_iota(jnp.int32, (rows, LANES), 1)


def rows_of(rows):
    return lax.broadcasted_iota(jnp.int32, (rows, LANES), 0)


def loop(count, load, body, init, unroll, prepare=lambda loaded: loaded):
    while count % unroll:
        unroll -= 1

    def several(i, carry):
        steps = [i * unroll + j for j in range(unroll)]
        loaded = prepare([load(step) for step in steps])
        stores = []
        for step, values in zip(steps, loaded):
            carry, store = body(step, values, carry)
            stores.append(store)
        for store in stores:
            store()
        return carry

    return lax.fori_loop(0, count // unroll, several, init)


def turn_scalars(code):
    cosine = jnp.where(code == 0, 1.0, jnp.where(code == 2, -1.0, 0.0)).astype(F32)
    sine = jnp.where(code == 1, 1.0, jnp.where(code == 3, -1.0, 0.0)).astype(F32)
    return cosine, sine


def pack_columns(acc, k, fields, lane, split):
    tracer, flow = (lane >= 4 * k) & (lane < split), lane >= split + 2 * k
    packed = []
    for g in range(2):
        rolled = jnp.where(tracer, pltpu.roll(fields[g], 4 * k + 2, 1), acc[g])
        packed.append(jnp.where(flow, pltpu.roll(fields[g + 2], split + 1 + 2 * k, 1), rolled))
    return tuple(packed)


def lane_moves(height, split):
    lane = lanes_of(height)
    tracer = lane < split
    first = jnp.where(tracer, lane % 4, 2 * (lane % 2)) < 2

    def up(x):
        return jnp.where(tracer, pltpu.roll(x, 2, 1), pltpu.roll(x, 1, 1))

    def down(x):
        return jnp.where(tracer, pltpu.roll(x, LANES - 2, 1), pltpu.roll(x, LANES - 1, 1))

    return first, up, down


def store_edge_rows(k, fields, ends, south_ref, north_ref):
    size = fields[0].shape[0]
    for c in range(4):
        if ends[0]:
            south_ref[k, 2 * c : 2 * c + 2, :] = fields[c][0:2, :]
        if ends[1]:
            north_ref[k, 2 * c : 2 * c + 2, :] = fields[c][size - 2 : size, :]


def write_rows(row_a, row_b, south_ref, north_ref):
    even = lax.axis_index("ty") % 2 == 0
    south, north = south_ref[...], north_ref[...]
    row_a[...] = jnp.where(even, north, south)
    row_b[...] = jnp.where(even, south, north)


def write_columns(col_a, col_b, low, high, split):
    even = lax.axis_index("tx") % 2 == 0
    first, up, down = lane_moves(low[0].shape[0], split)
    for g in range(2):
        east = jnp.where(first, low[g], up(high[g]))
        west = jnp.where(first, down(low[g]), high[g])
        col_a[g] = jnp.where(even, east, west)
        col_b[g] = jnp.where(even, west, east)


def read_rows(row_a, row_b, south_ref, north_ref):
    here = lax.axis_index("ty")
    even = here % 2 == 0
    first, second = row_a[...], row_b[...]
    south_ref[...] = jnp.where(here == 0, 0.0, jnp.where(even, second, first))
    north_ref[...] = jnp.where(here == lax.axis_size("ty") - 1, 0.0, jnp.where(even, first, second))


def read_columns(col_a, col_b, halo_ref, split):
    even = lax.axis_index("tx") % 2 == 0
    first, up, down = lane_moves(col_a.shape[1], split)
    for g in range(2):
        from_east = jnp.where(even, col_a[g], col_b[g])
        from_west = jnp.where(even, col_b[g], col_a[g])
        halo_ref[g, 0] = jnp.where(first, from_west, up(from_east))
        halo_ref[g, 1] = jnp.where(first, down(from_west), from_east)


def prep_kernel(rot_ref, adj_ref, ts_ref, uv_ref, col_a, col_b, row_a, row_b, raw_ref, south_ref, north_ref, sems):
    levels, height = adj_ref.shape[1], adj_ref.shape[2]
    cosine, sine = turn_scalars(rot_ref[0, 0])
    step = PREP_UNROLL
    chunks = levels // step
    copies = []
    for i in range(chunks):
        part = pl.ds(i * step, step)
        for h, target in enumerate((ts_ref, raw_ref)):
            copy = pltpu.make_async_copy(adj_ref.at[pl.ds(2 * h, 2), part], target.at[:, part], sems.at[2 * i + h])
            copy.start()
            copies.append(copy)
    lane = lanes_of(height)
    zero = jnp.zeros((height, LANES), F32)
    half = levels // 2
    accs = [(zero,) * 2, (zero,) * 2]
    for i in range(chunks):
        copies[2 * i].wait()
        copies[2 * i + 1].wait()
        group = range(i * step, (i + 1) * step)
        loaded = [(ts_ref[0, k], ts_ref[1, k], raw_ref[0, k], raw_ref[1, k]) for k in group]
        stores = []
        for k, (t, s, a, b) in zip(group, loaded):
            fields = (t, s, cosine * a - sine * b, sine * a + cosine * b)
            accs[k // half] = pack_columns(accs[k // half], k % half, fields, lane, 4 * half)
            stores.append((k, fields))
        for k, fields in stores:
            uv_ref[0, k] = fields[2]
            uv_ref[1, k] = fields[3]
            store_edge_rows(k, fields, (True, True), south_ref, north_ref)
    write_rows(row_a, row_b, south_ref, north_ref)
    write_columns(col_a, col_b, *accs, 4 * half)


def factor_kernel(vd_ref, wet_ref, w1_ref, w2_ref, h1_ref, h2_ref, g1_ref, g2_ref):
    levels, height = vd_ref.shape[0], vd_ref.shape[1]
    out = ((w1_ref, h1_ref, g1_ref, 1.0), (w2_ref, h2_ref, g2_ref, MOMENTUM_RATIO))
    size = FACTOR_ROWS
    for block in range(height // size):
        rows = pl.ds(block * size, size)
        wet = wet_ref[rows, :]
        zero = jnp.zeros((size, LANES), F32)

        def load(i, rows=rows):
            return vd_ref[jnp.maximum(levels - 2 - i, 0), rows, :]

        def level(i, loaded, carry, rows=rows, wet=wet):
            k = levels - 1 - i
            below, inverses = carry
            mask = jnp.where(k < wet, 1.0, 0.0).astype(F32)
            above = jnp.where(k > 0, loaded * mask, 0.0)
            kept, stores = [], []
            for (w_ref, h_ref, g_ref, factor), inverse in zip(out, inverses):
                low, high = factor * below, factor * above
                pivot = 1.0 + high + low - low * (low * inverse)
                inverse = 1.0 / pivot
                masked = inverse * mask
                stores += [(w_ref, masked), (h_ref, low * masked), (g_ref, high * masked)]
                kept.append(inverse)

            def store():
                for ref, value in stores:
                    ref[k, rows, :] = value

            return (above, tuple(kept)), store

        loop(levels, load, level, (zero, (zero, zero)), FACTOR_UNROLL)


def step_kernel(stage, blocks, *refs):
    refs = list(refs)

    def take(count):
        taken, refs[:] = refs[:count], refs[count:]
        return taken

    ts_ref, uv_ref, flow_ref, w1_ref, w2_ref, h1_ref, h2_ref, cor_ref, band_ref, col_b, col_a = take(11)
    south_ref = north_ref = None
    if stage != "inner":
        row_b, row_a = take(2)
    if stage == "outer":
        first_ref, inner_ref = take(2)
    if stage == "whole":
        g1_ref, g2_ref = take(2)
        ts_out, uv_out, surface_ref, *sent = take(7)
        south_out, north_out, value_ref = take(3)
    else:
        value_ref, surface_ref = take(2)
    (halo_ref,) = take(1)
    half = ts_ref.shape[1] // 2
    split = 4 * half
    read_columns(col_a, col_b, halo_ref, split)
    if stage != "inner":
        south_ref, north_ref = take(2)
        read_rows(row_a, row_b, south_ref, north_ref)
    levels, height = ts_ref.shape[1], ts_ref.shape[2]
    first_cor = pl.multiple_of(lax.axis_index("ty") * height, TILE)
    def get(c, k, start):
        rows = pl.ds(start, TILE)
        return ts_ref[c, k, rows, :] if c < 2 else uv_ref[c - 2, k, rows, :]

    def line(c, k, start, halos):
        if 0 <= start <= height - TILE:
            return get(c, k, start)
        south, north = halos
        part = rows_of(TILE)
        if start < 0:
            halo = pltpu.roll(south, (-2 * c - 2 - start) % TILE, 0)
            return jnp.where(part < -start, halo, pltpu.roll(get(c, k, 0), -start, 0))
        over = start + TILE - height
        halo = pltpu.roll(north, (TILE - over - 2 * c) % TILE, 0)
        return jnp.where(part >= TILE - over, halo, pltpu.roll(get(c, k, height - TILE), TILE - over, 0))

    for block, (first_row, size) in enumerate(blocks):
        lane = lanes_of(size)
        low_one, high_one = lane < 1, lane >= LANES - 1
        zero = jnp.zeros((size, LANES), F32)
        rows = pl.ds(first_row, size)
        kept_rows = pl.ds(block * size, size)
        south_end, north_end = first_row == 0, first_row + size == height
        cor = cor_ref[pl.ds(first_cor + first_row, size), :]
        up_unroll, down_unroll = UNROLLS[size]

        def fetch(c, k, shift, halos, first_row=first_row, size=size):
            start = first_row + shift
            if 0 <= start <= height - size:
                part = pl.ds(start, size)
                return ts_ref[c, k, part, :] if c < 2 else uv_ref[c - 2, k, part, :]
            lines = [line(c, k, start + i, halos) for i in range(0, size, TILE)]
            return lines[0] if len(lines) == 1 else jnp.concatenate(lines, axis=0)

        def load_up(i, rows=rows, ends=(south_end, north_end), fetch=fetch):
            k = levels - 1 - i
            halos = (south_ref[k] if ends[0] else None, north_ref[k] if ends[1] else None)
            part = jnp.where(k >= half, 1, 0)
            place = k - half * part
            packed = [halo_ref[g, part, rows, :] for g in range(2)]
            edges = [pltpu.roll(x, LANES - 2 - 4 * place, 1) for x in packed]
            edges += [pltpu.roll(x, LANES - 1 - split - 2 * place, 1) for x in packed]
            lines = [{s: fetch(c, k, s, halos) for s in ((0, 1, -1, 2, -2) if c < 2 else (0, 1, -1))} for c in range(4)]
            flow = [flow_ref[i, k, rows, :] for i in range(2)]
            factors = [ref[k, rows, :] for ref in (w1_ref, w2_ref, h1_ref, h2_ref)]
            return edges, lines, flow, factors

        def along_x(loaded, size=size):
            fields = [
                jnp.concatenate([item[1][c][0], item[0][c]], axis=1)
                for item in loaded
                for c in range(2)
            ]
            fields = jnp.concatenate(fields, axis=0)
            high = fields.astype(jnp.bfloat16)
            low = (fields - high.astype(F32)).astype(jnp.bfloat16)
            mixed = sum(jnp.dot(part, band_ref[...], preferred_element_type=F32) for part in (high, low))
            parts = [mixed[i * size : (i + 1) * size] for i in range(2 * len(loaded))]
            return [
                (*item, [(part[:, :LANES], part[:, LANES:]) for part in parts[2 * i : 2 * i + 2]])
                for i, item in enumerate(loaded)
            ]

        def upward(i, loaded, below, cor=cor, rows=kept_rows):
            k = levels - 1 - i
            edges, lines, flow, factors, mixed = loaded
            flow_x = flow[0] * (ADVECT_COEF / 12.0)
            flow_y = flow[1] * (ADVECT_COEF / 12.0)
            rhs, diff_y = [], []
            for c in range(2):
                mid = lines[c][0]
                n1, s1, n2, s2 = (lines[c][s] for s in (1, -1, 2, -2))
                grad_x, near_x = mixed[c]
                dy = n1 - s1
                grad = flow_x * grad_x + flow_y * (8.0 * dy - (n2 - s2))
                near = near_x + (n1 + s1)
                rhs.append((1.0 - 4.0 * DIFFUSE_COEF) * mid + DIFFUSE_COEF * near + grad)
                diff_y.append(dy)
            buoyant, at_edge = (pair[0] - SALINE_WEIGHT * pair[1] for pair in ((lines[0][0], lines[1][0]), edges))
            diff_x = pltpu.roll(jnp.where(low_one, at_edge, buoyant), LANES - 1, 1) - pltpu.roll(
                jnp.where(high_one, at_edge, buoyant), 1, 1
            )
            push = [(0.5 * PRESSURE_COEF) * d for d in (diff_x, diff_y[0] - SALINE_WEIGHT * diff_y[1])]
            sides = []
            for c in range(2, 4):
                mid = lines[c][0]
                e1 = pltpu.roll(jnp.where(low_one, edges[c], mid), LANES - 1, 1)
                w1 = pltpu.roll(jnp.where(high_one, edges[c], mid), 1, 1)
                n1, s1 = lines[c][1], lines[c][-1]
                near = (e1 + w1) + (n1 + s1)
                sides.append(e1 - w1 if c == 2 else n1 - s1)
                rhs.append((1.0 - 4.0 * VISCOUS_COEF) * mid + VISCOUS_COEF * near - push[c - 2])
            spread = sides[0] + sides[1]
            rhs[0] = rhs[0] + (0.5 * THERMAL_COEF) * spread
            rhs[1] = rhs[1] - (0.5 * HALINE_COEF) * spread
            rhs[2] = rhs[2] + cor * lines[3][0]
            rhs[3] = rhs[3] - cor * lines[2][0]
            values = tuple(
                factors[c // 2] * rhs[c] + factors[2 + c // 2] * below[c] for c in range(4)
            )

            def store():
                for c in range(4):
                    value_ref[c, k, rows, :] = values[c]

            return values, store

        top = loop(levels, load_up, upward, (zero,) * 4, up_unroll, along_x)
        for c in range(2):
            if stage == "outer":
                surface_ref[2 + c, rows, :] = top[c]
            else:
                surface_ref[c, kept_rows, :] = top[c]
        if stage != "whole":
            continue

        def load_down(k, rows=rows, kept_rows=kept_rows, base=0):
            k = base + k
            values = [value_ref[c, k, kept_rows, :] for c in range(4)]
            return values, (g1_ref[k, rows, :], g2_ref[k, rows, :])

        def downward(place, loaded, carry, rows=rows, ends=(south_end, north_end), lane=lane, base=0):
            k = base + place
            above, acc = carry
            values, gains = loaded
            fields = tuple(values[c] + gains[c // 2] * above[c] for c in range(4))

            def store():
                for c in range(2):
                    ts_out[c, k, rows, :] = fields[c]
                    uv_out[c, k, rows, :] = fields[c + 2]
                store_edge_rows(k, fields, ends, south_out, north_out)

            return (fields, pack_columns(acc, place, fields, lane, split)), store

        fields, accs = (zero,) * 4, []
        for base in (0, half):
            load, sweep = functools.partial(load_down, base=base), functools.partial(downward, base=base)
            fields, acc = loop(half, load, sweep, (fields, (zero,) * 2), down_unroll)
            accs.append(acc)
        write_rows(sent[2], sent[3], south_out, north_out)
        write_columns(sent[0], sent[1], *accs, split)
    if stage == "outer":
        surface_ref[0:2] = first_ref[...]
        for c in range(2):
            surface_ref[2 + c, blocks[0][1] : blocks[1][0], :] = inner_ref[c]


def last_kernel(rot_ref, inner_ref, outer_ref, g1_ref, g2_ref, out_ref, token_ref, field_ref, sems):
    token_ref[...] = jnp.zeros_like(token_ref)
    levels = inner_ref.shape[1]
    cosine, sine = turn_scalars(rot_ref[0, 0])
    step = DOWN_UNROLL

    def column(c, k):
        return jnp.concatenate([outer_ref[c, k, 0:EDGE, :], inner_ref[c, k], outer_ref[c, k, EDGE:, :]], axis=0)

    above, copies = None, []
    for i in range(levels // step):
        group = range(i * step, (i + 1) * step)
        loaded = [([column(c, k) for c in range(4)], (g1_ref[k], g2_ref[k])) for k in group]
        done = []
        for values, gains in loaded:
            if above is not None:
                values = [values[c] + gains[c // 2] * above[c] for c in range(4)]
            above = values
            u, v = values[2:]
            done.append((values[0], values[1], cosine * u + sine * v, cosine * v - sine * u))
        for k, fields in zip(group, done):
            for c in range(4):
                field_ref[c, k] = fields[c]
        part = pl.ds(i * step, step)
        copy = pltpu.make_async_copy(field_ref.at[:, part], out_ref.at[:, part], sems.at[i])
        copy.start()
        copies.append(copy)
    for copy in copies:
        copy.wait()


HIGHEST = lax.Precision.HIGHEST


def halving_order(count):
    bits = [1 << i for i in range(1, count.bit_length() - 1)]
    order = [0]
    for bit in reversed(bits):
        order = order + [place | bit for place in order]
    return order


def transform_kernel(count, norm, owner_ref, face_ref, row_table_ref, col_table_ref, _, *refs):
    parts, (keep_ref, send_ref, cells, table, inverse) = refs[: -5], refs[-5:]
    height, width = parts[0].shape[1:]
    here_y, here_x = lax.axis_index("ty"), lax.axis_index("tx")
    targets = owner_ref.shape[0]
    per_face = targets // NFACE

    def note(i, _):
        inverse[owner_ref[i]] = i
        return 0

    lax.fori_loop(0, targets, note, 0)
    for i, part in enumerate(parts):
        rows = pl.ds(pl.multiple_of((here_y ^ i) * height, TILE), height)
        for c in range(4):
            cells[rows, c * width : (c + 1) * width] = part[c]
    along_rows = jnp.dot(row_table_ref[...], cells[...], precision=HIGHEST, preferred_element_type=F32)
    stacked = jnp.concatenate([along_rows[:, c * width : (c + 1) * width] for c in range(4)], axis=0)
    columns = col_table_ref[pl.ds(pl.multiple_of(here_x * width, TILE), width), :]
    table[...] = norm * jnp.dot(stacked, columns, precision=HIGHEST, preferred_element_type=F32)
    size = table.shape[0] // per_face
    for i, place in enumerate(halving_order(count)):
        for ref, relative in ((keep_ref, place), (send_ref, place ^ 1)):
            tile = inverse[here_y * count + (here_x ^ relative)]
            start = pl.multiple_of(lax.rem(tile, per_face) * size, TILE)
            mine = lax.div(tile, per_face) == face_ref[0, 0]
            ref[i * size : (i + 1) * size, :] = jnp.where(mine, table[pl.ds(start, size), :], 0.0)


def call(kernel, outs, in_specs, scratch=(), out_specs=None, limit=4, aliases=None, work=0):
    return pl.pallas_call(
        kernel,
        out_shape=outs,
        in_specs=in_specs,
        out_specs=out_specs or [VMEM] * len(outs),
        scratch_shapes=list(scratch),
        input_output_aliases=aliases or {},
        cost_estimate=pl.CostEstimate(flops=work, transcendentals=0, bytes_accessed=work) if work else None,
        compiler_params=pltpu.CompilerParams(vmem_limit_bytes=limit << 20),
    )


def swap(block, axis, bit):
    return lax.ppermute(block, axis, [(i, i ^ bit) for i in range(lax.axis_size(axis))])


def exchange(axis, first, second):
    count = lax.axis_size(axis)
    others = [(i, (i + 1 if i % 2 else i - 1) % count) for i in range(count)]
    return lax.ppermute(second, axis, others), swap(first, axis, 1)


def band_matrix():
    band = np.zeros((2 * LANES, 2 * LANES))
    for out in range(LANES):
        for shift, gradient, near in ((1, 8, 1), (-1, -8, 1), (2, -1, 0), (-2, 1, 0)):
            source = out + shift
            row = source if 0 <= source < LANES else LANES + source % LANES
            band[row, out] = gradient
            band[row, LANES + out] = near
    return band


def cosines(total, mode_count):
    phase = (2 * np.arange(total)[:, None] + 1) * np.arange(mode_count)[None, :] % (4 * total)
    return np.cos(phase * (math.pi / (2 * total)))


def body(adjoint, background_flow, vert_diff, wet_levels, rotation, face_map, ctrl_owner):
    _, levels, height, width = adjoint.shape
    ty, tx = lax.axis_size("ty"), lax.axis_size("tx")
    rows_total, cols_total = height * ty, width * tx
    full = shape(levels, height, width)
    pair = shape(2, levels, height, width)
    row_pair, col_pair = [shape(levels, TILE, width)] * 2, [shape(2, height, LANES)] * 2
    rows_scratch = [pltpu.VMEM((levels, TILE, width), F32)] * 2
    cols_scratch = [pltpu.VMEM((2, 2, height, LANES), F32)]
    surface = shape(2, height, width)

    def kept(rows):
        return pltpu.VMEM((4, levels, rows, width), F32)

    places = np.arange(rows_total)
    coriolis = CORIOLIS_PEAK * np.sin(math.pi * (places + 0.5) / rows_total - 0.5 * math.pi)
    coriolis = jnp.asarray(np.repeat(coriolis[:, None], width, axis=1), F32)
    row_table = jnp.asarray(cosines(rows_total, KY).T, F32)
    col_table = jnp.asarray(cosines(cols_total, KX), F32)
    norm = math.sqrt(2.0 * NFACE / (rows_total * cols_total))

    dma = pltpu.SemaphoreType.DMA
    adjoint = pltpu.with_memory_space_constraint(adjoint, pltpu.HBM)
    ts, uv, *sent = call(
        prep_kernel,
        [pair, pair] + col_pair + row_pair,
        [SMEM, ANY],
        [pltpu.VMEM((2, levels, height, width), F32)] + rows_scratch + [dma((2 * levels // PREP_UNROLL,))],
        limit=6,
        work=1 << 23,
    )(rotation, adjoint)
    cols, rows = exchange("tx", *sent[:2]), exchange("ty", *sent[2:])
    w1, w2, h1, h2, g1, g2 = call(factor_kernel, [full] * 6, [VMEM] * 2, work=1 << 22)(vert_diff, wet_levels)
    coefficients = (background_flow, w1, w2, h1, h2, coriolis, jnp.asarray(band_matrix(), jnp.bfloat16))
    ts, uv, first, *sent = call(
        functools.partial(step_kernel, "whole", ((0, height),)),
        [pair, pair, surface] + col_pair + row_pair,
        [VMEM] * 15,
        rows_scratch + [kept(height)] + cols_scratch + rows_scratch,
        limit=12,
    )(ts, uv, *coefficients, *cols, *rows, g1, g2)
    cols, rows = exchange("tx", *sent[:2]), exchange("ty", *sent[2:])
    middle = height - 2 * EDGE
    inner, inner_surface = call(
        functools.partial(step_kernel, "inner", ((EDGE, middle),)),
        [shape(4, levels, middle, width), shape(2, middle, width)],
        [VMEM] * 11,
        cols_scratch,
        work=1 << 24,
    )(ts, uv, *coefficients, *cols)
    outer, surfaces = call(
        functools.partial(step_kernel, "outer", ((0, EDGE), (height - EDGE, EDGE))),
        [shape(4, levels, 2 * EDGE, width), shape(4, height, width)],
        [VMEM] * 15,
        cols_scratch + rows_scratch,
    )(ts, uv, *coefficients, *cols, *rows, first, inner_surface)
    parts = [surfaces] + [swap(surfaces, "ty", bit) for bit in range(1, ty)]
    adjoint_out, token = call(
        last_kernel,
        [shape(*adjoint.shape), shape(TILE, LANES)],
        [SMEM] + [VMEM] * 4,
        [kept(height), dma((levels // DOWN_UNROLL,))],
        out_specs=[ANY, VMEM],
        limit=8,
        work=1 << 23,
    )(rotation, inner, outer, g1, g2)
    size = 4 * KY * NFACE // ctrl_owner.shape[0]
    keep, send = call(
        functools.partial(transform_kernel, tx, norm),
        [shape(size * tx // 2, KX)] * 2,
        [SMEM] * 2 + [VMEM] * (ty + 3),
        [pltpu.VMEM((rows_total, 4 * width), F32), pltpu.VMEM((4 * KY, KX), F32), pltpu.SMEM(ctrl_owner.shape, jnp.int32)],
        limit=6,
    )(ctrl_owner, face_map, row_table, col_table, token, *parts)
    bit = 1
    while True:
        keep = keep + swap(send, "tx", bit)
        bit *= 2
        if bit == tx:
            break
        half = keep.shape[0] // 2
        keep, send = keep[:half], keep[half:]
    return adjoint_out, keep.reshape(1, -1)


def solution(mesh):
    return jax.shard_map(
        body,
        mesh=mesh,
        in_specs=(
            P(None, None, "ty", "tx"),
            P(None, None, "ty", "tx"),
            P(None, "ty", "tx"),
            P("ty", "tx"),
            P("ty", "tx"),
            P("ty", "tx"),
            P(),
        ),
        out_specs=(P(None, None, "ty", "tx"), P(("ty", "tx"), None)),
        check_vma=False,
    )
```

```python
import functools
import math

import jax
import jax.numpy as jnp
import numpy as np
from jax import lax
from jax.experimental import pallas as pl
from jax.experimental.pallas import tpu as pltpu
from jax.sharding import PartitionSpec as P

KY = 128
KX = 128
NFACE = 4

ADVECT_COEF = 0.3
DIFFUSE_COEF = 0.12
VISCOUS_COEF = 0.1
THERMAL_COEF = 0.4
HALINE_COEF = 0.3
PRESSURE_COEF = 0.4
SALINE_WEIGHT = 0.8
CORIOLIS_PEAK = 0.5
MOMENTUM_RATIO = 1.5

TILE = 8
LANES = 128
ANY = pl.BlockSpec(memory_space=pl.ANY)
VMEM = pl.BlockSpec(memory_space=pltpu.VMEM)
SMEM = pl.BlockSpec(memory_space=pltpu.SMEM)
F32 = jnp.float32
PREP_UNROLL = 6
FACTOR_ROWS, FACTOR_UNROLL = 64, 4
UNROLLS = {16: (18, 9), 32: (12, 6), 64: (9, 18)}
DOWN_UNROLL = 6
EDGE = 16


def shape(*dims):
    return jax.ShapeDtypeStruct(dims, F32)


def lanes_of(rows):
    return lax.broadcasted_iota(jnp.int32, (rows, LANES), 1)


def rows_of(rows):
    return lax.broadcasted_iota(jnp.int32, (rows, LANES), 0)


def loop(count, load, body, init, unroll, prepare=lambda loaded: loaded):
    while count % unroll:
        unroll -= 1

    def several(i, carry):
        steps = [i * unroll + j for j in range(unroll)]
        loaded = prepare([load(step) for step in steps])
        stores = []
        for step, values in zip(steps, loaded):
            carry, store = body(step, values, carry)
            stores.append(store)
        for store in stores:
            store()
        return carry

    return lax.fori_loop(0, count // unroll, several, init)


def turn_scalars(code):
    cosine = jnp.where(code == 0, 1.0, jnp.where(code == 2, -1.0, 0.0)).astype(F32)
    sine = jnp.where(code == 1, 1.0, jnp.where(code == 3, -1.0, 0.0)).astype(F32)
    return cosine, sine


def pack_columns(acc, k, fields, lane, split):
    tracer, flow = (lane >= 4 * k) & (lane < split), lane >= split + 2 * k
    packed = []
    for g in range(2):
        rolled = jnp.where(tracer, pltpu.roll(fields[g], 4 * k + 2, 1), acc[g])
        packed.append(jnp.where(flow, pltpu.roll(fields[g + 2], split + 1 + 2 * k, 1), rolled))
    return tuple(packed)


def lane_moves(height, split):
    lane = lanes_of(height)
    tracer = lane < split
    first = jnp.where(tracer, lane % 4, 2 * (lane % 2)) < 2

    def up(x):
        return jnp.where(tracer, pltpu.roll(x, 2, 1), pltpu.roll(x, 1, 1))

    def down(x):
        return jnp.where(tracer, pltpu.roll(x, LANES - 2, 1), pltpu.roll(x, LANES - 1, 1))

    return first, up, down


def store_edge_rows(k, fields, ends, south_ref, north_ref):
    size = fields[0].shape[0]
    for c, (at, count) in enumerate(((0, 2), (2, 2), (4, 1), (5, 1))):
        if ends[0]:
            south_ref[k, at : at + count, :] = fields[c][0:count, :]
        if ends[1]:
            north_ref[k, at : at + count, :] = fields[c][size - count : size, :]


def write_rows(row_a, row_b, south_ref, north_ref):
    even = lax.axis_index("ty") % 2 == 0
    row = rows_of(TILE)
    for group in range(south_ref.shape[0] // 4):
        for message, choose in ((row_a, (north_ref, south_ref)), (row_b, (south_ref, north_ref))):
            tiles = [jnp.where(even, choose[0][4 * group + i], choose[1][4 * group + i]) for i in range(4)]
            for i in range(3):
                message[3 * group + i] = jnp.where(row < 6, tiles[i], pltpu.roll(tiles[3], 6 - 2 * i, 0))


def write_columns(col_a, col_b, low, high, split):
    even = lax.axis_index("tx") % 2 == 0
    first, up, down = lane_moves(low[0].shape[0], split)
    for g in range(2):
        east = jnp.where(first, low[g], up(high[g]))
        west = jnp.where(first, down(low[g]), high[g])
        col_a[g, : low[0].shape[0]] = jnp.where(even, east, west)
        col_b[g, : low[0].shape[0]] = jnp.where(even, west, east)


def read_rows(row_a, row_b, south_ref, north_ref):
    here = lax.axis_index("ty")
    even = here % 2 == 0
    row = rows_of(TILE)
    at_south, at_north = here == 0, here == lax.axis_size("ty") - 1
    for group in range(south_ref.shape[0] // 4):
        first, second = ([ref[3 * group + i] for i in range(3)] for ref in (row_a, row_b))
        for ref, end, pair in ((south_ref, at_south, (second, first)), (north_ref, at_north, (first, second))):
            tiles = [jnp.where(end, 0.0, jnp.where(even, x, y)) for x, y in zip(*pair)]
            turned = [pltpu.roll(tile, 2 * i + 2, 0) for i, tile in enumerate(tiles)]
            tiles.append(jnp.where(row < 2, turned[0], jnp.where(row < 4, turned[1], turned[2])))
            for i in range(4):
                ref[4 * group + i] = tiles[i]


def read_columns(col_a, col_b, halo_ref, split):
    even = lax.axis_index("tx") % 2 == 0
    height = halo_ref.shape[2]
    first, up, down = lane_moves(height, split)
    for g in range(2):
        from_a, from_b = col_a[g, :height], col_b[g, :height]
        from_east = jnp.where(even, from_a, from_b)
        from_west = jnp.where(even, from_b, from_a)
        halo_ref[g, 0] = jnp.where(first, from_west, up(from_east))
        halo_ref[g, 1] = jnp.where(first, down(from_west), from_east)


def prep_kernel(rot_ref, adj_ref, ts_ref, uv_ref, col_a, col_b, row_a, row_b, raw_ref, south_ref, north_ref, sems):
    levels, height = adj_ref.shape[1], adj_ref.shape[2]
    cosine, sine = turn_scalars(rot_ref[0, 0])
    step = PREP_UNROLL
    chunks = levels // step
    copies = []
    for i in range(chunks):
        part = pl.ds(i * step, step)
        for h, target in enumerate((ts_ref, raw_ref)):
            copy = pltpu.make_async_copy(adj_ref.at[pl.ds(2 * h, 2), part], target.at[:, part], sems.at[2 * i + h])
            copy.start()
            copies.append(copy)
    lane = lanes_of(height)
    zero = jnp.zeros((height, LANES), F32)
    half = levels // 2
    accs = [(zero,) * 2, (zero,) * 2]
    for i in range(chunks):
        copies[2 * i].wait()
        copies[2 * i + 1].wait()
        group = range(i * step, (i + 1) * step)
        loaded = [(ts_ref[0, k], ts_ref[1, k], raw_ref[0, k], raw_ref[1, k]) for k in group]
        stores = []
        for k, (t, s, a, b) in zip(group, loaded):
            fields = (t, s, cosine * a - sine * b, sine * a + cosine * b)
            accs[k // half] = pack_columns(accs[k // half], k % half, fields, lane, 4 * half)
            stores.append((k, fields))
        for k, fields in stores:
            uv_ref[0, k] = fields[2]
            uv_ref[1, k] = fields[3]
            store_edge_rows(k, fields, (True, True), south_ref, north_ref)
    write_rows(row_a, row_b, south_ref, north_ref)
    write_columns(col_a, col_b, *accs, 4 * half)


def factor_kernel(vd_ref, wet_ref, w1_ref, w2_ref, h1_ref, h2_ref, g1_ref, g2_ref):
    levels, height = vd_ref.shape[0], vd_ref.shape[1]
    out = ((w1_ref, h1_ref, g1_ref, 1.0), (w2_ref, h2_ref, g2_ref, MOMENTUM_RATIO))
    size = FACTOR_ROWS
    for block in range(height // size):
        rows = pl.ds(block * size, size)
        wet = wet_ref[rows, :]
        zero = jnp.zeros((size, LANES), F32)

        def load(i, rows=rows):
            return vd_ref[jnp.maximum(levels - 2 - i, 0), rows, :]

        def level(i, loaded, carry, rows=rows, wet=wet):
            k = levels - 1 - i
            below, inverses = carry
            mask = jnp.where(k < wet, 1.0, 0.0).astype(F32)
            above = jnp.where(k > 0, loaded * mask, 0.0)
            kept, stores = [], []
            for (w_ref, h_ref, g_ref, factor), inverse in zip(out, inverses):
                low, high = factor * below, factor * above
                pivot = 1.0 + high + low - low * (low * inverse)
                inverse = 1.0 / pivot
                masked = inverse * mask
                stores += [(w_ref, masked), (h_ref, low * masked), (g_ref, high * masked)]
                kept.append(inverse)

            def store():
                for ref, value in stores:
                    ref[k, rows, :] = value

            return (above, tuple(kept)), store

        loop(levels, load, level, (zero, (zero, zero)), FACTOR_UNROLL)


def step_kernel(stage, blocks, *refs):
    refs = list(refs)

    def take(count):
        taken, refs[:] = refs[:count], refs[count:]
        return taken

    ts_ref, uv_ref, flow_ref, w1_ref, w2_ref, h1_ref, h2_ref, cor_ref, band_ref, col_b, col_a = take(11)
    south_ref = north_ref = None
    if stage != "inner":
        row_b, row_a = take(2)
    if stage == "outer":
        first_ref, inner_ref = take(2)
    if stage == "whole":
        g1_ref, g2_ref = take(2)
        ts_out, uv_out, surface_ref, *sent = take(7)
        south_out, north_out, value_ref = take(3)
    else:
        value_ref, surface_ref = take(2)
    (halo_ref,) = take(1)
    half = ts_ref.shape[1] // 2
    split = 4 * half
    read_columns(col_a, col_b, halo_ref, split)
    if stage != "inner":
        south_ref, north_ref = take(2)
        read_rows(row_a, row_b, south_ref, north_ref)
    levels, height = ts_ref.shape[1], ts_ref.shape[2]
    first_cor = pl.multiple_of(lax.axis_index("ty") * height, TILE)
    def get(c, k, start):
        rows = pl.ds(start, TILE)
        return ts_ref[c, k, rows, :] if c < 2 else uv_ref[c - 2, k, rows, :]

    def line(c, k, start, halos):
        if 0 <= start <= height - TILE:
            return get(c, k, start)
        south, north = halos
        part = rows_of(TILE)
        if start < 0:
            halo = pltpu.roll(south, (-2 * c - 2 - start if c < 2 else -2 - c) % TILE, 0)
            return jnp.where(part < -start, halo, pltpu.roll(get(c, k, 0), -start, 0))
        over = start + TILE - height
        halo = pltpu.roll(north, (-over - 2 * c if c < 2 else -3 - c) % TILE, 0)
        return jnp.where(part >= TILE - over, halo, pltpu.roll(get(c, k, height - TILE), TILE - over, 0))

    for block, (first_row, size) in enumerate(blocks):
        lane = lanes_of(size)
        low_one, high_one = lane < 1, lane >= LANES - 1
        zero = jnp.zeros((size, LANES), F32)
        rows = pl.ds(first_row, size)
        kept_rows = pl.ds(block * size, size)
        south_end, north_end = first_row == 0, first_row + size == height
        cor = cor_ref[pl.ds(first_cor + first_row, size), :]
        up_unroll, down_unroll = UNROLLS[size]

        def fetch(c, k, shift, halos, first_row=first_row, size=size):
            start = first_row + shift
            if 0 <= start <= height - size:
                part = pl.ds(start, size)
                return ts_ref[c, k, part, :] if c < 2 else uv_ref[c - 2, k, part, :]
            lines = [line(c, k, start + i, halos) for i in range(0, size, TILE)]
            return lines[0] if len(lines) == 1 else jnp.concatenate(lines, axis=0)

        def load_up(i, rows=rows, ends=(south_end, north_end), fetch=fetch):
            k = levels - 1 - i
            halos = (south_ref[k] if ends[0] else None, north_ref[k] if ends[1] else None)
            part = jnp.where(k >= half, 1, 0)
            place = k - half * part
            packed = [halo_ref[g, part, rows, :] for g in range(2)]
            edges = [pltpu.roll(x, LANES - 2 - 4 * place, 1) for x in packed]
            edges += [pltpu.roll(x, LANES - 1 - split - 2 * place, 1) for x in packed]
            lines = [{s: fetch(c, k, s, halos) for s in ((0, 1, -1, 2, -2) if c < 2 else (0, 1, -1))} for c in range(4)]
            flow = [flow_ref[i, k, rows, :] for i in range(2)]
            factors = [ref[k, rows, :] for ref in (w1_ref, w2_ref, h1_ref, h2_ref)]
            return edges, lines, flow, factors

        def along_x(loaded, size=size):
            fields = [
                jnp.concatenate([item[1][c][0], item[0][c]], axis=1)
                for item in loaded
                for c in range(2)
            ]
            fields = jnp.concatenate(fields, axis=0)
            high = fields.astype(jnp.bfloat16)
            low = (fields - high.astype(F32)).astype(jnp.bfloat16)
            mixed = sum(jnp.dot(part, band_ref[...], preferred_element_type=F32) for part in (high, low))
            parts = [mixed[i * size : (i + 1) * size] for i in range(2 * len(loaded))]
            return [
                (*item, [(part[:, :LANES], part[:, LANES:]) for part in parts[2 * i : 2 * i + 2]])
                for i, item in enumerate(loaded)
            ]

        def upward(i, loaded, below, cor=cor, rows=kept_rows):
            k = levels - 1 - i
            edges, lines, flow, factors, mixed = loaded
            flow_x = flow[0] * (ADVECT_COEF / 12.0)
            flow_y = flow[1] * (ADVECT_COEF / 12.0)
            rhs, diff_y = [], []
            for c in range(2):
                mid = lines[c][0]
                n1, s1, n2, s2 = (lines[c][s] for s in (1, -1, 2, -2))
                grad_x, near_x = mixed[c]
                dy = n1 - s1
                grad = flow_x * grad_x + flow_y * (8.0 * dy - (n2 - s2))
                near = near_x + (n1 + s1)
                rhs.append((1.0 - 4.0 * DIFFUSE_COEF) * mid + DIFFUSE_COEF * near + grad)
                diff_y.append(dy)
            buoyant, at_edge = (pair[0] - SALINE_WEIGHT * pair[1] for pair in ((lines[0][0], lines[1][0]), edges))
            diff_x = pltpu.roll(jnp.where(low_one, at_edge, buoyant), LANES - 1, 1) - pltpu.roll(
                jnp.where(high_one, at_edge, buoyant), 1, 1
            )
            push = [(0.5 * PRESSURE_COEF) * d for d in (diff_x, diff_y[0] - SALINE_WEIGHT * diff_y[1])]
            sides = []
            for c in range(2, 4):
                mid = lines[c][0]
                e1 = pltpu.roll(jnp.where(low_one, edges[c], mid), LANES - 1, 1)
                w1 = pltpu.roll(jnp.where(high_one, edges[c], mid), 1, 1)
                n1, s1 = lines[c][1], lines[c][-1]
                near = (e1 + w1) + (n1 + s1)
                sides.append(e1 - w1 if c == 2 else n1 - s1)
                rhs.append((1.0 - 4.0 * VISCOUS_COEF) * mid + VISCOUS_COEF * near - push[c - 2])
            spread = sides[0] + sides[1]
            rhs[0] = rhs[0] + (0.5 * THERMAL_COEF) * spread
            rhs[1] = rhs[1] - (0.5 * HALINE_COEF) * spread
            rhs[2] = rhs[2] + cor * lines[3][0]
            rhs[3] = rhs[3] - cor * lines[2][0]
            values = tuple(
                factors[c // 2] * rhs[c] + factors[2 + c // 2] * below[c] for c in range(4)
            )

            def store():
                for c in range(4):
                    value_ref[c, k, rows, :] = values[c]

            return values, store

        top = loop(levels, load_up, upward, (zero,) * 4, up_unroll, along_x)
        for c in range(2):
            if stage == "outer":
                surface_ref[2 + c, rows, :] = top[c]
            else:
                surface_ref[c, kept_rows, :] = top[c]
        if stage != "whole":
            continue

        def load_down(k, rows=rows, kept_rows=kept_rows, base=0):
            k = base + k
            values = [value_ref[c, k, kept_rows, :] for c in range(4)]
            return values, (g1_ref[k, rows, :], g2_ref[k, rows, :])

        def downward(place, loaded, carry, rows=rows, ends=(south_end, north_end), lane=lane, base=0):
            k = base + place
            above, acc = carry
            values, gains = loaded
            fields = tuple(values[c] + gains[c // 2] * above[c] for c in range(4))

            def store():
                for c in range(2):
                    ts_out[c, k, rows, :] = fields[c]
                    uv_out[c, k, rows, :] = fields[c + 2]
                store_edge_rows(k, fields, ends, south_out, north_out)

            return (fields, pack_columns(acc, place, fields, lane, split)), store

        fields, accs = (zero,) * 4, []
        for base in (0, half):
            load, sweep = functools.partial(load_down, base=base), functools.partial(downward, base=base)
            fields, acc = loop(half, load, sweep, (fields, (zero,) * 2), down_unroll)
            accs.append(acc)
        write_rows(sent[2], sent[3], south_out, north_out)
        write_columns(sent[0], sent[1], *accs, split)
    if stage == "outer":
        surface_ref[0:2] = first_ref[...]
        for c in range(2):
            surface_ref[2 + c, blocks[0][1] : blocks[1][0], :] = inner_ref[c]


def last_kernel(rot_ref, inner_ref, outer_ref, g1_ref, g2_ref, out_ref, token_ref, field_ref, sems):
    token_ref[...] = jnp.zeros_like(token_ref)
    levels = inner_ref.shape[1]
    cosine, sine = turn_scalars(rot_ref[0, 0])
    step = DOWN_UNROLL

    def column(c, k):
        return jnp.concatenate([outer_ref[c, k, 0:EDGE, :], inner_ref[c, k], outer_ref[c, k, EDGE:, :]], axis=0)

    above, copies = None, []
    for i in range(levels // step):
        group = range(i * step, (i + 1) * step)
        loaded = [([column(c, k) for c in range(4)], (g1_ref[k], g2_ref[k])) for k in group]
        done = []
        for values, gains in loaded:
            if above is not None:
                values = [values[c] + gains[c // 2] * above[c] for c in range(4)]
            above = values
            u, v = values[2:]
            done.append((values[0], values[1], cosine * u + sine * v, cosine * v - sine * u))
        for k, fields in zip(group, done):
            for c in range(4):
                field_ref[c, k] = fields[c]
        part = pl.ds(i * step, step)
        copy = pltpu.make_async_copy(field_ref.at[:, part], out_ref.at[:, part], sems.at[i])
        copy.start()
        copies.append(copy)
    for copy in copies:
        copy.wait()


HIGHEST = lax.Precision.HIGHEST


def halving_order(count):
    bits = [1 << i for i in range(1, count.bit_length() - 1)]
    order = [0]
    for bit in reversed(bits):
        order = order + [place | bit for place in order]
    return order


def transform_kernel(count, norm, owner_ref, face_ref, row_table_ref, col_table_ref, _, *refs):
    parts, (keep_ref, send_ref, cells, table, inverse) = refs[: -5], refs[-5:]
    height, width = parts[0].shape[1:]
    here_y, here_x = lax.axis_index("ty"), lax.axis_index("tx")
    targets = owner_ref.shape[0]
    per_face = targets // NFACE

    def note(i, _):
        inverse[owner_ref[i]] = i
        return 0

    lax.fori_loop(0, targets, note, 0)
    for i, part in enumerate(parts):
        rows = pl.ds(pl.multiple_of((here_y ^ i) * height, TILE), height)
        for c in range(4):
            cells[rows, c * width : (c + 1) * width] = part[c]
    along_rows = jnp.dot(row_table_ref[...], cells[...], precision=HIGHEST, preferred_element_type=F32)
    stacked = jnp.concatenate([along_rows[:, c * width : (c + 1) * width] for c in range(4)], axis=0)
    columns = col_table_ref[pl.ds(pl.multiple_of(here_x * width, TILE), width), :]
    table[...] = norm * jnp.dot(stacked, columns, precision=HIGHEST, preferred_element_type=F32)
    size = table.shape[0] // per_face
    for i, place in enumerate(halving_order(count)):
        for ref, relative in ((keep_ref, place), (send_ref, place ^ 1)):
            tile = inverse[here_y * count + (here_x ^ relative)]
            start = pl.multiple_of(lax.rem(tile, per_face) * size, TILE)
            mine = lax.div(tile, per_face) == face_ref[0, 0]
            ref[i * size : (i + 1) * size, :] = jnp.where(mine, table[pl.ds(start, size), :], 0.0)


def call(kernel, outs, in_specs, scratch=(), out_specs=None, limit=4, aliases=None, work=0):
    return pl.pallas_call(
        kernel,
        out_shape=outs,
        in_specs=in_specs,
        out_specs=out_specs or [VMEM] * len(outs),
        scratch_shapes=list(scratch),
        input_output_aliases=aliases or {},
        cost_estimate=pl.CostEstimate(flops=work, transcendentals=0, bytes_accessed=work) if work else None,
        compiler_params=pltpu.CompilerParams(vmem_limit_bytes=limit << 20),
    )


def swap(block, axis, bit):
    return lax.ppermute(block, axis, [(i, i ^ bit) for i in range(lax.axis_size(axis))])


def exchange(axis, first, second):
    count = lax.axis_size(axis)
    others = [(i, (i + 1 if i % 2 else i - 1) % count) for i in range(count)]
    return lax.ppermute(second, axis, others), swap(first, axis, 1)


def band_matrix():
    band = np.zeros((2 * LANES, 2 * LANES))
    for out in range(LANES):
        for shift, gradient, near in ((1, 8, 1), (-1, -8, 1), (2, -1, 0), (-2, 1, 0)):
            source = out + shift
            row = source if 0 <= source < LANES else LANES + source % LANES
            band[row, out] = gradient
            band[row, LANES + out] = near
    return band


def cosines(total, mode_count):
    phase = (2 * np.arange(total)[:, None] + 1) * np.arange(mode_count)[None, :] % (4 * total)
    return np.cos(phase * (math.pi / (2 * total)))


def body(adjoint, background_flow, vert_diff, wet_levels, rotation, face_map, ctrl_owner):
    _, levels, height, width = adjoint.shape
    ty, tx = lax.axis_size("ty"), lax.axis_size("tx")
    rows_total, cols_total = height * ty, width * tx
    full = shape(levels, height, width)
    pair = shape(2, levels, height, width)
    row_pair, col_pair = [shape(3 * levels // 4, TILE, width)] * 2, [shape(2, height, LANES)] * 2
    rows_scratch = [pltpu.VMEM((levels, TILE, width), F32)] * 2
    cols_scratch = [pltpu.VMEM((2, 2, height, LANES), F32)]
    surface = shape(2, height, width)

    def kept(rows):
        return pltpu.VMEM((4, levels, rows, width), F32)

    places = np.arange(rows_total)
    coriolis = CORIOLIS_PEAK * np.sin(math.pi * (places + 0.5) / rows_total - 0.5 * math.pi)
    coriolis = jnp.asarray(np.repeat(coriolis[:, None], width, axis=1), F32)
    row_table = jnp.asarray(cosines(rows_total, KY).T, F32)
    col_table = jnp.asarray(cosines(cols_total, KX), F32)
    norm = math.sqrt(2.0 * NFACE / (rows_total * cols_total))

    dma = pltpu.SemaphoreType.DMA
    adjoint = pltpu.with_memory_space_constraint(adjoint, pltpu.HBM)
    ts, uv, *sent = call(
        prep_kernel,
        [pair, pair] + col_pair + row_pair,
        [SMEM, ANY],
        [pltpu.VMEM((2, levels, height, width), F32)] + rows_scratch + [dma((2 * levels // PREP_UNROLL,))],
        limit=6,
        work=1 << 23,
    )(rotation, adjoint)
    cols, rows = exchange("tx", *sent[:2]), exchange("ty", *sent[2:])
    w1, w2, h1, h2, g1, g2 = call(factor_kernel, [full] * 6, [VMEM] * 2, work=1 << 22)(vert_diff, wet_levels)
    coefficients = (background_flow, w1, w2, h1, h2, coriolis, jnp.asarray(band_matrix(), jnp.bfloat16))
    ts, uv, first, *sent = call(
        functools.partial(step_kernel, "whole", ((0, height),)),
        [pair, pair, surface] + [shape(2, 7 * height // 4, LANES)] * 2 + row_pair,
        [VMEM] * 15,
        rows_scratch + [kept(height)] + cols_scratch + rows_scratch,
        limit=12,
    )(ts, uv, *coefficients, *cols, *rows, g1, g2)
    cols, rows = exchange("tx", *sent[:2]), exchange("ty", *sent[2:])
    middle = height - 2 * EDGE
    inner, inner_surface = call(
        functools.partial(step_kernel, "inner", ((EDGE, middle),)),
        [shape(4, levels, middle, width), shape(2, middle, width)],
        [VMEM] * 11,
        cols_scratch,
        work=1 << 24,
    )(ts, uv, *coefficients, *cols)
    outer, surfaces = call(
        functools.partial(step_kernel, "outer", ((0, EDGE), (height - EDGE, EDGE))),
        [shape(4, levels, 2 * EDGE, width), shape(4, height, width)],
        [VMEM] * 15,
        cols_scratch + rows_scratch,
    )(ts, uv, *coefficients, *cols, *rows, first, inner_surface)
    parts = [surfaces] + [swap(surfaces, "ty", bit) for bit in range(1, ty)]
    adjoint_out, token = call(
        last_kernel,
        [shape(*adjoint.shape), shape(TILE, LANES)],
        [SMEM] + [VMEM] * 4,
        [kept(height), dma((levels // DOWN_UNROLL,))],
        out_specs=[ANY, VMEM],
        limit=8,
        work=1 << 23,
    )(rotation, inner, outer, g1, g2)
    size = 4 * KY * NFACE // ctrl_owner.shape[0]
    keep, send = call(
        functools.partial(transform_kernel, tx, norm),
        [shape(size * tx // 2, KX)] * 2,
        [SMEM] * 2 + [VMEM] * (ty + 3),
        [pltpu.VMEM((rows_total, 4 * width), F32), pltpu.VMEM((4 * KY, KX), F32), pltpu.SMEM(ctrl_owner.shape, jnp.int32)],
        limit=6,
    )(ctrl_owner, face_map, row_table, col_table, token, *parts)
    bit = 1
    while True:
        keep = keep + swap(send, "tx", bit)
        bit *= 2
        if bit == tx:
            break
        half = keep.shape[0] // 2
        keep, send = keep[:half], keep[half:]
    return adjoint_out, keep.reshape(1, -1)


def solution(mesh):
    return jax.shard_map(
        body,
        mesh=mesh,
        in_specs=(
            P(None, None, "ty", "tx"),
            P(None, None, "ty", "tx"),
            P(None, "ty", "tx"),
            P("ty", "tx"),
            P("ty", "tx"),
            P("ty", "tx"),
            P(),
        ),
        out_specs=(P(None, None, "ty", "tx"), P(("ty", "tx"), None)),
        check_vma=False,
    )
```

```python
import functools
import math

import jax
import jax.numpy as jnp
import numpy as np
from jax import lax
from jax.experimental import pallas as pl
from jax.experimental.pallas import tpu as pltpu
from jax.sharding import PartitionSpec as P

KY = 128
KX = 128
NFACE = 4

ADVECT_COEF = 0.3
DIFFUSE_COEF = 0.12
VISCOUS_COEF = 0.1
THERMAL_COEF = 0.4
HALINE_COEF = 0.3
PRESSURE_COEF = 0.4
SALINE_WEIGHT = 0.8
CORIOLIS_PEAK = 0.5
MOMENTUM_RATIO = 1.5

TILE = 8
LANES = 128
ANY = pl.BlockSpec(memory_space=pl.ANY)
VMEM = pl.BlockSpec(memory_space=pltpu.VMEM)
SMEM = pl.BlockSpec(memory_space=pltpu.SMEM)
F32 = jnp.float32
PREP_UNROLL = 6
FACTOR_ROWS, FACTOR_UNROLL = 64, 4
UNROLLS = {16: (18, 9), 32: (18, 6), 64: (9, 18)}
DOWN_UNROLL = 6
EDGE = 16


def shape(*dims):
    return jax.ShapeDtypeStruct(dims, F32)


def lanes_of(rows):
    return lax.broadcasted_iota(jnp.int32, (rows, LANES), 1)


def rows_of(rows):
    return lax.broadcasted_iota(jnp.int32, (rows, LANES), 0)


def loop(count, load, body, init, unroll, prepare=lambda loaded: loaded):
    while count % unroll:
        unroll -= 1

    def several(i, carry):
        steps = [i * unroll + j for j in range(unroll)]
        loaded = prepare([load(step) for step in steps])
        stores = []
        for step, values in zip(steps, loaded):
            carry, store = body(step, values, carry)
            stores.append(store)
        for store in stores:
            store()
        return carry

    return lax.fori_loop(0, count // unroll, several, init)


def turn_scalars(code):
    cosine = jnp.where(code == 0, 1.0, jnp.where(code == 2, -1.0, 0.0)).astype(F32)
    sine = jnp.where(code == 1, 1.0, jnp.where(code == 3, -1.0, 0.0)).astype(F32)
    return cosine, sine


def pack_columns(acc, k, fields, lane, split):
    tracer, flow = (lane >= 4 * k) & (lane < split), lane >= split + 2 * k
    packed = []
    for g in range(2):
        rolled = jnp.where(tracer, pltpu.roll(fields[g], 4 * k + 2, 1), acc[g])
        packed.append(jnp.where(flow, pltpu.roll(fields[g + 2], split + 1 + 2 * k, 1), rolled))
    return tuple(packed)


def lane_moves(height, split):
    lane = lanes_of(height)
    tracer = lane < split
    first = jnp.where(tracer, lane % 4, 2 * (lane % 2)) < 2

    def up(x):
        return jnp.where(tracer, pltpu.roll(x, 2, 1), pltpu.roll(x, 1, 1))

    def down(x):
        return jnp.where(tracer, pltpu.roll(x, LANES - 2, 1), pltpu.roll(x, LANES - 1, 1))

    return first, up, down


def store_edge_rows(k, fields, ends, south_ref, north_ref):
    size = fields[0].shape[0]
    for c, (at, count) in enumerate(((0, 2), (2, 2), (4, 1), (5, 1))):
        if ends[0]:
            south_ref[k, at : at + count, :] = fields[c][0:count, :]
        if ends[1]:
            north_ref[k, at : at + count, :] = fields[c][size - count : size, :]


def write_rows(row_a, row_b, south_ref, north_ref):
    even = lax.axis_index("ty") % 2 == 0
    row = rows_of(TILE)
    for group in range(south_ref.shape[0] // 4):
        for message, choose in ((row_a, (north_ref, south_ref)), (row_b, (south_ref, north_ref))):
            tiles = [jnp.where(even, choose[0][4 * group + i], choose[1][4 * group + i]) for i in range(4)]
            for i in range(3):
                message[3 * group + i] = jnp.where(row < 6, tiles[i], pltpu.roll(tiles[3], 6 - 2 * i, 0))


def write_columns(col_a, col_b, low, high, split):
    even = lax.axis_index("tx") % 2 == 0
    first, up, down = lane_moves(low[0].shape[0], split)
    for g in range(2):
        east = jnp.where(first, low[g], up(high[g]))
        west = jnp.where(first, down(low[g]), high[g])
        col_a[g, : low[0].shape[0]] = jnp.where(even, east, west)
        col_b[g, : low[0].shape[0]] = jnp.where(even, west, east)


def read_rows(row_a, row_b, south_ref, north_ref):
    here = lax.axis_index("ty")
    even = here % 2 == 0
    row = rows_of(TILE)
    at_south, at_north = here == 0, here == lax.axis_size("ty") - 1
    for group in range(south_ref.shape[0] // 4):
        first, second = ([ref[3 * group + i] for i in range(3)] for ref in (row_a, row_b))
        for ref, end, pair in ((south_ref, at_south, (second, first)), (north_ref, at_north, (first, second))):
            tiles = [jnp.where(end, 0.0, jnp.where(even, x, y)) for x, y in zip(*pair)]
            turned = [pltpu.roll(tile, 2 * i + 2, 0) for i, tile in enumerate(tiles)]
            tiles.append(jnp.where(row < 2, turned[0], jnp.where(row < 4, turned[1], turned[2])))
            for i in range(4):
                ref[4 * group + i] = tiles[i]


def read_columns(col_a, col_b, halo_ref, split):
    even = lax.axis_index("tx") % 2 == 0
    height = halo_ref.shape[2]
    first, up, down = lane_moves(height, split)
    for g in range(2):
        from_a, from_b = col_a[g, :height], col_b[g, :height]
        from_east = jnp.where(even, from_a, from_b)
        from_west = jnp.where(even, from_b, from_a)
        halo_ref[g, 0] = jnp.where(first, from_west, up(from_east))
        halo_ref[g, 1] = jnp.where(first, down(from_west), from_east)


def prep_kernel(rot_ref, adj_ref, ts_ref, uv_ref, col_a, col_b, row_a, row_b, raw_ref, south_ref, north_ref, sems):
    levels, height = adj_ref.shape[1], adj_ref.shape[2]
    cosine, sine = turn_scalars(rot_ref[0, 0])
    step = PREP_UNROLL
    chunks = levels // step
    copies = []
    for i in range(chunks):
        part = pl.ds(i * step, step)
        for h, target in enumerate((ts_ref, raw_ref)):
            copy = pltpu.make_async_copy(adj_ref.at[pl.ds(2 * h, 2), part], target.at[:, part], sems.at[2 * i + h])
            copy.start()
            copies.append(copy)
    lane = lanes_of(height)
    zero = jnp.zeros((height, LANES), F32)
    half = levels // 2
    accs = [(zero,) * 2, (zero,) * 2]
    for i in range(chunks):
        copies[2 * i].wait()
        copies[2 * i + 1].wait()
        group = range(i * step, (i + 1) * step)
        loaded = [(ts_ref[0, k], ts_ref[1, k], raw_ref[0, k], raw_ref[1, k]) for k in group]
        stores = []
        for k, (t, s, a, b) in zip(group, loaded):
            fields = (t, s, cosine * a - sine * b, sine * a + cosine * b)
            accs[k // half] = pack_columns(accs[k // half], k % half, fields, lane, 4 * half)
            stores.append((k, fields))
        for k, fields in stores:
            uv_ref[0, k] = fields[2]
            uv_ref[1, k] = fields[3]
            store_edge_rows(k, fields, (True, True), south_ref, north_ref)
    write_rows(row_a, row_b, south_ref, north_ref)
    write_columns(col_a, col_b, *accs, 4 * half)


def factor_kernel(vd_ref, wet_ref, w1_ref, w2_ref, h1_ref, h2_ref, g1_ref, g2_ref):
    levels, height = vd_ref.shape[0], vd_ref.shape[1]
    out = ((w1_ref, h1_ref, g1_ref, 1.0), (w2_ref, h2_ref, g2_ref, MOMENTUM_RATIO))
    size = FACTOR_ROWS
    for block in range(height // size):
        rows = pl.ds(block * size, size)
        wet = wet_ref[rows, :]
        zero = jnp.zeros((size, LANES), F32)

        def load(i, rows=rows):
            return vd_ref[jnp.maximum(levels - 2 - i, 0), rows, :]

        def level(i, loaded, carry, rows=rows, wet=wet):
            k = levels - 1 - i
            below, inverses = carry
            mask = jnp.where(k < wet, 1.0, 0.0).astype(F32)
            above = jnp.where(k > 0, loaded * mask, 0.0)
            kept, stores = [], []
            for (w_ref, h_ref, g_ref, factor), inverse in zip(out, inverses):
                low, high = factor * below, factor * above
                pivot = 1.0 + high + low - low * (low * inverse)
                inverse = 1.0 / pivot
                masked = inverse * mask
                stores += [(w_ref, masked), (h_ref, low * masked), (g_ref, high * masked)]
                kept.append(inverse)

            def store():
                for ref, value in stores:
                    ref[k, rows, :] = value

            return (above, tuple(kept)), store

        loop(levels, load, level, (zero, (zero, zero)), FACTOR_UNROLL)


def step_kernel(stage, blocks, *refs):
    refs = list(refs)

    def take(count):
        taken, refs[:] = refs[:count], refs[count:]
        return taken

    ts_ref, uv_ref, flow_ref, w1_ref, w2_ref, h1_ref, h2_ref, cor_ref, band_ref, col_b, col_a = take(11)
    south_ref = north_ref = None
    if stage != "inner":
        row_b, row_a = take(2)
    if stage == "outer":
        first_ref, inner_ref = take(2)
    if stage == "whole":
        g1_ref, g2_ref = take(2)
        ts_out, uv_out, surface_ref, *sent = take(7)
        south_out, north_out, value_ref = take(3)
    else:
        value_ref, surface_ref = take(2)
    (halo_ref,) = take(1)
    half = ts_ref.shape[1] // 2
    split = 4 * half
    read_columns(col_a, col_b, halo_ref, split)
    if stage != "inner":
        south_ref, north_ref = take(2)
        read_rows(row_a, row_b, south_ref, north_ref)
    levels, height = ts_ref.shape[1], ts_ref.shape[2]
    first_cor = pl.multiple_of(lax.axis_index("ty") * height, TILE)
    def get(c, k, start):
        rows = pl.ds(start, TILE)
        return ts_ref[c, k, rows, :] if c < 2 else uv_ref[c - 2, k, rows, :]

    def line(c, k, start, halos):
        if 0 <= start <= height - TILE:
            return get(c, k, start)
        south, north = halos
        part = rows_of(TILE)
        if start < 0:
            halo = pltpu.roll(south, (-2 * c - 2 - start if c < 2 else -2 - c) % TILE, 0)
            return jnp.where(part < -start, halo, pltpu.roll(get(c, k, 0), -start, 0))
        over = start + TILE - height
        halo = pltpu.roll(north, (-over - 2 * c if c < 2 else -3 - c) % TILE, 0)
        return jnp.where(part >= TILE - over, halo, pltpu.roll(get(c, k, height - TILE), TILE - over, 0))

    for block, (first_row, size) in enumerate(blocks):
        lane = lanes_of(size)
        low_one, high_one = lane < 1, lane >= LANES - 1
        zero = jnp.zeros((size, LANES), F32)
        rows = pl.ds(first_row, size)
        kept_rows = pl.ds(block * size, size)
        south_end, north_end = first_row == 0, first_row + size == height
        cor = cor_ref[pl.ds(first_cor + first_row, size), :]
        up_unroll, down_unroll = UNROLLS[size]

        def fetch(c, k, shift, halos, first_row=first_row, size=size):
            start = first_row + shift
            if 0 <= start <= height - size:
                part = pl.ds(start, size)
                return ts_ref[c, k, part, :] if c < 2 else uv_ref[c - 2, k, part, :]
            lines = [line(c, k, start + i, halos) for i in range(0, size, TILE)]
            return lines[0] if len(lines) == 1 else jnp.concatenate(lines, axis=0)

        def load_up(i, rows=rows, ends=(south_end, north_end), fetch=fetch):
            k = levels - 1 - i
            halos = (south_ref[k] if ends[0] else None, north_ref[k] if ends[1] else None)
            part = jnp.where(k >= half, 1, 0)
            place = k - half * part
            packed = [halo_ref[g, part, rows, :] for g in range(2)]
            edges = [pltpu.roll(x, LANES - 2 - 4 * place, 1) for x in packed]
            edges += [pltpu.roll(x, LANES - 1 - split - 2 * place, 1) for x in packed]
            lines = [{s: fetch(c, k, s, halos) for s in ((0, 1, -1, 2, -2) if c < 2 else (0, 1, -1))} for c in range(4)]
            flow = [flow_ref[i, k, rows, :] for i in range(2)]
            factors = [ref[k, rows, :] for ref in (w1_ref, w2_ref, h1_ref, h2_ref)]
            return edges, lines, flow, factors

        def along_x(loaded, size=size):
            fields = [
                jnp.concatenate([item[1][c][0], item[0][c]], axis=1)
                for item in loaded
                for c in range(2)
            ]
            fields = jnp.concatenate(fields, axis=0)
            high = fields.astype(jnp.bfloat16)
            low = (fields - high.astype(F32)).astype(jnp.bfloat16)
            mixed = sum(jnp.dot(part, band_ref[...], preferred_element_type=F32) for part in (high, low))
            parts = [mixed[i * size : (i + 1) * size] for i in range(2 * len(loaded))]
            return [
                (*item, [(part[:, :LANES], part[:, LANES:]) for part in parts[2 * i : 2 * i + 2]])
                for i, item in enumerate(loaded)
            ]

        def upward(i, loaded, below, cor=cor, rows=kept_rows):
            k = levels - 1 - i
            edges, lines, flow, factors, mixed = loaded
            flow_x = flow[0] * (ADVECT_COEF / 12.0)
            flow_y = flow[1] * (ADVECT_COEF / 12.0)
            rhs, diff_y = [], []
            for c in range(2):
                mid = lines[c][0]
                n1, s1, n2, s2 = (lines[c][s] for s in (1, -1, 2, -2))
                grad_x, near_x = mixed[c]
                dy = n1 - s1
                grad = flow_x * grad_x + flow_y * (8.0 * dy - (n2 - s2))
                near = near_x + (n1 + s1)
                rhs.append((1.0 - 4.0 * DIFFUSE_COEF) * mid + DIFFUSE_COEF * near + grad)
                diff_y.append(dy)
            buoyant, at_edge = (pair[0] - SALINE_WEIGHT * pair[1] for pair in ((lines[0][0], lines[1][0]), edges))
            diff_x = pltpu.roll(jnp.where(low_one, at_edge, buoyant), LANES - 1, 1) - pltpu.roll(
                jnp.where(high_one, at_edge, buoyant), 1, 1
            )
            push = [(0.5 * PRESSURE_COEF) * d for d in (diff_x, diff_y[0] - SALINE_WEIGHT * diff_y[1])]
            sides = []
            for c in range(2, 4):
                mid = lines[c][0]
                e1 = pltpu.roll(jnp.where(low_one, edges[c], mid), LANES - 1, 1)
                w1 = pltpu.roll(jnp.where(high_one, edges[c], mid), 1, 1)
                n1, s1 = lines[c][1], lines[c][-1]
                near = (e1 + w1) + (n1 + s1)
                sides.append(e1 - w1 if c == 2 else n1 - s1)
                rhs.append((1.0 - 4.0 * VISCOUS_COEF) * mid + VISCOUS_COEF * near - push[c - 2])
            spread = sides[0] + sides[1]
            rhs[0] = rhs[0] + (0.5 * THERMAL_COEF) * spread
            rhs[1] = rhs[1] - (0.5 * HALINE_COEF) * spread
            rhs[2] = rhs[2] + cor * lines[3][0]
            rhs[3] = rhs[3] - cor * lines[2][0]
            values = tuple(
                factors[c // 2] * rhs[c] + factors[2 + c // 2] * below[c] for c in range(4)
            )

            def store():
                for c in range(4):
                    value_ref[c, k, rows, :] = values[c]

            return values, store

        top = loop(levels, load_up, upward, (zero,) * 4, up_unroll, along_x)
        for c in range(2):
            if stage == "outer":
                surface_ref[2 + c, rows, :] = top[c]
            else:
                surface_ref[c, kept_rows, :] = top[c]
        if stage != "whole":
            continue

        def load_down(k, rows=rows, kept_rows=kept_rows, base=0):
            k = base + k
            values = [value_ref[c, k, kept_rows, :] for c in range(4)]
            return values, (g1_ref[k, rows, :], g2_ref[k, rows, :])

        def downward(place, loaded, carry, rows=rows, ends=(south_end, north_end), lane=lane, base=0):
            k = base + place
            above, acc = carry
            values, gains = loaded
            fields = tuple(values[c] + gains[c // 2] * above[c] for c in range(4))

            def store():
                for c in range(2):
                    ts_out[c, k, rows, :] = fields[c]
                    uv_out[c, k, rows, :] = fields[c + 2]
                store_edge_rows(k, fields, ends, south_out, north_out)

            return (fields, pack_columns(acc, place, fields, lane, split)), store

        fields, accs = (zero,) * 4, []
        for base in (0, half):
            load, sweep = functools.partial(load_down, base=base), functools.partial(downward, base=base)
            fields, acc = loop(half, load, sweep, (fields, (zero,) * 2), down_unroll)
            accs.append(acc)
        write_rows(sent[2], sent[3], south_out, north_out)
        write_columns(sent[0], sent[1], *accs, split)
    if stage == "outer":
        surface_ref[0:2] = first_ref[...]
        for c in range(2):
            surface_ref[2 + c, blocks[0][1] : blocks[1][0], :] = inner_ref[c]


def last_kernel(rot_ref, inner_ref, outer_ref, g1_ref, g2_ref, out_ref, token_ref, field_ref, sems):
    token_ref[...] = jnp.zeros_like(token_ref)
    levels = inner_ref.shape[1]
    cosine, sine = turn_scalars(rot_ref[0, 0])
    step = DOWN_UNROLL

    def column(c, k):
        return jnp.concatenate([outer_ref[c, k, 0:EDGE, :], inner_ref[c, k], outer_ref[c, k, EDGE:, :]], axis=0)

    above, copies = None, []
    for i in range(levels // step):
        group = range(i * step, (i + 1) * step)
        loaded = [([column(c, k) for c in range(4)], (g1_ref[k], g2_ref[k])) for k in group]
        done = []
        for values, gains in loaded:
            if above is not None:
                values = [values[c] + gains[c // 2] * above[c] for c in range(4)]
            above = values
            u, v = values[2:]
            done.append((values[0], values[1], cosine * u + sine * v, cosine * v - sine * u))
        for k, fields in zip(group, done):
            for c in range(4):
                field_ref[c, k] = fields[c]
        part = pl.ds(i * step, step)
        copy = pltpu.make_async_copy(field_ref.at[:, part], out_ref.at[:, part], sems.at[i])
        copy.start()
        copies.append(copy)
    for copy in copies:
        copy.wait()


HIGHEST = lax.Precision.HIGHEST


def halving_order(count):
    bits = [1 << i for i in range(1, count.bit_length() - 1)]
    order = [0]
    for bit in reversed(bits):
        order = order + [place | bit for place in order]
    return order


def transform_kernel(count, norm, owner_ref, face_ref, row_table_ref, col_table_ref, _, *refs):
    parts, (keep_ref, send_ref, cells, table, inverse) = refs[: -5], refs[-5:]
    height, width = parts[0].shape[1:]
    here_y, here_x = lax.axis_index("ty"), lax.axis_index("tx")
    targets = owner_ref.shape[0]
    per_face = targets // NFACE

    def note(i, _):
        inverse[owner_ref[i]] = i
        return 0

    lax.fori_loop(0, targets, note, 0)
    for i, part in enumerate(parts):
        rows = pl.ds(pl.multiple_of((here_y ^ i) * height, TILE), height)
        for c in range(4):
            cells[rows, c * width : (c + 1) * width] = part[c]
    along_rows = jnp.dot(row_table_ref[...], cells[...], precision=HIGHEST, preferred_element_type=F32)
    stacked = jnp.concatenate([along_rows[:, c * width : (c + 1) * width] for c in range(4)], axis=0)
    columns = col_table_ref[pl.ds(pl.multiple_of(here_x * width, TILE), width), :]
    table[...] = norm * jnp.dot(stacked, columns, precision=HIGHEST, preferred_element_type=F32)
    size = table.shape[0] // per_face
    for i, place in enumerate(halving_order(count)):
        for ref, relative in ((keep_ref, place), (send_ref, place ^ 1)):
            tile = inverse[here_y * count + (here_x ^ relative)]
            start = pl.multiple_of(lax.rem(tile, per_face) * size, TILE)
            mine = lax.div(tile, per_face) == face_ref[0, 0]
            ref[i * size : (i + 1) * size, :] = jnp.where(mine, table[pl.ds(start, size), :], 0.0)


def call(kernel, outs, in_specs, scratch=(), out_specs=None, limit=4, aliases=None, work=0):
    return pl.pallas_call(
        kernel,
        out_shape=outs,
        in_specs=in_specs,
        out_specs=out_specs or [VMEM] * len(outs),
        scratch_shapes=list(scratch),
        input_output_aliases=aliases or {},
        cost_estimate=pl.CostEstimate(flops=work, transcendentals=0, bytes_accessed=work) if work else None,
        compiler_params=pltpu.CompilerParams(vmem_limit_bytes=limit << 20),
    )


def swap(block, axis, bit):
    return lax.ppermute(block, axis, [(i, i ^ bit) for i in range(lax.axis_size(axis))])


def exchange(axis, first, second):
    count = lax.axis_size(axis)
    others = [(i, (i + 1 if i % 2 else i - 1) % count) for i in range(count)]
    return lax.ppermute(second, axis, others), swap(first, axis, 1)


def band_matrix():
    band = np.zeros((2 * LANES, 2 * LANES))
    for out in range(LANES):
        for shift, gradient, near in ((1, 8, 1), (-1, -8, 1), (2, -1, 0), (-2, 1, 0)):
            source = out + shift
            row = source if 0 <= source < LANES else LANES + source % LANES
            band[row, out] = gradient
            band[row, LANES + out] = near
    return band


def cosines(total, mode_count):
    phase = (2 * np.arange(total)[:, None] + 1) * np.arange(mode_count)[None, :] % (4 * total)
    return np.cos(phase * (math.pi / (2 * total)))


def body(adjoint, background_flow, vert_diff, wet_levels, rotation, face_map, ctrl_owner):
    _, levels, height, width = adjoint.shape
    ty, tx = lax.axis_size("ty"), lax.axis_size("tx")
    rows_total, cols_total = height * ty, width * tx
    full = shape(levels, height, width)
    pair = shape(2, levels, height, width)
    row_pair, col_pair = [shape(3 * levels // 4, TILE, width)] * 2, [shape(2, height, LANES)] * 2
    rows_scratch = [pltpu.VMEM((levels, TILE, width), F32)] * 2
    cols_scratch = [pltpu.VMEM((2, 2, height, LANES), F32)]
    surface = shape(2, height, width)

    def kept(rows):
        return pltpu.VMEM((4, levels, rows, width), F32)

    places = np.arange(rows_total)
    coriolis = CORIOLIS_PEAK * np.sin(math.pi * (places + 0.5) / rows_total - 0.5 * math.pi)
    coriolis = jnp.asarray(np.repeat(coriolis[:, None], width, axis=1), F32)
    row_table = jnp.asarray(cosines(rows_total, KY).T, F32)
    col_table = jnp.asarray(cosines(cols_total, KX), F32)
    norm = math.sqrt(2.0 * NFACE / (rows_total * cols_total))

    dma = pltpu.SemaphoreType.DMA
    adjoint = pltpu.with_memory_space_constraint(adjoint, pltpu.HBM)
    ts, uv, *sent = call(
        prep_kernel,
        [pair, pair] + col_pair + row_pair,
        [SMEM, ANY],
        [pltpu.VMEM((2, levels, height, width), F32)] + rows_scratch + [dma((2 * levels // PREP_UNROLL,))],
        limit=6,
        work=1 << 23,
    )(rotation, adjoint)
    cols, rows = exchange("tx", *sent[:2]), exchange("ty", *sent[2:])
    w1, w2, h1, h2, g1, g2 = call(factor_kernel, [full] * 6, [VMEM] * 2, work=1 << 22)(vert_diff, wet_levels)
    coefficients = (background_flow, w1, w2, h1, h2, coriolis, jnp.asarray(band_matrix(), jnp.bfloat16))
    ts, uv, first, *sent = call(
        functools.partial(step_kernel, "whole", ((0, height),)),
        [pair, pair, surface] + [shape(2, 7 * height // 4, LANES)] * 2 + row_pair,
        [VMEM] * 15,
        rows_scratch + [kept(height)] + cols_scratch + rows_scratch,
        limit=12,
    )(ts, uv, *coefficients, *cols, *rows, g1, g2)
    cols, rows = exchange("tx", *sent[:2]), exchange("ty", *sent[2:])
    middle = height - 2 * EDGE
    inner, inner_surface = call(
        functools.partial(step_kernel, "inner", ((EDGE, middle),)),
        [shape(4, levels, middle, width), shape(2, middle, width)],
        [VMEM] * 11,
        cols_scratch,
        limit=8,
        work=1 << 24,
    )(ts, uv, *coefficients, *cols)
    outer, surfaces = call(
        functools.partial(step_kernel, "outer", ((0, EDGE), (height - EDGE, EDGE))),
        [shape(4, levels, 2 * EDGE, width), shape(4, height, width)],
        [VMEM] * 15,
        cols_scratch + rows_scratch,
    )(ts, uv, *coefficients, *cols, *rows, first, inner_surface)
    parts = [surfaces] + [swap(surfaces, "ty", bit) for bit in range(1, ty)]
    adjoint_out, token = call(
        last_kernel,
        [shape(*adjoint.shape), shape(TILE, LANES)],
        [SMEM] + [VMEM] * 4,
        [kept(height), dma((levels // DOWN_UNROLL,))],
        out_specs=[ANY, VMEM],
        limit=8,
        work=1 << 23,
    )(rotation, inner, outer, g1, g2)
    size = 4 * KY * NFACE // ctrl_owner.shape[0]
    keep, send = call(
        functools.partial(transform_kernel, tx, norm),
        [shape(size * tx // 2, KX)] * 2,
        [SMEM] * 2 + [VMEM] * (ty + 3),
        [pltpu.VMEM((rows_total, 4 * width), F32), pltpu.VMEM((4 * KY, KX), F32), pltpu.SMEM(ctrl_owner.shape, jnp.int32)],
        limit=6,
    )(ctrl_owner, face_map, row_table, col_table, token, *parts)
    bit = 1
    while True:
        keep = keep + swap(send, "tx", bit)
        bit *= 2
        if bit == tx:
            break
        half = keep.shape[0] // 2
        keep, send = keep[:half], keep[half:]
    return adjoint_out, keep.reshape(1, -1)


def solution(mesh):
    return jax.shard_map(
        body,
        mesh=mesh,
        in_specs=(
            P(None, None, "ty", "tx"),
            P(None, None, "ty", "tx"),
            P(None, "ty", "tx"),
            P("ty", "tx"),
            P("ty", "tx"),
            P("ty", "tx"),
            P(),
        ),
        out_specs=(P(None, None, "ty", "tx"), P(("ty", "tx"), None)),
        check_vma=False,
    )
```
